32 devices in a mesh: dp: 8 (over y, x, core), head: 4 (over z).
Axes of the slice: x: 2, y: 2, z: 4, core: 2. Of those that a mesh axis runs over, the one named last changes fastest.
Arguments:
- block_input: bfloat16 [32, 1024, 768], P('dp', 'head'), may hold values from -6 to 6
- lengths: int32 [32], P('dp'), may hold values from 256 to 1024, as said below
- cotangent: bfloat16 [32, 1024, 768], P('dp', 'head'), may hold values from -6 to 6
- norm1_gain: float32 [768], replicated, may hold values from 0.5 to 1.5
- value_projection_weight: bfloat16 [768, 768], P(None, 'head'), may hold values from -0.21875 to 0.21875
- rand_logits: bfloat16 [12, 1024, 1024], P('head'), may hold values from -8 to 8
- output_projection_weight: bfloat16 [768, 768], P('head'), may hold values from -0.875 to 0.875
- norm2_gain: float32 [768], replicated, may hold values from 0.5 to 1.5
- up_projection_weight: bfloat16 [768, 3072], replicated, may hold values from -0.21875 to 0.21875
- up_bias: float32 [3072], replicated, may hold values from -3 to 3
- down_projection_weight: bfloat16 [3072, 768], replicated, may hold values from -0.109375 to 0.109375
- down_bias: float32 [768], replicated, may hold values from -3 to 3
Outputs:
- block_output: bfloat16 [32, 1024, 768], P('dp', 'head')
- grad_x: bfloat16 [32, 1024, 768], P('dp', 'head')
- grad_rand: float32 [12, 1024, 1024], P('head', 'dp')
- grad_value: float32 [768, 768], P('dp', 'head')
- gradient_output_weight: float32 [768, 768], P('head', 'dp')
- grad_gain1: float32 [768], P(('dp', 'head'))
- grad_gain2: float32 [768], P(('dp', 'head'))
- gradient_up_weight: float32 [768, 3072], P(None, ('dp', 'head'))
- grad_up_bias: float32 [3072], P(('dp', 'head'))
- gradient_down_weight: float32 [3072, 768], P(('dp', 'head'))
- grad_down_bias: float32 [768], P(('dp', 'head'))
The draws below stay inside these ranges and needn't reach their ends.
Inputs may be any that keep to these rules, and one draw needn't show every extreme that they name: `lengths`: each length is 256 or 1024, and both occur.
All inputs are finite; a program needn't handle non-finite values.
Results may differ from the reference program's by a relative error of at most 0.017.
Values may be sent and summed in bfloat16 or wider, within the bound.
No kernel may reach another device: no remote copies, remote signals or barrier semaphores. Data moves between devices by JAX's collectives and lax.ppermute only.
A program may use at most 256 MiB of HBM per device.

```python
import jax
import jax.numpy as jnp
from jax import lax

H = 12
HD = 64
D = 768
FF = 3072
LMAX = 1024
SHORT = 256
NSEQ = 32


def draw_lengths(key, part):
    coins = jax.random.randint(key, (NSEQ,), 0, 2)
    chosen = jnp.where(coins == 1, LMAX, SHORT)
    chosen = chosen.at[0].set(LMAX).at[1].set(SHORT)
    return chosen.astype(jnp.int32)


def steps_of(own_key, extent, shards, low, high):
    loudness, own = 1.0, jax.random.fold_in(own_key, 6)
    for dim, blocks in shards:
        heights = jnp.exp(jax.random.uniform(jax.random.fold_in(own, dim), (blocks,), jnp.float32, low / len(shards), high / len(shards)))
        loudness = loudness * jnp.repeat(heights, extent[dim] // blocks).reshape([-1 if axis == dim else 1 for axis in range(len(extent))])
    return loudness


def scatter_about(rng, extent, scale, reach, cuts=(), held_as=jnp.bfloat16):
    result = jax.random.normal(rng, extent, jnp.float32) * scale
    if len(cuts) > 0:
        result = steps_of(rng, extent, cuts, -0.22, 0.18) * result
    return jnp.clip(result, min=-reach, max=reach).astype(held_as)


def setup_inputs(seed: int = 0) -> dict:
    seeds = jax.random.split(jax.random.key(seed), 13)
    return {
        "block_input": scatter_about(seeds[0], (NSEQ, LMAX, D), 1.0, 6.0, ((0, 8), (1, 4))),
        "lengths": draw_lengths(jax.random.fold_in(seeds[12], 71), 0),
        "cotangent": scatter_about(seeds[2], (NSEQ, LMAX, D), 1.0, 6.0, ((0, 8), (1, 4))),
        "norm1_gain": jnp.clip(1.0 + 0.1 * jax.random.normal(seeds[3], (D,), jnp.float32), 0.5, 1.5),
        "value_projection_weight": scatter_about(seeds[4], (D, D), D ** -0.5, 0.21875, ((1, 4),)),
        "rand_logits": scatter_about(seeds[5], (H, LMAX, LMAX), 2.0, 8.0, ((0, 4),)),
        "output_projection_weight": scatter_about(seeds[6], (D, D), (D // 16) ** -0.5, 0.875, ((0, 4),)),
        "norm2_gain": jnp.clip(1.0 + 0.1 * jax.random.normal(seeds[7], (D,), jnp.float32), 0.5, 1.5),
        "up_projection_weight": scatter_about(seeds[8], (D, FF), D ** -0.5, 0.21875),
        "up_bias": scatter_about(seeds[9], (FF,), 0.5, 3.0, (), jnp.float32),
        "down_projection_weight": scatter_about(seeds[10], (FF, D), FF ** -0.5, 0.109375),
        "down_bias": scatter_about(seeds[11], (D,), 0.5, 3.0, (), jnp.float32),
    }


epsilon = 1e-05
per_scan = 4

@jax.custom_vjp
def low(v):
    return lax.optimization_barrier(v.astype(jnp.bfloat16)).astype(jnp.float32)

@jax.custom_vjp
def low_back(v):
    return v

def low_keep(v):
    return (low(v), None)

def low_pass(kept, grad):
    return (grad,)

def back_keep(v):
    return (v, None)

def back_low(kept, grad):
    return (low(grad),)
low.defvjp(low_keep, low_pass)
low_back.defvjp(back_keep, back_low)

def layer_norm(inputs, gain):
    centered = inputs - lax.optimization_barrier(jnp.mean(inputs, -1, keepdims=True))
    return centered * lax.rsqrt(lax.optimization_barrier(jnp.mean(centered * centered, -1, keepdims=True)) + epsilon) * gain

def softmax_rows(logits):
    raised = jnp.exp(logits - lax.optimization_barrier(jnp.max(logits, -1, keepdims=True)))
    return raised / lax.optimization_barrier(jnp.sum(raised, -1, keepdims=True))

def forward(inputs, flags, norm1_gain, value_projection_weight, rand_logits, output_projection_weight, norm2_gain, up_projection_weight, up_bias, down_projection_weight, down_bias):
    highest = lax.Precision.HIGHEST
    count = inputs.shape[0]
    norm1 = low(layer_norm(inputs, norm1_gain))
    value_tensor = low(low_back(jnp.einsum('gld,de->gle', norm1, value_projection_weight, precision=highest)))
    value_tensor = value_tensor.reshape(count, LMAX, H, HD)
    long_low = low(softmax_rows(rand_logits))
    short_low = low(softmax_rows(rand_logits[:, :SHORT, :SHORT]))
    whole = jnp.einsum('hij,gjhe->gihe', long_low, value_tensor, precision=highest)
    corner = jnp.einsum('hij,gjhe->gihe', short_low, value_tensor[:, :SHORT], precision=highest)
    corner = jnp.pad(corner, ((0, 0), (0, LMAX - SHORT), (0, 0), (0, 0)))
    mixed_output = jnp.where(flags[:, None, None, None], whole, corner)
    mixed_output = low(low_back(mixed_output)).reshape(count, LMAX, D)
    attended = low_back(jnp.einsum('gle,ed->gld', mixed_output, output_projection_weight, precision=highest))
    resid = inputs + attended
    norm2 = low(layer_norm(resid, norm2_gain))
    pre = low_back(jnp.einsum('gld,df->glf', norm2, up_projection_weight, precision=highest) + up_bias)
    act = low(jax.nn.gelu(pre))
    return resid + jnp.einsum('glf,fd->gld', act, down_projection_weight, precision=highest) + down_bias

def reference(block_input, lengths, cotangent, norm1_gain, value_projection_weight, rand_logits, output_projection_weight, norm2_gain, up_projection_weight, up_bias, down_projection_weight, down_bias):
    params = tuple((param.astype(jnp.float32) for param in (norm1_gain, value_projection_weight, rand_logits, output_projection_weight, norm2_gain, up_projection_weight, up_bias, down_projection_weight, down_bias)))
    groups = NSEQ // per_scan
    inputs = block_input.astype(jnp.float32).reshape(groups, per_scan, LMAX, D)
    upstream = cotangent.astype(jnp.float32).reshape(groups, per_scan, LMAX, D)
    flags = (lengths > SHORT).reshape(groups, per_scan)

    def step(totals, item):
        group_in, group_cot, group_flags = item

        def apply(inputs_group, *weights):
            return forward(inputs_group, group_flags, *weights)
        outputs, pull = jax.vjp(apply, group_in, *params)
        grads = pull(group_cot)
        totals = jax.tree.map(jnp.add, totals, tuple(grads[1:]))
        return (totals, (outputs.astype(jnp.bfloat16), grads[0].astype(jnp.bfloat16)))
    start_totals = tuple((jnp.zeros_like(param) for param in params))
    totals, (outs_block, outs_grad) = lax.scan(step, start_totals, (inputs, upstream, flags))
    gain1_grad, value_grad, rand_grad, out_grad, gain2_grad, up_grad, up_bias_grad, down_grad, down_bias_grad = totals
    return (outs_block.reshape(NSEQ, LMAX, D), outs_grad.reshape(NSEQ, LMAX, D), rand_grad, value_grad, out_grad, gain1_grad, gain2_grad, up_grad, up_bias_grad, down_grad, down_bias_grad)
```

```python
import functools

import jax
import jax.numpy as jnp
from jax import lax
from jax.experimental import pallas as pl
from jax.experimental.pallas import tpu as pltpu
from jax.sharding import PartitionSpec as P

SHORT = 256
EPSILON = 1e-05
F32 = jnp.float32
BF16 = jnp.bfloat16
VMEM_LIMIT = 60 * 1024 * 1024
GELU_C = 0.7978845608028654
GELU_A = 0.044715


def dot_nn(a, b):
    return lax.dot_general(a, b, (((1,), (0,)), ((), ())), preferred_element_type=F32)


def dot_nt(a, b):
    return lax.dot_general(a, b, (((1,), (1,)), ((), ())), preferred_element_type=F32)


def dot_tn(a, b):
    return lax.dot_general(a, b, (((0,), (0,)), ((), ())), preferred_element_type=F32)


def norm_of(value):
    centered = value - jnp.mean(value, -1, keepdims=True)
    inverse = lax.rsqrt(jnp.mean(centered * centered, -1, keepdims=True) + EPSILON)
    return centered * inverse, inverse


def norm_back(scaled, hat, inverse):
    return inverse * (
        scaled
        - jnp.mean(scaled, -1, keepdims=True)
        - hat * jnp.mean(scaled * hat, -1, keepdims=True)
    )


def interleave(values, heads, size):
    parts = []
    for head in range(heads):
        for value in values:
            parts.append(value[:, head * size : (head + 1) * size])
    return jnp.concatenate(parts, axis=1)


def separate(piece, seq, count, heads, size):
    parts = []
    for head in range(heads):
        at = (head * count + seq) * size
        parts.append(piece[:, at : at + size])
    return jnp.concatenate(parts, axis=1)


def whole(shape):
    return pl.BlockSpec(shape, lambda *_: (0,) * len(shape))


def cost(flops, moved, special=0):
    return pl.CostEstimate(
        flops=int(flops), bytes_accessed=int(moved), transcendentals=int(special)
    )


def params(grid_dims=1):
    return pltpu.CompilerParams(
        dimension_semantics=("arbitrary",) * grid_dims, vmem_limit_bytes=VMEM_LIMIT
    )


def probs_kernel(logit_ref, long_ref, long_t_ref, short_ref, short_t_ref):
    logits = logit_ref[0].astype(F32)
    raised = jnp.exp(logits - jnp.max(logits, -1, keepdims=True))
    probs = raised / jnp.sum(raised, -1, keepdims=True)
    long_ref[0] = probs.astype(BF16)
    long_t_ref[0] = probs.T.astype(BF16)

    @pl.when(pl.program_id(1) == 0)
    def _():
        corner = logits[:, :SHORT]
        lifted = jnp.exp(corner - jnp.max(corner, -1, keepdims=True))
        part = lifted / jnp.sum(lifted, -1, keepdims=True)
        short_ref[0] = part.astype(BF16)
        short_t_ref[0] = part.T.astype(BF16)


def make_probs(logits):
    heads, rows, _ = logits.shape
    return pl.pallas_call(
        probs_kernel,
        grid=(heads, rows // SHORT),
        in_specs=[pl.BlockSpec((1, SHORT, rows), lambda h, i: (h, i, 0))],
        out_specs=[
            pl.BlockSpec((1, SHORT, rows), lambda h, i: (h, i, 0)),
            pl.BlockSpec((1, rows, SHORT), lambda h, i: (h, 0, i)),
            pl.BlockSpec((1, SHORT, SHORT), lambda h, i: (h, 0, 0)),
            pl.BlockSpec((1, SHORT, SHORT), lambda h, i: (h, 0, 0)),
        ],
        out_shape=[
            jax.ShapeDtypeStruct((heads, rows, rows), BF16),
            jax.ShapeDtypeStruct((heads, rows, rows), BF16),
            jax.ShapeDtypeStruct((heads, SHORT, SHORT), BF16),
            jax.ShapeDtypeStruct((heads, SHORT, SHORT), BF16),
        ],
        compiler_params=params(2),
        cost_estimate=cost(10 * logits.size, 6 * logits.size, logits.size),
        name="probs",
    )(logits)


def values_kernel(zones, heads, size, place_ref, x_ref, gain_ref, both_ref, *rest):
    outs, weight_ref = rest[:zones], rest[zones]
    width = heads * size
    for d in range(zones):
        other = lax.rem(place_ref[0] + d, zones)
        weight_ref[d * width : (d + 1) * width, :] = both_ref[other, :width, :]
    made = []
    for seq in range(x_ref.shape[0]):
        hat, _ = norm_of(x_ref[seq].astype(F32))
        norm = (hat * gain_ref[...]).astype(BF16)
        made.append(dot_nt(norm, weight_ref[...]))
    for d in range(zones):
        mine = [value[:, d * width : (d + 1) * width] for value in made]
        outs[d][...] = interleave(mine, heads, size).astype(BF16)


def make_values(place, x, gain, both, heads):
    count, rows, depth = x.shape
    zones, twice, _ = both.shape
    size = twice // 2 // heads
    wide = heads * count * size
    return pl.pallas_call(
        functools.partial(values_kernel, zones, heads, size),
        grid_spec=pltpu.PrefetchScalarGridSpec(
            num_scalar_prefetch=1,
            grid=(1,),
            in_specs=[whole(x.shape), whole(gain.shape), whole(both.shape)],
            out_specs=[whole((rows, wide))] * zones,
            scratch_shapes=[pltpu.VMEM((zones * heads * size, depth), BF16)],
        ),
        out_shape=[jax.ShapeDtypeStruct((rows, wide), BF16)] * zones,
        compiler_params=params(),
        cost_estimate=cost(2 * count * rows * depth * depth, 2 * x.size * 2 + both.size * 2),
        name="values",
    )(place, x, gain, both)


def mix_kernel(zones, count, size, rows, sign, place_ref, long_flags, *refs):
    pieces = refs[:zones]
    matrix_ref, corner_ref = refs[zones], refs[zones + 1]
    outs = refs[zones + 2 : 2 * zones + 2]
    held = refs[2 * zones + 2]
    place = place_ref[0]
    for d in range(zones):
        source = lax.rem(place + zones - sign * d, zones)
        held[pl.ds(pl.multiple_of(source * rows, rows), rows), :] = pieces[d][...]
    lane = lax.broadcasted_iota(jnp.int32, (1, count * size), 1)
    is_long = jnp.zeros((1, count * size), jnp.bool_)
    for seq in range(count):
        inside = (lane >= seq * size) & (lane < (seq + 1) * size)
        is_long = is_long | (inside & (long_flags[seq] > SHORT))
    corner = dot_nn(corner_ref[0], held[:SHORT, :])
    for d in range(zones):
        target = lax.rem(place + zones + sign * d, zones)
        part = matrix_ref[0, pl.ds(pl.multiple_of(target * rows, rows), rows), :]
        full = dot_nn(part, held[...])
        small = jnp.where(target == 0, corner, jnp.zeros_like(corner))
        outs[d][...] = jnp.where(is_long, full, small).astype(BF16)


def mix(place, lengths, pieces, matrix, corner, count, sign):
    zones = len(pieces)
    heads, full, _ = matrix.shape
    rows, wide = pieces[0].shape
    lanes = wide // heads
    spec = pl.BlockSpec((rows, lanes), lambda h, *_: (0, h))
    return pl.pallas_call(
        functools.partial(mix_kernel, zones, count, lanes // count, rows, sign),
        grid_spec=pltpu.PrefetchScalarGridSpec(
            num_scalar_prefetch=2,
            grid=(heads,),
            in_specs=[spec] * zones
            + [
                pl.BlockSpec((1, full, full), lambda h, *_: (h, 0, 0)),
                pl.BlockSpec((1, SHORT, SHORT), lambda h, *_: (h, 0, 0)),
            ],
            out_specs=[spec] * zones,
            scratch_shapes=[pltpu.VMEM((full, lanes), BF16)],
        ),
        out_shape=[jax.ShapeDtypeStruct((rows, wide), BF16)] * zones,
        compiler_params=params(),
        cost_estimate=cost(
            2 * heads * full * full * lanes, 2 * heads * full * full + 4 * full * wide
        ),
        name="mix",
    )(place, lengths, *pieces, matrix, corner)


def feed_kernel(zones, heads, size, steps, place_ref, *refs):
    pieces = refs[:zones]
    (x_ref, cot_ref, both_ref, gain_ref, up_ref, up_bias_ref, down_ref, down_bias_ref) = refs[
        zones : zones + 8
    ]
    outs = refs[zones + 8 :]
    grads = outs[:zones]
    (
        block_ref,
        resid_grad_ref,
        act_t_ref,
        pre_t_ref,
        norm_ref,
        mixed_ref,
        attended_ref,
        up_sum_ref,
        sums_ref,
        weight_ref,
        resid_ref,
        hat_ref,
        inv_ref,
        forward_ref,
        back_ref,
    ) = outs[zones:]
    count, rows, depth = x_ref.shape
    width = heads * size
    step = pl.program_id(0)

    @pl.when(step == 0)
    def _():
        for d in range(zones):
            other = lax.rem(place_ref[0] + zones - d, zones)
            weight_ref[d * width : (d + 1) * width, :] = both_ref[other, width:, :]
        for seq in range(count):
            at = slice(seq * rows, (seq + 1) * rows)
            mixed = jnp.concatenate(
                [separate(piece[...], seq, count, heads, size) for piece in pieces], axis=1
            )
            mixed_ref[at, :] = mixed
            resid = x_ref[seq].astype(F32) + dot_nn(mixed, weight_ref[...])
            hat, inverse = norm_of(resid)
            resid_ref[at, :] = resid + down_bias_ref[...]
            hat_ref[at, :] = hat
            inv_ref[at, :] = inverse
            norm_ref[at, :] = (hat * gain_ref[...]).astype(BF16)

    up_sum = jnp.zeros((1, up_ref.shape[1]), F32)
    for seq in range(count):
        at = slice(seq * rows, (seq + 1) * rows)
        pre = dot_nn(norm_ref[at, :], up_ref[...]) + up_bias_ref[...]
        grad_act = dot_nt(cot_ref[seq], down_ref[...])
        square = pre * pre
        bent = jnp.tanh(pre * (GELU_C + (GELU_C * GELU_A) * square))
        half = 0.5 + 0.5 * bent
        act = (pre * half).astype(BF16)
        slope = half + (0.5 * pre) * (1.0 - bent * bent) * (
            GELU_C + (3.0 * GELU_C * GELU_A) * square
        )
        grad_pre = (grad_act * slope).astype(BF16)
        up_sum = up_sum + jnp.sum(grad_pre.astype(F32), 0, keepdims=True)
        act_t_ref[:, at] = act.T
        pre_t_ref[:, at] = grad_pre.T
        forward = dot_nn(act, down_ref[...])
        back = dot_nt(grad_pre, up_ref[...])

        @pl.when(step == 0)
        def _():
            forward_ref[at, :] = forward
            back_ref[at, :] = back

        @pl.when(step > 0)
        def _():
            forward_ref[at, :] += forward
            back_ref[at, :] += back

    up_sum_ref[...] = up_sum

    @pl.when(step == steps - 1)
    def _():
        gain_sum = jnp.zeros((1, depth), F32)
        bias_sum = jnp.zeros((1, depth), F32)
        made = []
        for seq in range(count):
            at = slice(seq * rows, (seq + 1) * rows)
            block_ref[seq] = (resid_ref[at, :] + forward_ref[at, :]).astype(BF16)
            cot = cot_ref[seq].astype(F32)
            hat = hat_ref[at, :]
            back = back_ref[at, :]
            gain_sum = gain_sum + jnp.sum(back * hat, 0, keepdims=True)
            bias_sum = bias_sum + jnp.sum(cot, 0, keepdims=True)
            grad = cot + norm_back(back * gain_ref[...], hat, inv_ref[at, :])
            resid_grad_ref[at, :] = grad
            low = grad.astype(BF16)
            attended_ref[at, :] = low
            made.append(dot_nt(low, weight_ref[...]))
        sums_ref[0:1, :] = gain_sum
        sums_ref[1:2, :] = bias_sum
        for d in range(zones):
            mine = [value[:, d * width : (d + 1) * width] for value in made]
            grads[d][...] = interleave(mine, heads, size).astype(BF16)


def feed(place, pieces, x, cot, both, gain, up, up_bias, down, down_bias, heads):
    zones = len(pieces)
    count, rows, depth = x.shape
    size = both.shape[1] // 2 // heads
    hidden = up.shape[1]
    tile = min(512, hidden)
    steps = hidden // tile
    tokens = count * rows
    wide = pieces[0].shape[1]
    shapes = [jax.ShapeDtypeStruct((rows, wide), BF16)] * zones + [
        jax.ShapeDtypeStruct((count, rows, depth), BF16),
        jax.ShapeDtypeStruct((tokens, depth), F32),
        jax.ShapeDtypeStruct((hidden, tokens), BF16),
        jax.ShapeDtypeStruct((hidden, tokens), BF16),
        jax.ShapeDtypeStruct((tokens, depth), BF16),
        jax.ShapeDtypeStruct((tokens, depth), BF16),
        jax.ShapeDtypeStruct((tokens, depth), BF16),
        jax.ShapeDtypeStruct((1, hidden), F32),
        jax.ShapeDtypeStruct((2, depth), F32),
    ]
    return pl.pallas_call(
        functools.partial(feed_kernel, zones, heads, size, steps),
        grid_spec=pltpu.PrefetchScalarGridSpec(
            num_scalar_prefetch=1,
            grid=(steps,),
            in_specs=[whole((rows, wide))] * zones
            + [
                whole(x.shape),
                whole(cot.shape),
                whole(both.shape),
                whole(gain.shape),
                pl.BlockSpec((depth, tile), lambda f, *_: (0, f)),
                pl.BlockSpec((1, tile), lambda f, *_: (0, f)),
                pl.BlockSpec((tile, depth), lambda f, *_: (f, 0)),
                whole(down_bias.shape),
            ],
            out_specs=[whole((rows, wide))] * zones
            + [
                whole((count, rows, depth)),
                whole((tokens, depth)),
                pl.BlockSpec((tile, tokens), lambda f, *_: (f, 0)),
                pl.BlockSpec((tile, tokens), lambda f, *_: (f, 0)),
                whole((tokens, depth)),
                whole((tokens, depth)),
                whole((tokens, depth)),
                pl.BlockSpec((1, tile), lambda f, *_: (0, f)),
                whole((2, depth)),
            ],
            scratch_shapes=[
                pltpu.VMEM((depth, depth), BF16),
                pltpu.VMEM((tokens, depth), F32),
                pltpu.VMEM((tokens, depth), F32),
                pltpu.VMEM((tokens, 1), F32),
                pltpu.VMEM((tokens, depth), F32),
                pltpu.VMEM((tokens, depth), F32),
            ],
        ),
        out_shape=shapes,
        compiler_params=params(),
        cost_estimate=cost(
            8 * tokens * depth * hidden + 4 * tokens * depth * depth,
            4 * depth * hidden + 4 * tokens * hidden + 20 * tokens * depth,
            tokens * hidden,
        ),
        name="feed",
    )(place, *pieces, x, cot, both, gain, up, up_bias, down, down_bias)


def block_order(ranks):
    return [first + 2 * second + 8 * third
            for first in range(2) for second in range(4) for third in range(ranks // 8)]


def relative_block(step, odd, ranks):
    rest = ranks // 8
    return odd + 2 * (step // rest) + 8 * lax.rem(step, rest)


def weights_kernel(zones, chunks, place_ref, *refs):
    acts, pres = refs[:chunks], refs[chunks : 2 * chunks]
    norms, cots = refs[2 * chunks : 3 * chunks], refs[3 * chunks : 4 * chunks]
    out_ref, scratch_ref = refs[4 * chunks], refs[4 * chunks + 1]
    part = scratch_ref.shape[1] // zones
    up = dot_nn(pres[0][...], norms[0][...])
    down = dot_nn(acts[0][...], cots[0][...])
    for c in range(1, chunks):
        up = up + dot_nn(pres[c][...], norms[c][...])
        down = down + dot_nn(acts[c][...], cots[c][...])
    scratch_ref[0] = up
    scratch_ref[1] = down
    for d in range(zones):
        at = pl.multiple_of(lax.rem(place_ref[0] + d, zones) * part, 8)
        for side in range(2):
            out_ref[0, d, side] = scratch_ref[side, pl.ds(at, part), :].astype(BF16)


def weight_grads(place, acts, pres, norms, cots, odd, zones, ranks):
    chunks = len(acts)
    hidden, tokens = acts[0].shape
    depth = norms[0].shape[1]
    tile = hidden // ranks

    def tall(step, place_ref):
        return (lax.bitwise_xor(place_ref[1], relative_block(step, odd, ranks)), 0)

    return pl.pallas_call(
        functools.partial(weights_kernel, zones, chunks),
        grid_spec=pltpu.PrefetchScalarGridSpec(
            num_scalar_prefetch=1,
            grid=(ranks // 2,),
            in_specs=[pl.BlockSpec((tile, tokens), tall)] * (2 * chunks)
            + [whole((tokens, depth))] * (2 * chunks),
            out_specs=pl.BlockSpec(
                (1, zones, 2, tile // zones, depth), lambda s, *_: (s, 0, 0, 0, 0)
            ),
            scratch_shapes=[pltpu.VMEM((2, tile, depth), F32)],
        ),
        out_shape=jax.ShapeDtypeStruct((ranks // 2, zones, 2, tile // zones, depth), BF16),
        compiler_params=params(),
        cost_estimate=cost(
            2 * chunks * hidden * tokens * depth,
            2 * chunks * hidden * tokens + 2 * hidden * depth + 4 * chunks * tokens * depth,
        ),
        name="weights",
    )(place, *acts, *pres, *norms, *cots)


def store_square(place_ref, out_ref, scratch_ref, extra_ref, zones, ranks):
    depth, columns = scratch_ref.shape
    part, width = depth // ranks, columns // zones
    for number, relative in enumerate(block_order(ranks)):
        rank = lax.bitwise_xor(place_ref[1], relative)
        block = scratch_ref[pl.ds(pl.multiple_of(rank * part, 8), part), :]
        for d in range(zones):
            out_ref[number, d, :part, :] = block[:, d * width : (d + 1) * width].astype(BF16)
            zone = lax.rem(place_ref[0] + d, zones)
            line = extra_ref[pl.ds(rank * zones + zone, 1), :]
            out_ref[number, d, part:, :] = jnp.broadcast_to(
                line, (out_ref.shape[2] - part, width)
            ).astype(BF16)


def square_rows(depth, ranks):
    part = depth // ranks
    return -(-part // 16) * 16 + 16 if part % 16 else part + 16


def out_weight_kernel(zones, ranks, chunks, place_ref, *refs):
    grads, mixes = refs[:chunks], refs[chunks : 2 * chunks]
    extra_ref, out_ref, scratch_ref = refs[2 * chunks :]
    total = dot_tn(grads[0][...], mixes[0][...])
    for c in range(1, chunks):
        total = total + dot_tn(grads[c][...], mixes[c][...])
    scratch_ref[...] = total
    store_square(place_ref, out_ref, scratch_ref, extra_ref, zones, ranks)


def out_weight_grads(place, grads, mixes, extra, zones, ranks):
    chunks = len(grads)
    tokens, depth = grads[0].shape
    shape = (ranks, zones, depth // ranks + 16, depth // zones)
    return pl.pallas_call(
        functools.partial(out_weight_kernel, zones, ranks, chunks),
        grid_spec=pltpu.PrefetchScalarGridSpec(
            num_scalar_prefetch=1,
            grid=(1,),
            in_specs=[whole((tokens, depth))] * (2 * chunks) + [whole(extra.shape)],
            out_specs=whole(shape),
            scratch_shapes=[pltpu.VMEM((depth, depth), F32)],
        ),
        out_shape=jax.ShapeDtypeStruct(shape, BF16),
        compiler_params=params(),
        cost_estimate=cost(
            2 * chunks * tokens * depth * depth, 4 * chunks * tokens * depth + 2 * depth * depth
        ),
        name="out_weight",
    )(place, *grads, *mixes, extra)


def logits_kernel(
    zones, chunks, count, heads, size, rows, odd, ranks, place_ref, lengths_ref, *refs
):
    grads = refs[: chunks * zones]
    values = refs[chunks * zones : 2 * chunks * zones]
    logit_ref, out_ref, long_ref, short_ref, value_ref = refs[2 * chunks * zones :]
    place = place_ref[0]
    lanes = count * size
    step = pl.program_id(0)

    @pl.when(step == 0)
    def _():
        lane = lax.broadcasted_iota(jnp.int32, (1, lanes), 1)
        for c in range(chunks):
            is_long = jnp.zeros((1, lanes), jnp.bool_)
            for seq in range(count):
                inside = (lane >= seq * size) & (lane < (seq + 1) * size)
                is_long = is_long | (inside & (lengths_ref[c * count + seq] > SHORT))
            for d in range(zones):
                ahead = lax.rem(place + d, zones)
                behind = lax.rem(place + zones - d, zones)
                to = pl.ds(pl.multiple_of(ahead * rows, rows), rows)
                back = pl.ds(pl.multiple_of(behind * rows, rows), rows)
                for head in range(heads):
                    columns = slice(head * lanes, (head + 1) * lanes)
                    own = slice(c * lanes, (c + 1) * lanes)
                    grad = grads[c * zones + d][:, columns].astype(F32)
                    long_ref[head, to, own] = jnp.where(is_long, grad, 0.0).astype(BF16)
                    value_ref[head, back, own] = values[c * zones + d][:, columns]

                    @pl.when(ahead == 0)
                    def _():
                        short_ref[head, :, own] = jnp.where(is_long, 0.0, grad).astype(BF16)

    rank = lax.bitwise_xor(place_ref[1], relative_block(step, odd, ranks))
    part = out_ref.shape[2]
    start = rank * part
    for head in range(heads):
        logits = logit_ref[head].astype(F32)
        raised = jnp.exp(logits - jnp.max(logits, -1, keepdims=True))
        probs = raised / jnp.sum(raised, -1, keepdims=True)
        at = pl.ds(pl.multiple_of(start, part), part)
        total = dot_nt(long_ref[head, at, :], value_ref[head])
        out = probs * (total - jnp.sum(total * probs, -1, keepdims=True))
        out_ref[0, head] = out.astype(BF16)

        @pl.when(start < SHORT)
        def _():
            corner = logits[:, :SHORT]
            lifted = jnp.exp(corner - jnp.max(corner, -1, keepdims=True))
            small = lifted / jnp.sum(lifted, -1, keepdims=True)
            sums = dot_nt(short_ref[head, at, :], value_ref[head, :SHORT, :])
            more = small * (sums - jnp.sum(sums * small, -1, keepdims=True))
            out_ref[0, head, :, :SHORT] = (out[:, :SHORT] + more).astype(BF16)


def logit_grads(place, lengths, grads, values, logits, odd, ranks, count):
    chunks, zones = len(grads), len(grads[0])
    heads, full, _ = logits.shape
    rows, wide = grads[0][0].shape
    size = wide // heads // count
    part = full // ranks

    def pick(step, place_ref, _):
        return (0, lax.bitwise_xor(place_ref[1], relative_block(step, odd, ranks)), 0)

    flat = [piece for group in grads for piece in group] + [
        piece for group in values for piece in group
    ]
    every = chunks * count * size
    return pl.pallas_call(
        functools.partial(
            logits_kernel, zones, chunks, count, heads, size, rows, odd, ranks
        ),
        grid_spec=pltpu.PrefetchScalarGridSpec(
            num_scalar_prefetch=2,
            grid=(ranks // 2,),
            in_specs=[whole((rows, wide))] * len(flat)
            + [pl.BlockSpec((heads, part, full), pick)],
            out_specs=pl.BlockSpec((1, heads, part, full), lambda s, *_: (s, 0, 0, 0)),
            scratch_shapes=[
                pltpu.VMEM((heads, full, every), BF16),
                pltpu.VMEM((heads, SHORT, every), BF16),
                pltpu.VMEM((heads, full, every), BF16),
            ],
        ),
        out_shape=jax.ShapeDtypeStruct((ranks // 2, heads, part, full), BF16),
        compiler_params=params(),
        cost_estimate=cost(
            heads * full * full * every, 2 * heads * full * full, heads * full * full // 2
        ),
        name="logits",
    )(place, lengths, *flat, logits)


def input_kernel(zones, heads, size, ranks, first, last, place_ref, *refs):
    pieces = refs[:zones]
    x_ref, gain_ref, both_ref, resid_ref = refs[zones : zones + 4]
    refs = refs[zones + 4 :]
    if not first:
        old_ref, old_gain_ref = refs[:2]
        refs = refs[2:]
    grad_ref, total_ref = refs[:2]
    refs = refs[2:]
    if not last:
        gain_out_ref = refs[0]
        refs = refs[1:]
    weight_ref, norm_ref, back_ref = refs[:3]
    count, rows, depth = x_ref.shape
    width = heads * size
    for d in range(zones):
        other = lax.rem(place_ref[0] + d, zones)
        weight_ref[d * width : (d + 1) * width, :] = both_ref[other, :width, :]
    gain_sum = jnp.zeros((1, depth), F32) if first else old_gain_ref[...]
    for seq in range(count):
        at = slice(seq * rows, (seq + 1) * rows)
        hat, inverse = norm_of(x_ref[seq].astype(F32))
        norm_ref[at, :] = (hat * gain_ref[...]).astype(BF16)
        back = jnp.concatenate(
            [separate(piece[...], seq, count, heads, size) for piece in pieces], axis=1
        )
        back_ref[at, :] = back
        grad_norm = dot_nn(back, weight_ref[...])
        gain_sum = gain_sum + jnp.sum(grad_norm * hat, 0, keepdims=True)
        grad = resid_ref[at, :] + norm_back(grad_norm * gain_ref[...], hat, inverse)
        grad_ref[seq] = grad.astype(BF16)
    total = dot_tn(norm_ref[...], back_ref[...])
    if not first:
        total = total + old_ref[...]
    if not last:
        total_ref[...] = total
        gain_out_ref[...] = gain_sum
        return
    scratch_ref, extra_ref = refs[3:]
    scratch_ref[...] = total
    share = depth // ranks // zones
    for index in range(ranks * zones):
        extra_ref[index : index + 1, :share] = gain_sum[:, index * share : (index + 1) * share]
    store_square(place_ref, total_ref, scratch_ref, extra_ref, zones, ranks)


def input_grads(place, pieces, x, gain, both, resid, old, heads, ranks, last):
    zones = len(pieces)
    count, rows, depth = x.shape
    tokens = count * rows
    size = both.shape[1] // 2 // heads
    width = heads * size
    first = old is None
    operands = [*pieces, x, gain, both, resid] + ([] if first else list(old))
    shapes = [jax.ShapeDtypeStruct(x.shape, BF16)]
    scratch = [
        pltpu.VMEM((depth, depth), BF16),
        pltpu.VMEM((tokens, depth), BF16),
        pltpu.VMEM((tokens, depth), BF16),
    ]
    if last:
        shapes.append(
            jax.ShapeDtypeStruct((ranks, zones, depth // ranks + 16, depth // zones), BF16)
        )
        scratch += [pltpu.VMEM((depth, depth), F32), pltpu.VMEM((ranks * zones, width), F32)]
    else:
        shapes += [
            jax.ShapeDtypeStruct((depth, depth), F32),
            jax.ShapeDtypeStruct((1, depth), F32),
        ]
    return pl.pallas_call(
        functools.partial(input_kernel, zones, heads, size, ranks, first, last),
        grid_spec=pltpu.PrefetchScalarGridSpec(
            num_scalar_prefetch=1,
            grid=(1,),
            in_specs=[whole(operand.shape) for operand in operands],
            out_specs=[whole(shape.shape) for shape in shapes],
            scratch_shapes=scratch,
        ),
        out_shape=shapes,
        compiler_params=params(),
        cost_estimate=cost(
            4 * tokens * depth * depth, 12 * tokens * depth + 8 * depth * depth
        ),
        name="input",
    )(place, *operands)


def shift(value, axis, extent, by):
    by = by % extent
    return lax.ppermute(value, axis, [(i, (i + by) % extent) for i in range(extent)])


def flip(value, axis, extent, mask):
    return lax.ppermute(value, axis, [(i, i ^ mask) for i in range(extent)])


def exchange(pieces, axis, extent, sign):
    return [pieces[0]] + [
        shift(pieces[d], axis, extent, sign * d) for d in range(1, extent)
    ]


def widen(value):
    return value.astype(F32)


def reduce_dp(send, keep, ranks):
    rest = ranks // 8
    came = flip(send, "dp", ranks, 1)
    both = [
        widen(keep[q * rest : (q + 1) * rest]) + widen(came[q * rest : (q + 1) * rest])
        for q in range(4)
    ]
    total = both[0]
    for q in range(1, 4):
        total = total + widen(flip(both[q].astype(BF16), "dp", ranks, 2 * q))
    own = total[0]
    for third in range(1, rest):
        own = own + widen(flip(total[third].astype(BF16), "dp", ranks, 8 * third))
    return own


def reduce_head(blocks, zones, sign):
    total = blocks[0]
    for d in range(1, zones):
        total = total + widen(shift(blocks[d].astype(BF16), "head", zones, sign * d))
    return total


def local(
    zones,
    ranks,
    block_input,
    lengths,
    cotangent,
    norm1_gain,
    value_projection_weight,
    rand_logits,
    output_projection_weight,
    norm2_gain,
    up_projection_weight,
    up_bias,
    down_projection_weight,
    down_bias,
):
    seq_count, rows, depth = block_input.shape
    heads, full, _ = rand_logits.shape
    hidden = up_bias.shape[0]
    assert rows == SHORT and full == rows * zones and ranks % 8 == 0
    count = 2
    chunks = seq_count // count
    place = jnp.stack([lax.axis_index("head"), lax.axis_index("dp")]).astype(jnp.int32)
    gain1, gain2 = norm1_gain[None], norm2_gain[None]
    width = value_projection_weight.shape[1]

    shard = jnp.concatenate([value_projection_weight.T, output_projection_weight], 0)
    slot = 2 * width // ranks
    shard = lax.dynamic_slice_in_dim(shard, place[1] * slot, slot, 0)
    both = lax.all_gather(shard, ("head", "dp"), axis=0, tiled=True)
    both = both.reshape(zones, 2 * width, depth)

    probs, probs_t, corner, corner_t = make_probs(rand_logits)

    def part(array, c):
        return array[c * count : (c + 1) * count]

    values, mixed = [], []
    for c in range(chunks):
        made = make_values(place, part(block_input, c), gain1, both, heads)
        values.append(exchange(made, "head", zones, 1))
    for c in range(chunks):
        made = mix(place, part(lengths, c), values[c], probs, corner, count, 1)
        mixed.append(exchange(made, "head", zones, 1))

    fed, grads = [], []
    for c in range(chunks):
        out = feed(
            place,
            mixed[c],
            part(block_input, c),
            part(cotangent, c),
            both,
            gain2,
            up_projection_weight,
            up_bias[None],
            down_projection_weight,
            down_bias[None],
            heads,
        )
        grads.append(exchange(out[:zones], "head", zones, -1))
        fed.append(out[zones:])
    blocks, resids, acts, pres, norms, mixes, attends, up_sums, sums = zip(*fed)

    cots = [part(cotangent, c).reshape(count * rows, depth) for c in range(chunks)]
    halves = [
        weight_grads(place, acts, pres, norms, cots, odd, zones, ranks) for odd in (1, 0)
    ]
    ff = reduce_dp(*halves, ranks)
    ff = reduce_head(ff, zones, 1)

    up_total = sum(up_sums[1:], up_sums[0]).reshape(ranks * zones, -1)
    rest_total = sum(sums[1:], sums[0])
    extra = jnp.concatenate(
        [
            up_total,
            rest_total[0].reshape(ranks * zones, -1),
            rest_total[1].reshape(ranks * zones, -1),
        ],
        1,
    )
    extra = jnp.pad(extra, ((0, 0), (0, width - extra.shape[1])))
    out_blocks = out_weight_grads(place, attends, mixes, extra, zones, ranks)
    half = ranks // 2
    out_total = reduce_dp(out_blocks[half:], out_blocks[:half], ranks)
    out_square = reduce_head(out_total[:, : depth // ranks], zones, -1)
    extra_total = reduce_head(out_total[:, depth // ranks], zones, 1)

    backs = []
    for c in range(chunks):
        made = mix(place, part(lengths, c), grads[c], probs_t, corner_t, count, -1)
        backs.append(exchange(made, "head", zones, -1))

    rand = [
        logit_grads(place, lengths, grads, values, rand_logits, odd, ranks, count)
        for odd in (1, 0)
    ]
    grad_rand = reduce_dp(*rand, ranks)

    inputs, old = [], None
    for c in range(chunks):
        out = input_grads(
            place,
            backs[c],
            part(block_input, c),
            gain1,
            both,
            resids[c],
            old,
            heads,
            ranks,
            c == chunks - 1,
        )
        inputs.append(out[0])
        old = out[1:]
    value_total = reduce_dp(old[0][half:], old[0][:half], ranks)
    value_total = reduce_head(value_total, zones, 1)
    block_rows = depth // ranks

    up_size, gain_size = hidden // ranks // zones, depth // ranks // zones
    return (
        jnp.concatenate(blocks, 0),
        jnp.concatenate(inputs, 0),
        grad_rand,
        value_total[:block_rows],
        out_square.T,
        value_total[block_rows, :gain_size],
        extra_total[up_size : up_size + gain_size],
        ff[0].T,
        extra_total[:up_size],
        ff[1],
        extra_total[up_size + gain_size : up_size + 2 * gain_size],
    )


def solution(mesh):
    in_specs = (
        P("dp", "head", None),
        P("dp"),
        P("dp", "head", None),
        P(),
        P(None, "head"),
        P("head", None, None),
        P("head", None),
        P(),
        P(),
        P(),
        P(),
        P(),
    )
    out_specs = (
        P("dp", "head", None),
        P("dp", "head", None),
        P("head", "dp", None),
        P("dp", "head"),
        P("head", "dp"),
        P(("dp", "head")),
        P(("dp", "head")),
        P(None, ("dp", "head")),
        P(("dp", "head")),
        P(("dp", "head"), None),
        P(("dp", "head")),
    )
    body = functools.partial(local, mesh.shape["head"], mesh.shape["dp"])
    return jax.shard_map(
        body, mesh=mesh, in_specs=in_specs, out_specs=out_specs, check_vma=False
    )
```

```python
import functools

import jax
import jax.numpy as jnp
from jax import lax
from jax.experimental import pallas as pl
from jax.experimental.pallas import tpu as pltpu
from jax.sharding import PartitionSpec as P

SHORT = 256
EPSILON = 1e-05
F32 = jnp.float32
BF16 = jnp.bfloat16
GELU_C = 0.7978845608028654
GELU_A = 0.044715
SHARE = 1.0


def dot_nn(a, b):
    return lax.dot_general(a, b, (((1,), (0,)), ((), ())), preferred_element_type=F32)


def dot_nt(a, b):
    return lax.dot_general(a, b, (((1,), (1,)), ((), ())), preferred_element_type=F32)


def dot_tn(a, b):
    return lax.dot_general(a, b, (((0,), (0,)), ((), ())), preferred_element_type=F32)


def norm_of(value):
    centered = value - jnp.mean(value, -1, keepdims=True)
    inverse = lax.rsqrt(jnp.mean(centered * centered, -1, keepdims=True) + EPSILON)
    return centered * inverse, inverse


def norm_back(scaled, hat, inverse):
    return inverse * (
        scaled
        - jnp.mean(scaled, -1, keepdims=True)
        - hat * jnp.mean(scaled * hat, -1, keepdims=True)
    )


def interleave(values, heads, size):
    parts = []
    for head in range(heads):
        for value in values:
            parts.append(value[:, head * size : (head + 1) * size])
    return jnp.concatenate(parts, axis=1)


def separate(piece, seq, count, heads, size):
    parts = []
    for head in range(heads):
        at = (head * count + seq) * size
        parts.append(piece[:, at : at + size])
    return jnp.concatenate(parts, axis=1)


def far(shape, dtype):
    return pltpu.HBM(shape, dtype)


def kept(value):
    return pltpu.with_memory_space_constraint(value, pltpu.HBM)


def whole(shape):
    return pl.BlockSpec(
        shape, lambda *_: (0,) * len(shape), pipeline_mode=pl.Buffered(buffer_count=1)
    )


def resident():
    return pl.BlockSpec(memory_space=pltpu.VMEM)


def cost(flops, moved, special=0):
    return pl.CostEstimate(
        flops=int(flops * SHARE), bytes_accessed=int(moved * SHARE), transcendentals=0
    )


def params(megabytes, grid_dims=1):
    return pltpu.CompilerParams(
        dimension_semantics=("arbitrary",) * grid_dims, vmem_limit_bytes=megabytes << 20
    )


def probs_kernel(logit_ref, long_ref, long_t_ref, short_ref, short_t_ref):
    logits = logit_ref[0].astype(F32)
    raised = jnp.exp(logits - jnp.max(logits, -1, keepdims=True))
    probs = raised / jnp.sum(raised, -1, keepdims=True)
    long_ref[0] = probs.astype(BF16)
    long_t_ref[0] = probs.T.astype(BF16)

    @pl.when(pl.program_id(1) == 0)
    def _():
        corner = logits[:, :SHORT]
        lifted = jnp.exp(corner - jnp.max(corner, -1, keepdims=True))
        part = lifted / jnp.sum(lifted, -1, keepdims=True)
        short_ref[0] = part.astype(BF16)
        short_t_ref[0] = part.T.astype(BF16)


def make_probs(logits):
    heads, rows, _ = logits.shape
    return pl.pallas_call(
        probs_kernel,
        grid=(heads, rows // SHORT),
        in_specs=[pl.BlockSpec((1, SHORT, rows), lambda h, i: (h, i, 0))],
        out_specs=[
            pl.BlockSpec((1, SHORT, rows), lambda h, i: (h, i, 0)),
            pl.BlockSpec((1, rows, SHORT), lambda h, i: (h, 0, i)),
            pl.BlockSpec((1, SHORT, SHORT), lambda h, i: (h, 0, 0)),
            pl.BlockSpec((1, SHORT, SHORT), lambda h, i: (h, 0, 0)),
        ],
        out_shape=[
            far((heads, rows, rows), BF16),
            far((heads, rows, rows), BF16),
            jax.ShapeDtypeStruct((heads, SHORT, SHORT), BF16),
            jax.ShapeDtypeStruct((heads, SHORT, SHORT), BF16),
        ],
        compiler_params=params(20, 2),
        cost_estimate=cost(10 * logits.size, 6 * logits.size, logits.size),
        name="probs",
    )(kept(logits))


def values_kernel(zones, heads, size, first, place_ref, x_ref, gain_ref, *rest):
    width = heads * size
    if first:
        own_ref, others_ref = rest[0], rest[zones]
        mine = rest[1:zones]
        outs, weight_ref = rest[zones + 1 : 2 * zones + 1], rest[2 * zones + 1]
        half = width // 2
        parity = lax.rem(place_ref[1], 2)
        weight_ref[:width, :] = own_ref[...]
        for d in range(1, zones):
            at = pl.multiple_of(d * width + parity * half, 16)
            weight_ref[pl.ds(at, half), :] = mine[d - 1][...]
            at = pl.multiple_of(d * width + (1 - parity) * half, 16)
            weight_ref[pl.ds(at, half), :] = others_ref[d - 1]
    else:
        weight_ref, outs = rest[0], rest[1:]
    made = []
    for seq in range(x_ref.shape[0]):
        hat, _ = norm_of(x_ref[seq].astype(F32))
        norm = (hat * gain_ref[...]).astype(BF16)
        made.append(dot_nt(norm, weight_ref[...]))
    for d in range(zones):
        own = [value[:, d * width : (d + 1) * width] for value in made]
        outs[d][...] = interleave(own, heads, size).astype(BF16)


def make_values(place, x, gain, weights, zones, heads, first):
    count, rows, depth = x.shape
    wide = count * depth // zones
    operands = [x, gain, *weights]
    shapes = [jax.ShapeDtypeStruct((rows, wide), BF16)] * zones
    if first:
        shapes.append(jax.ShapeDtypeStruct((depth, depth), BF16))
    return pl.pallas_call(
        functools.partial(values_kernel, zones, heads, depth // zones // heads, first),
        grid_spec=pltpu.PrefetchScalarGridSpec(
            num_scalar_prefetch=1,
            grid=(1,),
            in_specs=[whole(operand.shape) for operand in operands],
            out_specs=[whole(shape.shape) for shape in shapes],
        ),
        out_shape=shapes,
        compiler_params=params(12),
        cost_estimate=cost(
            2 * count * rows * depth * depth, 2 * x.size * 2 + 4 * depth * depth
        ),
        name="values",
    )(place, *operands)


def mix_kernel(zones, chunks, count, size, rows, sign, place_ref, long_flags, *refs):
    pieces = refs[: chunks * zones]
    matrix_ref, corner_ref = refs[chunks * zones : chunks * zones + 2]
    outs, held = refs[chunks * zones + 2 : -1], refs[-1]
    place = place_ref[0]
    wide = count * size
    for c in range(chunks):
        for d in range(zones):
            source = lax.rem(place + zones - sign * d, zones)
            at = pl.ds(pl.multiple_of(source * rows, rows), rows)
            held[at, c * wide : (c + 1) * wide] = pieces[c * zones + d][...]
    lane = lax.broadcasted_iota(jnp.int32, (1, chunks * wide), 1)
    is_long = jnp.zeros((1, chunks * wide), jnp.bool_)
    for seq in range(chunks * count):
        inside = (lane >= seq * size) & (lane < (seq + 1) * size)
        is_long = is_long | (inside & (long_flags[seq] > SHORT))
    corner = dot_nn(corner_ref[0], held[:SHORT, :])
    for d in range(zones):
        target = lax.rem(place + zones + sign * d, zones)
        part = matrix_ref[0, pl.ds(pl.multiple_of(target * rows, rows), rows), :]
        full = dot_nn(part, held[...])
        small = jnp.where(target == 0, corner, jnp.zeros_like(corner))
        outs[d][...] = jnp.where(is_long, full, small).astype(BF16)


def mix(place, lengths, groups, matrix, corner, count, sign):
    chunks, zones = len(groups), len(groups[0])
    heads, full, _ = matrix.shape
    rows, wide = groups[0][0].shape
    lanes = wide // heads
    spec = pl.BlockSpec((rows, lanes), lambda h, *_: (0, h))
    out_spec = pl.BlockSpec((rows, chunks * lanes), lambda h, *_: (0, h))
    return pl.pallas_call(
        functools.partial(mix_kernel, zones, chunks, count, lanes // count, rows, sign),
        grid_spec=pltpu.PrefetchScalarGridSpec(
            num_scalar_prefetch=2,
            grid=(heads,),
            in_specs=[spec] * (chunks * zones)
            + [
                pl.BlockSpec((1, full, full), lambda h, *_: (h, 0, 0)),
                pl.BlockSpec((1, SHORT, SHORT), lambda h, *_: (h, 0, 0)),
            ],
            out_specs=[out_spec] * zones,
            scratch_shapes=[pltpu.VMEM((full, chunks * lanes), BF16)],
        ),
        out_shape=[jax.ShapeDtypeStruct((rows, chunks * wide), BF16)] * zones,
        compiler_params=params(16),
        cost_estimate=cost(
            2 * heads * full * full * lanes * chunks,
            2 * heads * full * full + 4 * full * wide * chunks,
        ),
        name="mix",
    )(place, lengths, *(piece for group in groups for piece in group), kept(matrix), corner)


def feed_kernel(zones, heads, size, steps, place_ref, *refs):
    pieces = refs[:zones]
    (x_ref, cot_ref, project_ref, gain_ref, up_ref, up_bias_ref, down_ref, down_bias_ref) = refs[
        zones : zones + 8
    ]
    outs = refs[zones + 8 :]
    grads = outs[:zones]
    (
        block_ref,
        resid_grad_ref,
        act_t_ref,
        pre_t_ref,
        norm_ref,
        mixed_ref,
        attended_ref,
        up_sum_ref,
        sums_ref,
        weight_ref,
        resid_ref,
        hat_ref,
        inv_ref,
        forward_ref,
        back_ref,
    ) = outs[zones:]
    count, rows, depth = x_ref.shape
    width = heads * size
    step = pl.program_id(0)

    @pl.when(step == 0)
    def _():
        for d in range(zones):
            other = lax.rem(place_ref[0] + zones - d, zones)
            at = pl.multiple_of(other * width, 16)
            weight_ref[d * width : (d + 1) * width, :] = project_ref[pl.ds(at, width), :]
        for seq in range(count):
            at = slice(seq * rows, (seq + 1) * rows)
            mixed = jnp.concatenate(
                [separate(piece[...], seq, count, heads, size) for piece in pieces], axis=1
            )
            mixed_ref[at, :] = mixed
            resid = x_ref[seq].astype(F32) + dot_nn(mixed, weight_ref[...])
            hat, inverse = norm_of(resid)
            resid_ref[at, :] = resid + down_bias_ref[...]
            hat_ref[at, :] = hat
            inv_ref[at, :] = inverse
            norm_ref[at, :] = (hat * gain_ref[...]).astype(BF16)
        forward_ref[...] = jnp.zeros_like(forward_ref)
        back_ref[...] = jnp.zeros_like(back_ref)

    up_sum = jnp.zeros((1, up_ref.shape[1]), F32)
    for seq in range(count):
        at = slice(seq * rows, (seq + 1) * rows)
        pre = dot_nn(norm_ref[at, :], up_ref[...]) + up_bias_ref[...]
        grad_act = dot_nt(cot_ref[seq], down_ref[...])
        square = pre * pre
        bent = jnp.tanh(pre * (GELU_C + (GELU_C * GELU_A) * square))
        half = 0.5 + 0.5 * bent
        act = (pre * half).astype(BF16)
        slope = half + (0.5 * pre) * (1.0 - bent * bent) * (
            GELU_C + (3.0 * GELU_C * GELU_A) * square
        )
        grad_pre = (grad_act * slope).astype(BF16)
        up_sum = up_sum + jnp.sum(grad_pre.astype(F32), 0, keepdims=True)
        act_t_ref[:, at] = act.T
        pre_t_ref[:, at] = grad_pre.T
        forward = dot_nn(act, down_ref[...])
        back = dot_nt(grad_pre, up_ref[...])

        forward_ref[at, :] += forward
        back_ref[at, :] += back

    up_sum_ref[...] = up_sum

    @pl.when(step == steps - 1)
    def _():
        gain_sum = jnp.zeros((1, depth), F32)
        bias_sum = jnp.zeros((1, depth), F32)
        made = []
        for seq in range(count):
            at = slice(seq * rows, (seq + 1) * rows)
            block_ref[seq] = (resid_ref[at, :] + forward_ref[at, :]).astype(BF16)
            cot = cot_ref[seq].astype(F32)
            hat = hat_ref[at, :]
            back = back_ref[at, :]
            gain_sum = gain_sum + jnp.sum(back * hat, 0, keepdims=True)
            bias_sum = bias_sum + jnp.sum(cot, 0, keepdims=True)
            grad = cot + norm_back(back * gain_ref[...], hat, inv_ref[at, :])
            resid_grad_ref[at, :] = grad
            low = grad.astype(BF16)
            attended_ref[:, at] = low.T
            made.append(dot_nt(low, weight_ref[...]))
        sums_ref[0:1, :] = gain_sum
        sums_ref[1:2, :] = bias_sum
        for d in range(zones):
            mine = [value[:, d * width : (d + 1) * width] for value in made]
            grads[d][...] = interleave(mine, heads, size).astype(BF16)


def feed(place, pieces, x, cot, project, gain, up, up_bias, down, down_bias, heads):
    zones = len(pieces)
    count, rows, depth = x.shape
    size = depth // zones // heads
    hidden = up.shape[1]
    tile = min(512, hidden)
    steps = hidden // tile
    tokens = count * rows
    wide = pieces[0].shape[1]
    shapes = [jax.ShapeDtypeStruct((rows, wide), BF16)] * zones + [
        far((count, rows, depth), BF16),
        far((tokens, depth), F32),
        far((hidden, tokens), BF16),
        far((hidden, tokens), BF16),
        far((tokens, depth), BF16),
        far((tokens, depth), BF16),
        far((depth, tokens), BF16),
        jax.ShapeDtypeStruct((1, hidden), F32),
        jax.ShapeDtypeStruct((2, depth), F32),
    ]
    return pl.pallas_call(
        functools.partial(feed_kernel, zones, heads, size, steps),
        grid_spec=pltpu.PrefetchScalarGridSpec(
            num_scalar_prefetch=1,
            grid=(steps,),
            in_specs=[whole((rows, wide))] * zones
            + [
                whole(x.shape),
                whole(cot.shape),
                whole(project.shape),
                whole(gain.shape),
                pl.BlockSpec((depth, tile), lambda f, *_: (0, f)),
                pl.BlockSpec((1, tile), lambda f, *_: (0, f)),
                pl.BlockSpec((tile, depth), lambda f, *_: (f, 0)),
                whole(down_bias.shape),
            ],
            out_specs=[whole((rows, wide))] * zones
            + [
                whole((count, rows, depth)),
                whole((tokens, depth)),
                pl.BlockSpec((tile, tokens), lambda f, *_: (f, 0)),
                pl.BlockSpec((tile, tokens), lambda f, *_: (f, 0)),
                whole((tokens, depth)),
                whole((tokens, depth)),
                whole((depth, tokens)),
                pl.BlockSpec((1, tile), lambda f, *_: (0, f)),
                whole((2, depth)),
            ],
            scratch_shapes=[
                pltpu.VMEM((depth, depth), BF16),
                pltpu.VMEM((tokens, depth), F32),
                pltpu.VMEM((tokens, depth), F32),
                pltpu.VMEM((tokens, 1), F32),
                pltpu.VMEM((tokens, depth), F32),
                pltpu.VMEM((tokens, depth), F32),
            ],
        ),
        out_shape=shapes,
        compiler_params=params(28),
        cost_estimate=cost(
            8 * tokens * depth * hidden + 4 * tokens * depth * depth,
            4 * depth * hidden + 4 * tokens * hidden + 20 * tokens * depth,
            tokens * hidden,
        ),
        name="feed",
    )(
        place,
        *map(kept, pieces),
        kept(x),
        kept(cot),
        kept(project),
        gain,
        kept(up),
        up_bias,
        kept(down),
        down_bias,
    )


def relative_block(step, odd, ranks):
    rest = ranks // 8
    return odd + 2 * (step // rest) + 8 * lax.rem(step, rest)


def group_rows(rows, zones):
    return -(-rows // (8 * zones)) * 8


def pack(block, d, zones):
    rows, depth = block.shape
    width, group = depth // zones, group_rows(rows, zones)
    parts = []
    for k in range(zones):
        if k * group < rows:
            parts.append(block[k * group : (k + 1) * group, d * width : (d + 1) * width])
        else:
            parts.append(jnp.zeros((group, width), block.dtype))
    return jnp.concatenate(parts, axis=1)


def unpack(packed, rows, zones):
    group, depth = packed.shape
    spread = packed.reshape(group, zones, depth // zones).swapaxes(0, 1)
    return spread.reshape(group * zones, depth // zones)[:rows]


def place_first(second):
    return second // 2 + 2 * (1 - lax.rem(second, 2))


def place_second(second):
    return lax.rem(second + 2, 4)


def weights_kernel(zones, chunks, place_ref, *refs):
    acts, pres = refs[:chunks], refs[chunks : 2 * chunks]
    attends = refs[2 * chunks : 3 * chunks]
    norms, cots = refs[3 * chunks : 4 * chunks], refs[4 * chunks : 5 * chunks]
    mixes = refs[5 * chunks : 6 * chunks]
    first_ref, second_ref, scratch_ref = refs[6 * chunks :]
    part = scratch_ref.shape[1] // zones

    def total(lefts, rights):
        result = dot_nn(lefts[0][...], rights[0][...])
        for left, right in zip(lefts[1:], rights[1:]):
            result = result + dot_nn(left[...], right[...])
        return result

    scratch_ref[0] = total(pres, norms)
    scratch_ref[1] = total(acts, cots)
    square = total(attends, mixes)
    for d in range(zones):
        at = pl.ds(pl.multiple_of(lax.rem(place_ref[0] + d, zones) * part, 8), part)
        parts = [scratch_ref[0, at, :], scratch_ref[1, at, :], pack(square, -d % zones, zones)]
        used = sum(value.shape[0] for value in parts)
        parts.append(jnp.zeros((first_ref.shape[2] - used, first_ref.shape[3]), F32))
        side, number = (first_ref, d) if d < zones // 2 else (second_ref, d - zones // 2)
        side[0, number] = jnp.concatenate(parts, axis=0).astype(BF16)


def weight_grads(place, acts, pres, attends, norms, cots, mixes, odd, zones, ranks):
    chunks = len(acts)
    hidden, tokens = acts[0].shape
    depth = norms[0].shape[1]
    tile, square = hidden // ranks, depth // ranks
    rows = 2 * tile // zones + group_rows(square, zones)
    rows = -(-rows // 16) * 16
    rest = ranks // 8

    def tall(step, place_ref):
        return (lax.bitwise_xor(place_ref[1], relative_block(step, odd, ranks)), 0)

    def first(step, _):
        return (place_first(step // rest) * rest + lax.rem(step, rest), 0, 0, 0)

    def second(step, _):
        return (place_second(step // rest) * rest + lax.rem(step, rest), 0, 0, 0)

    shape = (ranks // 2, zones // 2, rows, depth)
    return pl.pallas_call(
        functools.partial(weights_kernel, zones, chunks),
        grid_spec=pltpu.PrefetchScalarGridSpec(
            num_scalar_prefetch=1,
            grid=(ranks // 2,),
            in_specs=[pl.BlockSpec((tile, tokens), tall)] * (2 * chunks)
            + [pl.BlockSpec((square, tokens), tall)] * chunks
            + [whole((tokens, depth))] * (3 * chunks),
            out_specs=[pl.BlockSpec((1, *shape[1:]), first), pl.BlockSpec((1, *shape[1:]), second)],
            scratch_shapes=[pltpu.VMEM((2, tile, depth), F32)],
        ),
        out_shape=[far(shape, BF16)] * 2,
        compiler_params=params(24),
        cost_estimate=cost(
            2 * chunks * hidden * tokens * depth,
            2 * chunks * hidden * tokens + 2 * hidden * depth + 4 * chunks * tokens * depth,
        ),
        name="weights",
    )(
        place,
        *map(kept, acts),
        *map(kept, pres),
        *map(kept, attends),
        *map(kept, norms),
        *map(kept, cots),
        *map(kept, mixes),
    )


def store_square(place_ref, outs, scratch_ref, extra_ref, zones, ranks):
    depth = scratch_ref.shape[0]
    part = depth // ranks
    for odd, out_ref in zip((1, 0), outs):
        for step in range(ranks // 2):
            rest = ranks // 8
            relative = odd + 2 * (step // rest) + 8 * (step % rest)
            rank = lax.bitwise_xor(place_ref[1], relative)
            block = scratch_ref[pl.ds(pl.multiple_of(rank * part, 8), part), :]
            for d in range(zones):
                zone = lax.rem(place_ref[0] + d, zones)
                line = extra_ref[pl.ds(rank * zones + zone, 1), :]
                packed = pack(block, d, zones)
                below = jnp.broadcast_to(line, (out_ref.shape[2] - packed.shape[0], depth))
                out_ref[step, d] = jnp.concatenate([packed, below], axis=0).astype(BF16)


def logits_kernel(
    zones, chunks, count, heads, size, rows, ranks, place_ref, lengths_ref, *refs
):
    grads = refs[: chunks * zones]
    values = refs[chunks * zones : 2 * chunks * zones]
    refs = refs[2 * chunks * zones :]
    logit_ref, sends, keeps = refs[0], refs[1:3], refs[3:5]
    long_ref, short_ref, value_ref, out_ref = refs[5:]
    place = place_ref[0]
    lanes = count * size
    step = pl.program_id(0)

    @pl.when(step == 0)
    def _():
        lane = lax.broadcasted_iota(jnp.int32, (1, lanes), 1)
        for c in range(chunks):
            is_long = jnp.zeros((1, lanes), jnp.bool_)
            for seq in range(count):
                inside = (lane >= seq * size) & (lane < (seq + 1) * size)
                is_long = is_long | (inside & (lengths_ref[c * count + seq] > SHORT))
            for d in range(zones):
                ahead = lax.rem(place + d, zones)
                behind = lax.rem(place + zones - d, zones)
                to = pl.ds(pl.multiple_of(ahead * rows, rows), rows)
                back = pl.ds(pl.multiple_of(behind * rows, rows), rows)
                for head in range(heads):
                    columns = slice(head * lanes, (head + 1) * lanes)
                    own = slice(c * lanes, (c + 1) * lanes)
                    grad = grads[c * zones + d][:, columns].astype(F32)
                    long_ref[head, to, own] = jnp.where(is_long, grad, 0.0).astype(BF16)
                    value_ref[head, back, own] = values[c * zones + d][:, columns]

                    @pl.when(ahead == 0)
                    def _():
                        short_ref[head, :, own] = jnp.where(is_long, 0.0, grad).astype(BF16)

    odd = jnp.where(step < ranks // 2, 1, 0)
    rank = lax.bitwise_xor(
        place_ref[1], relative_block(lax.rem(step, ranks // 2), odd, ranks)
    )
    part = logit_ref.shape[1]
    middle = part // 2
    start = rank * part
    for head in range(heads):
        logits = logit_ref[head].astype(F32)
        raised = jnp.exp(logits - jnp.max(logits, -1, keepdims=True))
        probs = raised / jnp.sum(raised, -1, keepdims=True)
        at = pl.ds(pl.multiple_of(start, part), part)
        total = dot_nt(long_ref[head, at, :], value_ref[head])
        out_ref[head] = probs * (total - jnp.sum(total * probs, -1, keepdims=True))

        @pl.when(start < SHORT)
        def _():
            corner = logits[:, :SHORT]
            lifted = jnp.exp(corner - jnp.max(corner, -1, keepdims=True))
            small = lifted / jnp.sum(lifted, -1, keepdims=True)
            sums = dot_nt(short_ref[head, at, :], value_ref[head, :SHORT, :])
            more = small * (sums - jnp.sum(sums * small, -1, keepdims=True))
            out_ref[head, :, :SHORT] += more

    @pl.when(step < ranks // 2)
    def _():
        sends[0][0] = out_ref[:, :middle, :].astype(BF16)
        sends[1][0] = out_ref[:, middle:, :].astype(BF16)

    @pl.when(step >= ranks // 2)
    def _():
        keeps[0][0] = out_ref[:, :middle, :].astype(BF16)
        keeps[1][0] = out_ref[:, middle:, :].astype(BF16)


def logit_grads(place, lengths, grads, values, logits, ranks, count):
    chunks, zones = len(grads), len(grads[0])
    heads, full, _ = logits.shape
    rows, wide = grads[0][0].shape
    size = wide // heads // count
    part = full // ranks
    half, rest = ranks // 2, ranks // 8

    def pick(step, place_ref, _):
        odd = jnp.where(step < half, 1, 0)
        block = relative_block(lax.rem(step, half), odd, ranks)
        return (0, lax.bitwise_xor(place_ref[1], block), 0)

    def spec(order, keep):
        def number(step, *_):
            at = jnp.maximum(step - half, 0) if keep else jnp.minimum(step, half - 1)
            return (order(at // rest) * rest + lax.rem(at, rest), 0, 0, 0)

        return pl.BlockSpec((1, heads, part // 2, full), number)

    flat = [piece for group in grads for piece in group] + [
        piece for group in values for piece in group
    ]
    every = chunks * count * size
    shape = (half, heads, part // 2, full)
    return pl.pallas_call(
        functools.partial(logits_kernel, zones, chunks, count, heads, size, rows, ranks),
        grid_spec=pltpu.PrefetchScalarGridSpec(
            num_scalar_prefetch=2,
            grid=(ranks,),
            in_specs=[whole((rows, wide))] * len(flat)
            + [pl.BlockSpec((heads, part, full), pick)],
            out_specs=[
                spec(order, keep) for keep in (False, True) for order in (place_first, place_second)
            ],
            scratch_shapes=[
                pltpu.VMEM((heads, full, every), BF16),
                pltpu.VMEM((heads, SHORT, every), BF16),
                pltpu.VMEM((heads, full, every), BF16),
                pltpu.VMEM((heads, part, full), F32),
            ],
        ),
        out_shape=[far(shape, BF16)] * 4,
        compiler_params=params(24),
        cost_estimate=cost(
            2 * heads * full * full * every, 4 * heads * full * full, heads * full * full
        ),
        name="logits",
    )(place, lengths, *map(kept, flat), kept(logits))


def input_kernel(zones, heads, size, ranks, count, place_ref, *refs):
    pieces = refs[:zones]
    x_ref, gain_ref, weight_ref, resid_ref, extra_in_ref = refs[zones : zones + 5]
    grad_ref, send_ref, keep_ref, total_ref, gain_sum_ref, extra_ref = refs[zones + 5 :]
    depth = x_ref.shape[2]
    seq = pl.program_id(0)

    @pl.when(seq == 0)
    def _():
        total_ref[...] = jnp.zeros_like(total_ref)
        gain_sum_ref[...] = jnp.zeros_like(gain_sum_ref)

    hat, inverse = norm_of(x_ref[0].astype(F32))
    norm = (hat * gain_ref[...]).astype(BF16)
    pair = 128 // size
    parts = []
    lane = lax.broadcasted_iota(jnp.int32, (1, 128), 1)
    for piece in pieces:
        for head in range(heads):
            at = pl.multiple_of((head * count + seq // pair * pair) * size, 128)
            both = piece[:, pl.ds(at, 128)].astype(F32)
            moved = pltpu.roll(both, shift=size, axis=1)
            parts.append(jnp.where(lax.rem(seq, pair) == 0, both, moved)[:, :size])
    back = jnp.concatenate(parts, axis=1).astype(BF16)
    grad_norm = dot_nn(back, weight_ref[...])
    gain_sum_ref[...] += jnp.sum(grad_norm * hat, 0, keepdims=True)
    grad = resid_ref[...] + norm_back(grad_norm * gain_ref[...], hat, inverse)
    grad_ref[0] = grad.astype(BF16)
    total_ref[...] += dot_tn(norm, back)

    @pl.when(seq == count - 1)
    def _():
        extra_ref[...] = extra_in_ref[...]
        share = depth // ranks // zones
        for index in range(ranks * zones):
            extra_ref[index : index + 1, :share] = gain_sum_ref[
                :, index * share : (index + 1) * share
            ]
        store_square(place_ref, (send_ref, keep_ref), total_ref, extra_ref, zones, ranks)


def input_grads(place, pieces, x, gain, weight, resid, extra, heads, ranks):
    zones = len(pieces)
    count, rows, depth = x.shape
    size = depth // zones // heads
    assert 2 * size == 128 and count % 2 == 0
    height = -(-(group_rows(depth // ranks, zones) + 1) // 16) * 16
    shape = (ranks // 2, zones, height, depth)
    return pl.pallas_call(
        functools.partial(input_kernel, zones, heads, size, ranks, count),
        grid_spec=pltpu.PrefetchScalarGridSpec(
            num_scalar_prefetch=1,
            grid=(count,),
            in_specs=[whole(pieces[0].shape)] * zones
            + [
                pl.BlockSpec((1, rows, depth), lambda s, *_: (s, 0, 0)),
                whole(gain.shape),
                whole(weight.shape),
                pl.BlockSpec((rows, depth), lambda s, *_: (s, 0)),
                whole(extra.shape),
            ],
            out_specs=[
                pl.BlockSpec((1, rows, depth), lambda s, *_: (s, 0, 0)),
                whole(shape),
                whole(shape),
            ],
            scratch_shapes=[
                pltpu.VMEM((depth, depth), F32),
                pltpu.VMEM((1, depth), F32),
                pltpu.VMEM(extra.shape, F32),
            ],
        ),
        out_shape=[
            far(x.shape, BF16),
            jax.ShapeDtypeStruct(shape, BF16),
            jax.ShapeDtypeStruct(shape, BF16),
        ],
        compiler_params=params(24),
        cost_estimate=cost(
            4 * count * rows * depth * depth, 12 * count * rows * depth + 8 * depth * depth
        ),
        name="input",
    )(place, *map(kept, pieces), kept(x), gain, kept(weight), kept(resid), extra)


def shift(value, axis, extent, by):
    by = by % extent
    return lax.ppermute(value, axis, [(i, (i + by) % extent) for i in range(extent)])


def flip(value, axis, extent, mask):
    return lax.ppermute(value, axis, [(i, i ^ mask) for i in range(extent)])


def widen(value):
    return value.astype(F32)


def after(value, *results):
    return lax.optimization_barrier((value, *results))[0]


def exchange(pieces, extent, sign, *results):
    sent = pieces[1:]
    if results:
        sent = lax.optimization_barrier((*sent, *results))[: extent - 1]
    return [pieces[0]] + [
        shift(piece, "head", extent, sign * (d + 1)) for d, piece in enumerate(sent)
    ]


def exchange_some(pieces, numbers, extent, sign, *results):
    sent = [pieces[d] for d in numbers]
    if results:
        sent = lax.optimization_barrier((*sent, *results))[: len(sent)]
    return [shift(piece, "head", extent, sign * d) for d, piece in zip(numbers, sent)]


class Reduce:
    masks = ((2, 4), (4, 2))

    def __init__(self, ranks):
        self.ranks = ranks

    def core(self, sends):
        self.came = [flip(send, "dp", self.ranks, 1) for send in sends]

    def first(self, keeps, *results):
        half = self.ranks // 4
        sent = [
            (widen(keep[:half]) + widen(came[:half])).astype(BF16)
            for keep, came in zip(keeps, self.came)
        ]
        if results:
            sent = lax.optimization_barrier((*sent, *results))[:2]
        self.keeps = keeps
        self.went = [
            flip(value, "dp", self.ranks, masks[0]) for value, masks in zip(sent, self.masks)
        ]

    def second(self, *results):
        half, rest = self.ranks // 4, self.ranks // 8
        rests = [
            widen(keep[half:]) + widen(came[half:]) + widen(went)
            for keep, came, went in zip(self.keeps, self.came, self.went)
        ]
        self.own = [value[:rest] for value in rests]
        sent = [value[rest:].astype(BF16) for value in rests]
        if results:
            sent = lax.optimization_barrier((*sent, *results))[:2]
        self.last = [
            flip(value, "dp", self.ranks, masks[1]) for value, masks in zip(sent, self.masks)
        ]

    def finish(self):
        sides = []
        for own, last in zip(self.own, self.last):
            total = own + widen(last)
            side = total[0]
            for third in range(1, self.ranks // 8):
                side = side + widen(flip(total[third].astype(BF16), "dp", self.ranks, 8 * third))
            sides.append(side)
        return sides


def reduce_direct(send, keep, ranks, *results):
    rest = ranks // 8
    came = flip(send, "dp", ranks, 1)
    both = [
        widen(keep[q * rest : (q + 1) * rest]) + widen(came[q * rest : (q + 1) * rest])
        for q in range(4)
    ]
    sent = lax.optimization_barrier((*(part.astype(BF16) for part in both[1:]), *results))
    total = both[0]
    for q in range(1, 4):
        total = total + widen(flip(sent[q - 1], "dp", ranks, 2 * q))
    own = total[0]
    for third in range(1, rest):
        own = own + widen(flip(total[third].astype(BF16), "dp", ranks, 8 * third))
    return own


def reduce_head(blocks, zones, *results):
    sent = [block.astype(BF16) for block in blocks[1:]]
    if results:
        sent = lax.optimization_barrier((*sent, *results))[: zones - 1]
    total = blocks[0]
    for d in range(1, zones):
        total = total + widen(shift(sent[d - 1], "head", zones, d))
    return total


def local(
    zones,
    ranks,
    block_input,
    lengths,
    cotangent,
    norm1_gain,
    value_projection_weight,
    rand_logits,
    output_projection_weight,
    norm2_gain,
    up_projection_weight,
    up_bias,
    down_projection_weight,
    down_bias,
):
    seq_count, rows, depth = block_input.shape
    heads, full, _ = rand_logits.shape
    hidden = up_bias.shape[0]
    assert rows == SHORT and full == rows * zones and ranks % 8 == 0
    count = seq_count // 2
    assert seq_count == 2 * count
    place = jnp.stack([lax.axis_index("head"), lax.axis_index("dp")]).astype(jnp.int32)
    gain1, gain2 = norm1_gain[None], norm2_gain[None]
    width = value_projection_weight.shape[1]

    slot = width // ranks
    project = lax.dynamic_slice_in_dim(output_projection_weight, place[1] * slot, slot, 0)
    project = lax.all_gather(project, ("head", "dp"), axis=0, tiled=True)

    own = value_projection_weight.T
    half = width // 2
    parity = lax.rem(place[1], 2)
    part_rows = lax.dynamic_slice_in_dim(own, parity * half, half, 0)
    mine = [shift(part_rows, "head", zones, -d) for d in range(1, zones)]
    probs, probs_t, corner, corner_t = make_probs(rand_logits)
    others = flip(after(jnp.stack(mine), corner), "dp", ranks, 1)
    place = after(place, corner)

    def part(array, c):
        return array[c * count : (c + 1) * count]

    def call_values(place, c, weights):
        return make_values(place, part(block_input, c), gain1, weights, zones, heads, c == 0)

    def call_feed(place, c, pieces):
        return feed(
            place,
            pieces,
            part(block_input, c),
            part(cotangent, c),
            project,
            gain2,
            up_projection_weight,
            up_bias[None],
            down_projection_weight,
            down_bias[None],
            heads,
        )

    made = call_values(place, 0, [own, *mine, others])
    weight = made[zones]
    place = after(place, weight)
    values0 = exchange(made[:zones], zones, 1)
    made = call_values(place, 1, [weight])
    place = after(place, made[0])
    values1 = exchange(made, zones, 1, *values0)

    made = mix(place, part(lengths, 0), [values0], probs, corner, count, 1)
    place = after(place, made[0])
    mixed0 = exchange(made, zones, 1, *values1)
    made = mix(place, part(lengths, 1), [values1], probs, corner, count, 1)
    place = after(place, made[0])
    mixed1 = exchange(made, zones, 1, *mixed0)

    feed0 = call_feed(place, 0, mixed0)
    place = after(place, feed0[0])
    grads0 = exchange(feed0[:zones], zones, -1, *mixed1)
    feed1 = call_feed(place, 1, mixed1)
    place = after(place, feed1[0], *grads0)
    blocks, resids, acts, pres, norms, mixes, attends, up_sums, sums = zip(
        feed0[zones:], feed1[zones:]
    )
    cots = [part(cotangent, c).reshape(count * rows, depth) for c in range(2)]

    weight_sum, rand_sum = Reduce(ranks), Reduce(ranks)

    def call_weights(place, odd):
        return weight_grads(
            place, acts, pres, attends, norms, cots, mixes, odd, zones, ranks
        )

    grads1 = exchange(feed1[:zones], zones, -1, *grads0)
    sends = call_weights(place, 1)
    place = after(place, sends[0], *grads1)
    weight_sum.core([after(value, *grads1) for value in sends])
    made = mix(place, lengths, [grads0, grads1], probs_t, corner_t, count, -1)
    place = after(place, made[0])
    evens = exchange_some(made, range(2, zones, 2), zones, -1)
    keeps = call_weights(place, 0)
    place = after(place, keeps[0], *evens, *weight_sum.came)
    odds = exchange_some(made, range(1, zones, 2), zones, -1, *evens)
    backs = [made[0]] + [(odds if d % 2 else evens)[(d - 1) // 2] for d in range(1, zones)]
    weight_sum.first(keeps, *evens)
    rand = logit_grads(
        place, lengths, (grads0, grads1), (values0, values1), rand_logits, ranks, count
    )
    place = after(place, rand[0], *weight_sum.went, *odds)

    rand_sum.core([after(value, *weight_sum.went, *odds) for value in rand[:2]])
    weight_sum.second(rand[0], *odds)
    place = after(place, *rand_sum.came)

    up_total = (up_sums[0] + up_sums[1]).reshape(ranks * zones, -1)
    rest_total = sums[0] + sums[1]
    gain_total, bias_total = (
        rest_total[i].reshape(ranks * zones, -1) for i in range(2)
    )
    up_size, gain_size = hidden // ranks // zones, depth // ranks // zones
    extra = jnp.concatenate([jnp.zeros_like(gain_total), gain_total, bias_total, up_total], 1)
    extra = jnp.pad(extra, ((0, 0), (0, depth - extra.shape[1])))

    rand_sum.first(rand[2:], *backs)
    resid = jnp.concatenate(resids, 0)
    grad_x, value_send, value_keep = input_grads(
        place, backs, block_input, gain1, weight, resid, extra, heads, ranks
    )
    sides = weight_sum.finish()
    blocks_ff = [side[d] for side in sides for d in range(zones // 2)]
    ff = reduce_head(blocks_ff, zones)
    rand_sum.second(value_send)
    value_own = reduce_direct(value_send, value_keep, ranks, *rand_sum.went)
    value_total = reduce_head([value_own[d] for d in range(zones)], zones)
    grad_rand = jnp.concatenate(rand_sum.finish(), 1)

    tile, square = hidden // ranks // zones, depth // ranks
    group = group_rows(square, zones)
    line = value_total[group]
    return (
        jnp.concatenate(blocks, 0),
        grad_x,
        grad_rand,
        unpack(value_total[:group], square, zones),
        unpack(ff[2 * tile : 2 * tile + group], square, zones).T,
        line[:gain_size],
        line[gain_size : 2 * gain_size],
        ff[:tile].T,
        line[3 * gain_size : 3 * gain_size + up_size],
        ff[tile : 2 * tile],
        line[2 * gain_size : 3 * gain_size],
    )


def solution(mesh):
    in_specs = (
        P("dp", "head", None),
        P("dp"),
        P("dp", "head", None),
        P(),
        P(None, "head"),
        P("head", None, None),
        P("head", None),
        P(),
        P(),
        P(),
        P(),
        P(),
    )
    out_specs = (
        P("dp", "head", None),
        P("dp", "head", None),
        P("head", "dp", None),
        P("dp", "head"),
        P("head", "dp"),
        P(("dp", "head")),
        P(("dp", "head")),
        P(None, ("dp", "head")),
        P(("dp", "head")),
        P(("dp", "head"), None),
        P(("dp", "head")),
    )
    body = functools.partial(local, mesh.shape["head"], mesh.shape["dp"])
    return jax.shard_map(
        body, mesh=mesh, in_specs=in_specs, out_specs=out_specs, check_vma=False
    )
```

```python
import functools

import jax
import jax.numpy as jnp
from jax import lax
from jax.experimental import pallas as pl
from jax.experimental.pallas import tpu as pltpu
from jax.sharding import PartitionSpec as P

SHORT = 256
EPSILON = 1e-05
F32 = jnp.float32
BF16 = jnp.bfloat16
GELU_C = 0.7978845608028654
GELU_A = 0.044715
SHARE = 1.0


def dot_nn(a, b):
    return lax.dot_general(a, b, (((1,), (0,)), ((), ())), preferred_element_type=F32)


def dot_nt(a, b):
    return lax.dot_general(a, b, (((1,), (1,)), ((), ())), preferred_element_type=F32)


def dot_tn(a, b):
    return lax.dot_general(a, b, (((0,), (0,)), ((), ())), preferred_element_type=F32)


def norm_of(value):
    centered = value - jnp.mean(value, -1, keepdims=True)
    inverse = lax.rsqrt(jnp.mean(centered * centered, -1, keepdims=True) + EPSILON)
    return centered * inverse, inverse


def norm_back(scaled, hat, inverse):
    return inverse * (
        scaled
        - jnp.mean(scaled, -1, keepdims=True)
        - hat * jnp.mean(scaled * hat, -1, keepdims=True)
    )


def interleave(values, heads, size):
    parts = []
    for head in range(heads):
        for value in values:
            parts.append(value[:, head * size : (head + 1) * size])
    return jnp.concatenate(parts, axis=1)


def separate(piece, seq, count, heads, size):
    parts = []
    for head in range(heads):
        at = (head * count + seq) * size
        parts.append(piece[:, at : at + size])
    return jnp.concatenate(parts, axis=1)


def far(shape, dtype):
    return pltpu.HBM(shape, dtype)


def kept(value):
    return pltpu.with_memory_space_constraint(value, pltpu.HBM)


def whole(shape):
    return pl.BlockSpec(
        shape, lambda *_: (0,) * len(shape), pipeline_mode=pl.Buffered(buffer_count=1)
    )


def resident():
    return pl.BlockSpec(memory_space=pltpu.VMEM)


def cost(flops, moved, special=0):
    return pl.CostEstimate(
        flops=int(flops * SHARE), bytes_accessed=int(moved * SHARE), transcendentals=0
    )


def params(megabytes, grid_dims=1):
    return pltpu.CompilerParams(
        dimension_semantics=("arbitrary",) * grid_dims, vmem_limit_bytes=megabytes << 20
    )


def probs_kernel(logit_ref, long_ref, long_t_ref, short_ref, short_t_ref):
    logits = logit_ref[0].astype(F32)
    raised = jnp.exp(logits - jnp.max(logits, -1, keepdims=True))
    probs = raised / jnp.sum(raised, -1, keepdims=True)
    long_ref[0] = probs.astype(BF16)
    long_t_ref[0] = probs.T.astype(BF16)

    @pl.when(pl.program_id(1) == 0)
    def _():
        corner = logits[:, :SHORT]
        lifted = jnp.exp(corner - jnp.max(corner, -1, keepdims=True))
        part = lifted / jnp.sum(lifted, -1, keepdims=True)
        short_ref[0] = part.astype(BF16)
        short_t_ref[0] = part.T.astype(BF16)


def make_probs(logits):
    heads, rows, _ = logits.shape
    return pl.pallas_call(
        probs_kernel,
        grid=(heads, rows // SHORT),
        in_specs=[pl.BlockSpec((1, SHORT, rows), lambda h, i: (h, i, 0))],
        out_specs=[
            pl.BlockSpec((1, SHORT, rows), lambda h, i: (h, i, 0)),
            pl.BlockSpec((1, rows, SHORT), lambda h, i: (h, 0, i)),
            pl.BlockSpec((1, SHORT, SHORT), lambda h, i: (h, 0, 0)),
            pl.BlockSpec((1, SHORT, SHORT), lambda h, i: (h, 0, 0)),
        ],
        out_shape=[
            far((heads, rows, rows), BF16),
            far((heads, rows, rows), BF16),
            jax.ShapeDtypeStruct((heads, SHORT, SHORT), BF16),
            jax.ShapeDtypeStruct((heads, SHORT, SHORT), BF16),
        ],
        compiler_params=params(20, 2),
        cost_estimate=cost(10 * logits.size, 6 * logits.size, logits.size),
        name="probs",
    )(kept(logits))


def values_kernel(zones, heads, size, first, place_ref, x_ref, gain_ref, *rest):
    width = heads * size
    if first:
        own_ref, others_ref = rest[0], rest[zones]
        mine = rest[1:zones]
        outs, weight_ref = rest[zones + 1 : 2 * zones + 1], rest[2 * zones + 1]
        half = width // 2
        parity = lax.rem(place_ref[1], 2)
        weight_ref[:width, :] = own_ref[...]
        for d in range(1, zones):
            at = pl.multiple_of(d * width + parity * half, 16)
            weight_ref[pl.ds(at, half), :] = mine[d - 1][...]
            at = pl.multiple_of(d * width + (1 - parity) * half, 16)
            weight_ref[pl.ds(at, half), :] = others_ref[d - 1]
    else:
        weight_ref, outs = rest[0], rest[1:]
    made = []
    for seq in range(x_ref.shape[0]):
        hat, _ = norm_of(x_ref[seq].astype(F32))
        norm = (hat * gain_ref[...]).astype(BF16)
        made.append(dot_nt(norm, weight_ref[...]))
    for d in range(zones):
        own = [value[:, d * width : (d + 1) * width] for value in made]
        outs[d][...] = interleave(own, heads, size).astype(BF16)


def make_values(place, x, gain, weights, zones, heads, first):
    count, rows, depth = x.shape
    wide = count * depth // zones
    operands = [x, gain, *weights]
    shapes = [jax.ShapeDtypeStruct((rows, wide), BF16)] * zones
    if first:
        shapes.append(jax.ShapeDtypeStruct((depth, depth), BF16))
    return pl.pallas_call(
        functools.partial(values_kernel, zones, heads, depth // zones // heads, first),
        grid_spec=pltpu.PrefetchScalarGridSpec(
            num_scalar_prefetch=1,
            grid=(1,),
            in_specs=[whole(operand.shape) for operand in operands],
            out_specs=[whole(shape.shape) for shape in shapes],
        ),
        out_shape=shapes,
        compiler_params=params(12),
        cost_estimate=cost(
            2 * count * rows * depth * depth, 2 * x.size * 2 + 4 * depth * depth
        ),
        name="values",
    )(place, *operands)


def mix_kernel(zones, chunks, count, size, rows, sign, place_ref, long_flags, *refs):
    pieces = refs[: chunks * zones]
    matrix_ref, corner_ref = refs[chunks * zones : chunks * zones + 2]
    outs, held = refs[chunks * zones + 2 : -1], refs[-1]
    place = place_ref[0]
    wide = count * size
    for c in range(chunks):
        for d in range(zones):
            source = lax.rem(place + zones - sign * d, zones)
            at = pl.ds(pl.multiple_of(source * rows, rows), rows)
            held[at, c * wide : (c + 1) * wide] = pieces[c * zones + d][...]
    lane = lax.broadcasted_iota(jnp.int32, (1, chunks * wide), 1)
    is_long = jnp.zeros((1, chunks * wide), jnp.bool_)
    for seq in range(chunks * count):
        inside = (lane >= seq * size) & (lane < (seq + 1) * size)
        is_long = is_long | (inside & (long_flags[seq] > SHORT))
    corner = dot_nn(corner_ref[0], held[:SHORT, :])
    for d in range(zones):
        target = lax.rem(place + zones + sign * d, zones)
        part = matrix_ref[0, pl.ds(pl.multiple_of(target * rows, rows), rows), :]
        full = dot_nn(part, held[...])
        small = jnp.where(target == 0, corner, jnp.zeros_like(corner))
        outs[d][...] = jnp.where(is_long, full, small).astype(BF16)


def mix(place, lengths, groups, matrix, corner, count, sign):
    chunks, zones = len(groups), len(groups[0])
    heads, full, _ = matrix.shape
    rows, wide = groups[0][0].shape
    lanes = wide // heads
    spec = pl.BlockSpec((rows, lanes), lambda h, *_: (0, h))
    out_spec = pl.BlockSpec((rows, chunks * lanes), lambda h, *_: (0, h))
    return pl.pallas_call(
        functools.partial(mix_kernel, zones, chunks, count, lanes // count, rows, sign),
        grid_spec=pltpu.PrefetchScalarGridSpec(
            num_scalar_prefetch=2,
            grid=(heads,),
            in_specs=[spec] * (chunks * zones)
            + [
                pl.BlockSpec((1, full, full), lambda h, *_: (h, 0, 0)),
                pl.BlockSpec((1, SHORT, SHORT), lambda h, *_: (h, 0, 0)),
            ],
            out_specs=[out_spec] * zones,
            scratch_shapes=[pltpu.VMEM((full, chunks * lanes), BF16)],
        ),
        out_shape=[jax.ShapeDtypeStruct((rows, chunks * wide), BF16)] * zones,
        compiler_params=params(16),
        cost_estimate=cost(
            2 * heads * full * full * lanes * chunks,
            2 * heads * full * full + 4 * full * wide * chunks,
        ),
        name="mix",
    )(place, lengths, *(piece for group in groups for piece in group), kept(matrix), corner)


def feed_kernel(zones, heads, size, steps, earlier, place_ref, *refs):
    pieces = refs[:zones]
    (x_ref, cot_ref, project_ref, gain_ref, up_ref, up_bias_ref, down_ref, down_bias_ref) = refs[
        zones : zones + 8
    ]
    outs = refs[zones + 8 + earlier :]
    grads = outs[:zones]
    (
        block_ref,
        act_t_ref,
        pre_t_ref,
        norm_out_ref,
        attended_ref,
        up_sum_ref,
        sums_ref,
        norm_ref,
        weight_ref,
        resid_ref,
        hat_ref,
        inv_ref,
        forward_ref,
        back_ref,
    ) = outs[zones:]
    count, rows, depth = x_ref.shape
    width = heads * size
    step = pl.program_id(0)

    @pl.when(step == 0)
    def _():
        for d in range(zones):
            other = lax.rem(place_ref[0] + zones - d, zones)
            at = pl.multiple_of(other * width, 16)
            weight_ref[d * width : (d + 1) * width, :] = project_ref[pl.ds(at, width), :]
        for seq in range(count):
            at = slice(seq * rows, (seq + 1) * rows)
            mixed = jnp.concatenate(
                [separate(piece[...], seq, count, heads, size) for piece in pieces], axis=1
            )
            resid = x_ref[seq].astype(F32) + dot_nn(mixed, weight_ref[...])
            hat, inverse = norm_of(resid)
            resid_ref[at, :] = resid + down_bias_ref[...]
            hat_ref[at, :] = hat
            inv_ref[at, :] = inverse
            norm_ref[at, :] = (hat * gain_ref[...]).astype(BF16)
        forward_ref[...] = jnp.zeros_like(forward_ref)
        back_ref[...] = jnp.zeros_like(back_ref)

    up_sum = jnp.zeros((1, up_ref.shape[1]), F32)
    for seq in range(count):
        at = slice(seq * rows, (seq + 1) * rows)
        pre = dot_nn(norm_ref[at, :], up_ref[...]) + up_bias_ref[...]
        grad_act = dot_nt(cot_ref[seq], down_ref[...])
        square = pre * pre
        bent = jnp.tanh(pre * (GELU_C + (GELU_C * GELU_A) * square))
        half = 0.5 + 0.5 * bent
        act = (pre * half).astype(BF16)
        slope = half + (0.5 * pre) * (1.0 - bent * bent) * (
            GELU_C + (3.0 * GELU_C * GELU_A) * square
        )
        grad_pre = (grad_act * slope).astype(BF16)
        up_sum = up_sum + jnp.sum(grad_pre.astype(F32), 0, keepdims=True)
        act_t_ref[:, at] = act.T
        pre_t_ref[:, at] = grad_pre.T
        forward = dot_nn(act, down_ref[...])
        back = dot_nt(grad_pre, up_ref[...])

        forward_ref[at, :] += forward
        back_ref[at, :] += back

    up_sum_ref[...] = up_sum
    share = norm_out_ref.shape[1]
    norm_out_ref[...] = norm_ref[:, pl.ds(pl.multiple_of(step * share, share), share)]

    @pl.when(step == steps - 1)
    def _():
        gain_sum = jnp.zeros((1, depth), F32)
        bias_sum = jnp.zeros((1, depth), F32)
        made = []
        for seq in range(count):
            at = slice(seq * rows, (seq + 1) * rows)
            block_ref[seq] = (resid_ref[at, :] + forward_ref[at, :]).astype(BF16)
            cot = cot_ref[seq].astype(F32)
            hat = hat_ref[at, :]
            back = back_ref[at, :]
            gain_sum = gain_sum + jnp.sum(back * hat, 0, keepdims=True)
            bias_sum = bias_sum + jnp.sum(cot, 0, keepdims=True)
            grad = cot + norm_back(back * gain_ref[...], hat, inv_ref[at, :])
            low = grad.astype(BF16)
            attended_ref[:, at] = low.T
            made.append(dot_nt(low, weight_ref[...]))
        sums_ref[0:1, :] = gain_sum
        sums_ref[1:2, :] = bias_sum
        for d in range(zones):
            mine = [value[:, d * width : (d + 1) * width] for value in made]
            grads[d][...] = interleave(mine, heads, size).astype(BF16)


def feed(place, pieces, x, cot, project, gain, up, up_bias, down, down_bias, heads, c, blocks):
    zones = len(pieces)
    count, rows, depth = x.shape
    size = depth // zones // heads
    hidden = up.shape[1]
    tile = min(512, hidden)
    steps = hidden // tile
    tokens = count * rows
    wide = pieces[0].shape[1]
    earlier = [] if blocks is None else [blocks]
    shapes = [jax.ShapeDtypeStruct((rows, wide), BF16)] * zones + [
        far((2 * count, rows, depth), BF16),
        far((hidden, tokens), BF16),
        far((hidden, tokens), BF16),
        far((tokens, depth), BF16),
        far((depth, tokens), BF16),
        jax.ShapeDtypeStruct((1, hidden), F32),
        jax.ShapeDtypeStruct((2, depth), F32),
    ]
    return pl.pallas_call(
        functools.partial(feed_kernel, zones, heads, size, steps, len(earlier)),
        grid_spec=pltpu.PrefetchScalarGridSpec(
            num_scalar_prefetch=1,
            grid=(steps,),
            in_specs=[whole((rows, wide))] * zones
            + [
                whole(x.shape),
                whole(cot.shape),
                whole(project.shape),
                whole(gain.shape),
                pl.BlockSpec((depth, tile), lambda f, *_: (0, f)),
                pl.BlockSpec((1, tile), lambda f, *_: (0, f)),
                pl.BlockSpec((tile, depth), lambda f, *_: (f, 0)),
                whole(down_bias.shape),
            ]
            + [pl.BlockSpec(memory_space=pltpu.HBM)] * len(earlier),
            out_specs=[whole((rows, wide))] * zones
            + [
                pl.BlockSpec(
                    (count, rows, depth),
                    lambda *_: (c, 0, 0),
                    pipeline_mode=pl.Buffered(buffer_count=1),
                ),
                pl.BlockSpec((tile, tokens), lambda f, *_: (f, 0)),
                pl.BlockSpec((tile, tokens), lambda f, *_: (f, 0)),
                pl.BlockSpec((tokens, depth // steps), lambda f, *_: (0, f)),
                whole((depth, tokens)),
                pl.BlockSpec((1, tile), lambda f, *_: (0, f)),
                whole((2, depth)),
            ],
            scratch_shapes=[
                pltpu.VMEM((tokens, depth), BF16),
                pltpu.VMEM((depth, depth), BF16),
                pltpu.VMEM((tokens, depth), F32),
                pltpu.VMEM((tokens, depth), F32),
                pltpu.VMEM((tokens, 1), F32),
                pltpu.VMEM((tokens, depth), F32),
                pltpu.VMEM((tokens, depth), F32),
            ],
        ),
        out_shape=shapes,
        compiler_params=params(28),
        cost_estimate=cost(
            8 * tokens * depth * hidden + 4 * tokens * depth * depth,
            4 * depth * hidden + 4 * tokens * hidden + 20 * tokens * depth,
            tokens * hidden,
        ),
        input_output_aliases={zones + 9: zones} if earlier else {},
        name="feed",
    )(
        place,
        *map(kept, pieces),
        kept(x),
        kept(cot),
        kept(project),
        gain,
        kept(up),
        up_bias,
        kept(down),
        down_bias,
        *earlier,
    )


def relative_block(step, odd, ranks):
    rest = ranks // 8
    return odd + 2 * (step // rest) + 8 * lax.rem(step, rest)


def group_rows(rows, zones):
    return -(-rows // (8 * zones)) * 8


def pack(block, d, zones):
    rows, depth = block.shape
    width, group = depth // zones, group_rows(rows, zones)
    parts = []
    for k in range(zones):
        if k * group < rows:
            parts.append(block[k * group : (k + 1) * group, d * width : (d + 1) * width])
        else:
            parts.append(jnp.zeros((group, width), block.dtype))
    return jnp.concatenate(parts, axis=1)


def place_first(second):
    return second // 2 + 2 * (1 - lax.rem(second, 2))


def place_second(second):
    return lax.rem(second + 2, 4)


def weights_kernel(zones, chunks, heads, place_ref, *refs):
    acts, pres = refs[:chunks], refs[chunks : 2 * chunks]
    attends = refs[2 * chunks : 3 * chunks]
    norms, cots = refs[3 * chunks : 4 * chunks], refs[4 * chunks : 5 * chunks]
    pieces = refs[5 * chunks : (5 + zones) * chunks]
    first_ref, second_ref, scratch_ref, mixed_ref = refs[(5 + zones) * chunks :]
    mixes = [mixed_ref.at[c] for c in range(chunks)]
    rows, wide = pieces[0].shape
    count = norms[0].shape[0] // rows

    @pl.when(pl.program_id(0) == 0)
    def _():
        for c in range(chunks):
            group = pieces[c * zones : (c + 1) * zones]
            for seq in range(count):
                parts = [
                    separate(piece[...], seq, count, heads, wide // heads // count)
                    for piece in group
                ]
                mixed_ref[c, seq * rows : (seq + 1) * rows, :] = jnp.concatenate(parts, axis=1)
    part = scratch_ref.shape[1] // zones

    def total(lefts, rights):
        result = dot_nn(lefts[0][...], rights[0][...])
        for left, right in zip(lefts[1:], rights[1:]):
            result = result + dot_nn(left[...], right[...])
        return result

    scratch_ref[0] = total(pres, norms)
    scratch_ref[1] = total(acts, cots)
    square = total(attends, mixes)
    for d in range(zones):
        at = pl.ds(pl.multiple_of(lax.rem(place_ref[0] + d, zones) * part, 8), part)
        parts = [scratch_ref[0, at, :], scratch_ref[1, at, :], pack(square, -d % zones, zones)]
        used = sum(value.shape[0] for value in parts)
        parts.append(jnp.zeros((first_ref.shape[2] - used, first_ref.shape[3]), F32))
        side, number = (first_ref, d) if d < zones // 2 else (second_ref, d - zones // 2)
        side[0, number] = jnp.concatenate(parts, axis=0).astype(BF16)


def weight_grads(place, acts, pres, attends, norms, cots, pieces, heads, odd, zones, ranks):
    chunks = len(acts)
    hidden, tokens = acts[0].shape
    depth = norms[0].shape[1]
    tile, square = hidden // ranks, depth // ranks
    rows = 2 * tile // zones + group_rows(square, zones)
    rows = -(-rows // 16) * 16
    rest = ranks // 8

    def tall(step, place_ref):
        return (lax.bitwise_xor(place_ref[1], relative_block(step, odd, ranks)), 0)

    def first(step, _):
        return (place_first(step // rest) * rest + lax.rem(step, rest), 0, 0, 0)

    def second(step, _):
        return (place_second(step // rest) * rest + lax.rem(step, rest), 0, 0, 0)

    shape = (ranks // 2, zones // 2, rows, depth)
    return pl.pallas_call(
        functools.partial(weights_kernel, zones, chunks, heads),
        grid_spec=pltpu.PrefetchScalarGridSpec(
            num_scalar_prefetch=1,
            grid=(ranks // 2,),
            in_specs=[pl.BlockSpec((tile, tokens), tall)] * (2 * chunks)
            + [pl.BlockSpec((square, tokens), tall)] * chunks
            + [whole((tokens, depth))] * (2 * chunks)
            + [whole(pieces[0][0].shape)] * (zones * chunks),
            out_specs=[pl.BlockSpec((1, *shape[1:]), first), pl.BlockSpec((1, *shape[1:]), second)],
            scratch_shapes=[
                pltpu.VMEM((2, tile, depth), F32),
                pltpu.VMEM((chunks, tokens, depth), BF16),
            ],
        ),
        out_shape=[far(shape, BF16)] * 2,
        compiler_params=params(24),
        cost_estimate=cost(
            2 * chunks * hidden * tokens * depth,
            2 * chunks * hidden * tokens + 2 * hidden * depth + 4 * chunks * tokens * depth,
        ),
        name="weights",
    )(
        place,
        *map(kept, acts),
        *map(kept, pres),
        *map(kept, attends),
        *map(kept, norms),
        *map(kept, cots),
        *(kept(piece) for group in pieces for piece in group),
    )


def store_square(place_ref, outs, scratch_ref, extra_ref, zones, ranks):
    depth = scratch_ref.shape[0]
    part = depth // ranks
    for odd, out_ref in zip((1, 0), outs):
        for step in range(ranks // 2):
            rest = ranks // 8
            relative = odd + 2 * (step // rest) + 8 * (step % rest)
            rank = lax.bitwise_xor(place_ref[1], relative)
            block = scratch_ref[pl.ds(pl.multiple_of(rank * part, 8), part), :]
            for d in range(zones):
                zone = lax.rem(place_ref[0] + d, zones)
                line = extra_ref[pl.ds(rank * zones + zone, 1), :]
                packed = pack(block, d, zones)
                below = jnp.broadcast_to(line, (out_ref.shape[2] - packed.shape[0], depth))
                out_ref[step, d] = jnp.concatenate([packed, below], axis=0).astype(BF16)


def logits_kernel(
    zones, chunks, count, heads, size, rows, ranks, place_ref, lengths_ref, *refs
):
    grads = refs[: chunks * zones]
    values = refs[chunks * zones : 2 * chunks * zones]
    refs = refs[2 * chunks * zones :]
    logit_ref, sends, keeps = refs[0], refs[1:3], refs[3:5]
    long_ref, short_ref, value_ref, out_ref = refs[5:]
    place = place_ref[0]
    lanes = count * size
    step = pl.program_id(0)

    @pl.when(step == 0)
    def _():
        lane = lax.broadcasted_iota(jnp.int32, (1, lanes), 1)
        for c in range(chunks):
            is_long = jnp.zeros((1, lanes), jnp.bool_)
            for seq in range(count):
                inside = (lane >= seq * size) & (lane < (seq + 1) * size)
                is_long = is_long | (inside & (lengths_ref[c * count + seq] > SHORT))
            for d in range(zones):
                ahead = lax.rem(place + d, zones)
                behind = lax.rem(place + zones - d, zones)
                to = pl.ds(pl.multiple_of(ahead * rows, rows), rows)
                back = pl.ds(pl.multiple_of(behind * rows, rows), rows)
                for head in range(heads):
                    columns = slice(head * lanes, (head + 1) * lanes)
                    own = slice(c * lanes, (c + 1) * lanes)
                    grad = grads[c * zones + d][:, columns].astype(F32)
                    long_ref[head, to, own] = jnp.where(is_long, grad, 0.0).astype(BF16)
                    value_ref[head, back, own] = values[c * zones + d][:, columns]

                    @pl.when(ahead == 0)
                    def _():
                        short_ref[head, :, own] = jnp.where(is_long, 0.0, grad).astype(BF16)

    odd = jnp.where(step < ranks // 2, 1, 0)
    rank = lax.bitwise_xor(
        place_ref[1], relative_block(lax.rem(step, ranks // 2), odd, ranks)
    )
    part = logit_ref.shape[1]
    middle = part // 2
    start = rank * part
    for head in range(heads):
        logits = logit_ref[head].astype(F32)
        raised = jnp.exp(logits - jnp.max(logits, -1, keepdims=True))
        probs = raised / jnp.sum(raised, -1, keepdims=True)
        at = pl.ds(pl.multiple_of(start, part), part)
        total = dot_nt(long_ref[head, at, :], value_ref[head])
        out_ref[head] = probs * (total - jnp.sum(total * probs, -1, keepdims=True))

        @pl.when(start < SHORT)
        def _():
            corner = logits[:, :SHORT]
            lifted = jnp.exp(corner - jnp.max(corner, -1, keepdims=True))
            small = lifted / jnp.sum(lifted, -1, keepdims=True)
            sums = dot_nt(short_ref[head, at, :], value_ref[head, :SHORT, :])
            more = small * (sums - jnp.sum(sums * small, -1, keepdims=True))
            out_ref[head, :, :SHORT] += more

    @pl.when(step < ranks // 2)
    def _():
        sends[0][0] = out_ref[:, :middle, :].astype(BF16)
        sends[1][0] = out_ref[:, middle:, :].astype(BF16)

    @pl.when(step >= ranks // 2)
    def _():
        keeps[0][0] = out_ref[:, :middle, :].astype(BF16)
        keeps[1][0] = out_ref[:, middle:, :].astype(BF16)


def logit_grads(place, lengths, grads, values, logits, ranks, count):
    chunks, zones = len(grads), len(grads[0])
    heads, full, _ = logits.shape
    rows, wide = grads[0][0].shape
    size = wide // heads // count
    part = full // ranks
    half, rest = ranks // 2, ranks // 8

    def pick(step, place_ref, _):
        odd = jnp.where(step < half, 1, 0)
        block = relative_block(lax.rem(step, half), odd, ranks)
        return (0, lax.bitwise_xor(place_ref[1], block), 0)

    def spec(order, keep):
        def number(step, *_):
            at = jnp.maximum(step - half, 0) if keep else jnp.minimum(step, half - 1)
            return (order(at // rest) * rest + lax.rem(at, rest), 0, 0, 0)

        return pl.BlockSpec((1, heads, part // 2, full), number)

    flat = [piece for group in grads for piece in group] + [
        piece for group in values for piece in group
    ]
    every = chunks * count * size
    shape = (half, heads, part // 2, full)
    return pl.pallas_call(
        functools.partial(logits_kernel, zones, chunks, count, heads, size, rows, ranks),
        grid_spec=pltpu.PrefetchScalarGridSpec(
            num_scalar_prefetch=2,
            grid=(ranks,),
            in_specs=[whole((rows, wide))] * len(flat)
            + [pl.BlockSpec((heads, part, full), pick)],
            out_specs=[
                spec(order, keep) for keep in (False, True) for order in (place_first, place_second)
            ],
            scratch_shapes=[
                pltpu.VMEM((heads, full, every), BF16),
                pltpu.VMEM((heads, SHORT, every), BF16),
                pltpu.VMEM((heads, full, every), BF16),
                pltpu.VMEM((heads, part, full), F32),
            ],
        ),
        out_shape=[far(shape, BF16)] * 4,
        compiler_params=params(24),
        cost_estimate=cost(
            2 * heads * full * full * every, 4 * heads * full * full, heads * full * full
        ),
        name="logits",
    )(place, lengths, *map(kept, flat), kept(logits))


def input_kernel(zones, heads, size, ranks, count, place_ref, *refs):
    pieces = refs[:zones]
    x_ref, gain_ref, weight_ref, extra_in_ref = refs[zones : zones + 4]
    resids = refs[zones + 4 : zones + 6]
    grad_ref, send_ref, keep_ref, total_ref, gain_sum_ref, extra_ref = refs[zones + 6 :]
    depth = x_ref.shape[2]
    seq = pl.program_id(0)

    @pl.when(seq == 0)
    def _():
        total_ref[...] = jnp.zeros_like(total_ref)
        gain_sum_ref[...] = jnp.zeros_like(gain_sum_ref)

    hat, inverse = norm_of(x_ref[0].astype(F32))
    norm = (hat * gain_ref[...]).astype(BF16)
    pair = 128 // size
    parts = []
    lane = lax.broadcasted_iota(jnp.int32, (1, 128), 1)
    for piece in pieces:
        for head in range(heads):
            at = pl.multiple_of((head * count + seq // pair * pair) * size, 128)
            both = piece[:, pl.ds(at, 128)].astype(F32)
            moved = pltpu.roll(both, shift=size, axis=1)
            parts.append(jnp.where(lax.rem(seq, pair) == 0, both, moved)[:, :size])
    back = jnp.concatenate(parts, axis=1).astype(BF16)
    grad_norm = dot_nn(back, weight_ref[...])
    gain_sum_ref[...] += jnp.sum(grad_norm * hat, 0, keepdims=True)
    resid = jnp.where(seq < count // 2, resids[0][...], resids[1][...]).astype(F32).T
    grad = resid + norm_back(grad_norm * gain_ref[...], hat, inverse)
    grad_ref[0] = grad.astype(BF16)
    total_ref[...] += dot_tn(norm, back)

    @pl.when(seq == count - 1)
    def _():
        extra_ref[...] = extra_in_ref[...]
        share = depth // ranks // zones
        for index in range(ranks * zones):
            extra_ref[index : index + 1, :share] = gain_sum_ref[
                :, index * share : (index + 1) * share
            ]
        store_square(place_ref, (send_ref, keep_ref), total_ref, extra_ref, zones, ranks)


def input_grads(place, pieces, x, gain, weight, resids, extra, heads, ranks):
    zones = len(pieces)
    count, rows, depth = x.shape
    size = depth // zones // heads
    assert 2 * size == 128 and count % 2 == 0
    height = -(-(group_rows(depth // ranks, zones) + 1) // 16) * 16
    shape = (ranks // 2, zones, height, depth)
    return pl.pallas_call(
        functools.partial(input_kernel, zones, heads, size, ranks, count),
        grid_spec=pltpu.PrefetchScalarGridSpec(
            num_scalar_prefetch=1,
            grid=(count,),
            in_specs=[whole(pieces[0].shape)] * zones
            + [
                pl.BlockSpec((1, rows, depth), lambda s, *_: (s, 0, 0)),
                whole(gain.shape),
                whole(weight.shape),
                whole(extra.shape),
                pl.BlockSpec((depth, rows), lambda s, *_: (0, jnp.minimum(s, count // 2 - 1))),
                pl.BlockSpec((depth, rows), lambda s, *_: (0, jnp.maximum(s - count // 2, 0))),
            ],
            out_specs=[
                pl.BlockSpec((1, rows, depth), lambda s, *_: (s, 0, 0)),
                whole(shape),
                whole(shape),
            ],
            scratch_shapes=[
                pltpu.VMEM((depth, depth), F32),
                pltpu.VMEM((1, depth), F32),
                pltpu.VMEM(extra.shape, F32),
            ],
        ),
        out_shape=[
            far(x.shape, BF16),
            jax.ShapeDtypeStruct(shape, BF16),
            jax.ShapeDtypeStruct(shape, BF16),
        ],
        compiler_params=params(24),
        cost_estimate=cost(
            4 * count * rows * depth * depth, 12 * count * rows * depth + 8 * depth * depth
        ),
        name="input",
    )(place, *map(kept, pieces), kept(x), gain, kept(weight), extra, *map(kept, resids))


def total_of(terms):
    total = terms[0][...]
    for term in terms[1:]:
        total = total + term[...].astype(F32)
    return total


def unpack(packed, rows, zones):
    width = packed.shape[1] // zones
    parts = [packed[:, k * width : (k + 1) * width] for k in range(zones)]
    return jnp.concatenate(parts, axis=0)[:rows]


def feed_sums_kernel(zones, tile, square, *refs):
    up_ref, down_ref, square_ref = refs[zones:]
    total = total_of(refs[:zones])
    up_ref[...] = total[:tile].T
    down_ref[...] = total[tile : 2 * tile]
    packed = total[2 * tile : 2 * tile + group_rows(square, zones)]
    square_ref[...] = unpack(packed, square, zones).T


def feed_sums(terms, tile, square, zones):
    depth = terms[0].shape[1]
    return pl.pallas_call(
        functools.partial(feed_sums_kernel, zones, tile, square),
        grid=(1,),
        in_specs=[whole(term.shape) for term in terms],
        out_specs=[whole((depth, tile)), whole((tile, depth)), whole((depth // zones, square))],
        out_shape=[
            far((depth, tile), F32),
            far((tile, depth), F32),
            far((depth // zones, square), F32),
        ],
        compiler_params=params(12),
        name="feed_sums",
    )(*map(kept, terms))


def value_sums_kernel(zones, square, *refs):
    square_ref, line_ref = refs[zones:]
    total = total_of(refs[:zones])
    group = group_rows(square, zones)
    square_ref[...] = unpack(total[:group], square, zones)
    line_ref[...] = total[group : group + 1]


def value_sums(terms, square, zones):
    depth = terms[0].shape[1]
    return pl.pallas_call(
        functools.partial(value_sums_kernel, zones, square),
        grid=(1,),
        in_specs=[whole(term.shape) for term in terms],
        out_specs=[whole((square, depth // zones)), whole((1, depth))],
        out_shape=[far((square, depth // zones), F32), jax.ShapeDtypeStruct((1, depth), F32)],
        compiler_params=params(12),
        name="value_sums",
    )(*terms)


def shift(value, axis, extent, by):
    by = by % extent
    return lax.ppermute(value, axis, [(i, (i + by) % extent) for i in range(extent)])


def flip(value, axis, extent, mask):
    return lax.ppermute(value, axis, [(i, i ^ mask) for i in range(extent)])


def widen(value):
    return value.astype(F32)


def after(value, *results):
    return lax.optimization_barrier((value, *results))[0]


def exchange(pieces, extent, sign, *results):
    sent = pieces[1:]
    if results:
        sent = lax.optimization_barrier((*sent, *results))[: extent - 1]
    return [pieces[0]] + [
        shift(piece, "head", extent, sign * (d + 1)) for d, piece in enumerate(sent)
    ]


def exchange_some(pieces, numbers, extent, sign, *results):
    sent = [pieces[d] for d in numbers]
    if results:
        sent = lax.optimization_barrier((*sent, *results))[: len(sent)]
    return [shift(piece, "head", extent, sign * d) for d, piece in zip(numbers, sent)]


class Reduce:
    masks = ((2, 4), (4, 2))

    def __init__(self, ranks):
        self.ranks = ranks

    def core(self, sends):
        self.came = [flip(send, "dp", self.ranks, 1) for send in sends]

    def first(self, keeps, *results):
        half = self.ranks // 4
        sent = [
            (widen(keep[:half]) + widen(came[:half])).astype(BF16)
            for keep, came in zip(keeps, self.came)
        ]
        if results:
            sent = lax.optimization_barrier((*sent, *results))[:2]
        self.keeps, self.sent = keeps, sent
        self.went = [
            flip(value, "dp", self.ranks, masks[0]) for value, masks in zip(sent, self.masks)
        ]

    def rest(self, start, stop):
        half = self.ranks // 4
        return [
            widen(keep[half + start : half + stop])
            + widen(came[half + start : half + stop])
            + widen(went[start:stop])
            for keep, came, went in zip(self.keeps, self.came, self.went)
        ]

    def second(self, *results):
        sent = [value.astype(BF16) for value in self.rest(self.ranks // 8, self.ranks // 4)]
        if results:
            sent = lax.optimization_barrier((*sent, *results))[:2]
        self.last = [
            flip(value, "dp", self.ranks, masks[1]) for value, masks in zip(sent, self.masks)
        ]

    def finish(self, *results):
        lasts = self.last
        if results:
            lasts = lax.optimization_barrier((*lasts, *results))[:2]
        sides = []
        for own, last in zip(self.rest(0, self.ranks // 8), lasts):
            total = own + widen(last)
            side = total[0]
            for third in range(1, self.ranks // 8):
                side = side + widen(flip(total[third].astype(BF16), "dp", self.ranks, 8 * third))
            sides.append(side)
        return sides


def reduce_direct(send, keep, ranks, *results):
    rest = ranks // 8
    came = flip(after(send, *results), "dp", ranks, 1)
    both = [
        widen(keep[q * rest : (q + 1) * rest]) + widen(came[q * rest : (q + 1) * rest])
        for q in range(4)
    ]
    total = both[0]
    for q in range(1, 4):
        total = total + widen(flip(both[q].astype(BF16), "dp", ranks, 2 * q))
    own = total[0]
    for third in range(1, rest):
        own = own + widen(flip(total[third].astype(BF16), "dp", ranks, 8 * third))
    return own


def spread_head(blocks, zones):
    return [blocks[0]] + [
        shift(blocks[d].astype(BF16), "head", zones, d) for d in range(1, zones)
    ]


def local(
    zones,
    ranks,
    block_input,
    lengths,
    cotangent,
    norm1_gain,
    value_projection_weight,
    rand_logits,
    output_projection_weight,
    norm2_gain,
    up_projection_weight,
    up_bias,
    down_projection_weight,
    down_bias,
):
    seq_count, rows, depth = block_input.shape
    heads, full, _ = rand_logits.shape
    hidden = up_bias.shape[0]
    assert rows == SHORT and full == rows * zones and ranks % 8 == 0
    count = seq_count // 2
    assert seq_count == 2 * count
    place = jnp.stack([lax.axis_index("head"), lax.axis_index("dp")]).astype(jnp.int32)
    gain1, gain2 = norm1_gain[None], norm2_gain[None]
    width = value_projection_weight.shape[1]

    slot = width // ranks
    project = lax.dynamic_slice_in_dim(output_projection_weight, place[1] * slot, slot, 0)
    project = lax.all_gather(project, ("head", "dp"), axis=0, tiled=True)

    own = value_projection_weight.T
    half = width // 2
    parity = lax.rem(place[1], 2)
    part_rows = lax.dynamic_slice_in_dim(own, parity * half, half, 0)
    mine = [shift(part_rows, "head", zones, -d) for d in range(1, zones)]
    probs, probs_t, corner, corner_t = make_probs(rand_logits)
    others = flip(after(jnp.stack(mine), corner), "dp", ranks, 1)
    place = after(place, corner)

    def part(array, c):
        return array[c * count : (c + 1) * count]

    def call_values(place, c, weights):
        return make_values(place, part(block_input, c), gain1, weights, zones, heads, c == 0)

    def call_feed(place, c, pieces, blocks):
        return feed(
            place,
            pieces,
            part(block_input, c),
            part(cotangent, c),
            project,
            gain2,
            up_projection_weight,
            up_bias[None],
            down_projection_weight,
            down_bias[None],
            heads,
            c,
            blocks,
        )

    made = call_values(place, 0, [own, *mine, others])
    weight = made[zones]
    place = after(place, weight)
    values0 = exchange(made[:zones], zones, 1)
    made = call_values(place, 1, [weight])
    place = after(place, made[0])
    values1 = exchange(made, zones, 1, *values0)

    made = mix(place, part(lengths, 0), [values0], probs, corner, count, 1)
    place = after(place, made[0])
    mixed0 = exchange(made, zones, 1, *values1)
    made = mix(place, part(lengths, 1), [values1], probs, corner, count, 1)
    place = after(place, made[0])
    mixed1 = exchange(made, zones, 1, *mixed0)

    feed0 = call_feed(place, 0, mixed0, None)
    place = after(place, feed0[0])
    grads0 = exchange(feed0[:zones], zones, -1, *mixed1)
    feed1 = call_feed(place, 1, mixed1, feed0[zones])
    place = after(place, feed1[0], *grads0)
    acts, pres, norms, attends, up_sums, sums = zip(feed0[zones + 1 :], feed1[zones + 1 :])
    cots = [part(cotangent, c).reshape(count * rows, depth) for c in range(2)]

    weight_sum, rand_sum = Reduce(ranks), Reduce(ranks)

    def call_weights(place, odd):
        return weight_grads(
            place,
            acts,
            pres,
            attends,
            norms,
            cots,
            (mixed0, mixed1),
            heads,
            odd,
            zones,
            ranks,
        )

    grads1 = exchange(feed1[:zones], zones, -1, *grads0)
    sends = call_weights(place, 1)
    place = after(place, sends[0], *grads1)
    weight_sum.core([after(value, *grads1) for value in sends])
    made = mix(place, lengths, [grads0, grads1], probs_t, corner_t, count, -1)
    place = after(place, made[0])
    evens = exchange_some(made, range(2, zones, 2), zones, -1)
    keeps = call_weights(place, 0)
    place = after(place, keeps[0], *evens, *weight_sum.came)
    odds = exchange_some(made, range(1, zones, 2), zones, -1, *evens)
    backs = [made[0]] + [(odds if d % 2 else evens)[(d - 1) // 2] for d in range(1, zones)]
    weight_sum.first(keeps, *evens)
    rand = logit_grads(
        place, lengths, (grads0, grads1), (values0, values1), rand_logits, ranks, count
    )
    place = after(place, rand[0], *weight_sum.went, *odds)

    rand_sum.core([after(value, *weight_sum.went, *odds) for value in rand[:2]])
    weight_sum.second(rand[0], *odds)
    place = after(place, *rand_sum.came)

    up_total = (up_sums[0] + up_sums[1]).reshape(ranks * zones, -1)
    rest_total = sums[0] + sums[1]
    gain_total, bias_total = (
        rest_total[i].reshape(ranks * zones, -1) for i in range(2)
    )
    up_size, gain_size = hidden // ranks // zones, depth // ranks // zones
    extra = jnp.concatenate([jnp.zeros_like(gain_total), gain_total, bias_total, up_total], 1)
    extra = jnp.pad(extra, ((0, 0), (0, depth - extra.shape[1])))

    rand_sum.first(rand[2:], *backs)
    grad_x, value_send, value_keep = input_grads(
        place, backs, block_input, gain1, weight, attends, extra, heads, ranks
    )
    sides = weight_sum.finish(*rand_sum.sent)
    terms = [side[d] for side in sides for d in range(zones // 2)]
    far_apart = zones // 2
    for d in (far_apart, *(d for d in range(1, zones) if d != far_apart)):
        sent = terms[d].astype(BF16)
        if d != far_apart:
            sent = after(sent, terms[far_apart])
        terms[d] = shift(sent, "head", zones, d)
    rand_sum.second(value_send, terms[far_apart])
    value_own = reduce_direct(value_send, value_keep, ranks, *rand_sum.went)
    tile, square = hidden // ranks // zones, depth // ranks
    terms = lax.optimization_barrier((*terms, *rand_sum.last))[:zones]
    grad_up, grad_down, grad_out = feed_sums(terms, tile, square, zones)
    value_terms = spread_head([value_own[d] for d in range(zones)], zones)
    grad_value, line = value_sums(value_terms, square, zones)
    line = line[0]
    grad_rand = jnp.concatenate(rand_sum.finish(), 1)
    return (
        feed1[zones],
        grad_x,
        grad_rand,
        grad_value,
        grad_out,
        line[:gain_size],
        line[gain_size : 2 * gain_size],
        grad_up,
        line[3 * gain_size : 3 * gain_size + up_size],
        grad_down,
        line[2 * gain_size : 3 * gain_size],
    )


def solution(mesh):
    in_specs = (
        P("dp", "head", None),
        P("dp"),
        P("dp", "head", None),
        P(),
        P(None, "head"),
        P("head", None, None),
        P("head", None),
        P(),
        P(),
        P(),
        P(),
        P(),
    )
    out_specs = (
        P("dp", "head", None),
        P("dp", "head", None),
        P("head", "dp", None),
        P("dp", "head"),
        P("head", "dp"),
        P(("dp", "head")),
        P(("dp", "head")),
        P(None, ("dp", "head")),
        P(("dp", "head")),
        P(("dp", "head"), None),
        P(("dp", "head")),
    )
    body = functools.partial(local, mesh.shape["head"], mesh.shape["dp"])
    return jax.shard_map(
        body, mesh=mesh, in_specs=in_specs, out_specs=out_specs, check_vma=False
    )
```

```python
import functools

import jax
import jax.numpy as jnp
from jax import lax
from jax.experimental import pallas as pl
from jax.experimental.pallas import tpu as pltpu
from jax.sharding import PartitionSpec as P

SHORT = 256
EPSILON = 1e-05
F32 = jnp.float32
BF16 = jnp.bfloat16
GELU_C = 0.7978845608028654
GELU_A = 0.044715
SHARE = 1.0


def dot_nn(a, b):
    return lax.dot_general(a, b, (((1,), (0,)), ((), ())), preferred_element_type=F32)


def dot_nt(a, b):
    return lax.dot_general(a, b, (((1,), (1,)), ((), ())), preferred_element_type=F32)


def dot_tn(a, b):
    return lax.dot_general(a, b, (((0,), (0,)), ((), ())), preferred_element_type=F32)


def norm_of(value):
    centered = value - jnp.mean(value, -1, keepdims=True)
    inverse = lax.rsqrt(jnp.mean(centered * centered, -1, keepdims=True) + EPSILON)
    return centered * inverse, inverse


def norm_back(scaled, hat, inverse):
    return inverse * (
        scaled
        - jnp.mean(scaled, -1, keepdims=True)
        - hat * jnp.mean(scaled * hat, -1, keepdims=True)
    )


def interleave(values, heads, size):
    parts = []
    for head in range(heads):
        for value in values:
            parts.append(value[:, head * size : (head + 1) * size])
    return jnp.concatenate(parts, axis=1)


def separate(piece, seq, count, heads, size):
    parts = []
    for head in range(heads):
        at = (head * count + seq) * size
        parts.append(piece[:, at : at + size])
    return jnp.concatenate(parts, axis=1)


def far(shape, dtype):
    return pltpu.HBM(shape, dtype)


def kept(value):
    return pltpu.with_memory_space_constraint(value, pltpu.HBM)


def whole(shape):
    return pl.BlockSpec(
        shape, lambda *_: (0,) * len(shape), pipeline_mode=pl.Buffered(buffer_count=1)
    )


def resident():
    return pl.BlockSpec(memory_space=pltpu.VMEM)


def cost(flops, moved, special=0):
    return pl.CostEstimate(
        flops=int(flops * SHARE), bytes_accessed=int(moved * SHARE), transcendentals=0
    )


def params(megabytes, grid_dims=1):
    return pltpu.CompilerParams(
        dimension_semantics=("arbitrary",) * grid_dims, vmem_limit_bytes=megabytes << 20
    )


def probs_kernel(logit_ref, long_ref, long_t_ref, short_ref, short_t_ref):
    logits = logit_ref[0].astype(F32)
    raised = jnp.exp(logits - jnp.max(logits, -1, keepdims=True))
    probs = raised / jnp.sum(raised, -1, keepdims=True)
    long_ref[0] = probs.astype(BF16)
    long_t_ref[0] = probs.T.astype(BF16)

    @pl.when(pl.program_id(1) == 0)
    def _():
        corner = logits[:, :SHORT]
        lifted = jnp.exp(corner - jnp.max(corner, -1, keepdims=True))
        part = lifted / jnp.sum(lifted, -1, keepdims=True)
        short_ref[0] = part.astype(BF16)
        short_t_ref[0] = part.T.astype(BF16)


def make_probs(logits):
    heads, rows, _ = logits.shape
    return pl.pallas_call(
        probs_kernel,
        grid=(heads, rows // SHORT),
        in_specs=[pl.BlockSpec((1, SHORT, rows), lambda h, i: (h, i, 0))],
        out_specs=[
            pl.BlockSpec((1, SHORT, rows), lambda h, i: (h, i, 0)),
            pl.BlockSpec((1, rows, SHORT), lambda h, i: (h, 0, i)),
            pl.BlockSpec((1, SHORT, SHORT), lambda h, i: (h, 0, 0)),
            pl.BlockSpec((1, SHORT, SHORT), lambda h, i: (h, 0, 0)),
        ],
        out_shape=[
            far((heads, rows, rows), BF16),
            far((heads, rows, rows), BF16),
            jax.ShapeDtypeStruct((heads, SHORT, SHORT), BF16),
            jax.ShapeDtypeStruct((heads, SHORT, SHORT), BF16),
        ],
        compiler_params=params(20, 2),
        cost_estimate=cost(10 * logits.size, 6 * logits.size, logits.size),
        name="probs",
    )(kept(logits))


def values_kernel(zones, heads, size, first, place_ref, x_ref, gain_ref, *rest):
    width = heads * size
    if first:
        own_ref, others_ref = rest[0], rest[zones]
        mine = rest[1:zones]
        outs, weight_ref = rest[zones + 1 : 2 * zones + 1], rest[2 * zones + 1]
        half = width // 2
        parity = lax.rem(place_ref[1], 2)
        weight_ref[:width, :] = own_ref[...]
        for d in range(1, zones):
            at = pl.multiple_of(d * width + parity * half, 16)
            weight_ref[pl.ds(at, half), :] = mine[d - 1][...]
            at = pl.multiple_of(d * width + (1 - parity) * half, 16)
            weight_ref[pl.ds(at, half), :] = others_ref[d - 1]
    else:
        weight_ref, outs = rest[0], rest[1:]
    made = []
    for seq in range(x_ref.shape[0]):
        hat, _ = norm_of(x_ref[seq].astype(F32))
        norm = (hat * gain_ref[...]).astype(BF16)
        made.append(dot_nt(norm, weight_ref[...]))
    for d in range(zones):
        own = [value[:, d * width : (d + 1) * width] for value in made]
        outs[d][...] = interleave(own, heads, size).astype(BF16)


def make_values(place, x, gain, weights, zones, heads, first):
    count, rows, depth = x.shape
    wide = count * depth // zones
    operands = [x, gain, *weights]
    shapes = [jax.ShapeDtypeStruct((rows, wide), BF16)] * zones
    if first:
        shapes.append(jax.ShapeDtypeStruct((depth, depth), BF16))
    return pl.pallas_call(
        functools.partial(values_kernel, zones, heads, depth // zones // heads, first),
        grid_spec=pltpu.PrefetchScalarGridSpec(
            num_scalar_prefetch=1,
            grid=(1,),
            in_specs=[whole(operand.shape) for operand in operands],
            out_specs=[whole(shape.shape) for shape in shapes],
        ),
        out_shape=shapes,
        compiler_params=params(12),
        cost_estimate=cost(
            2 * count * rows * depth * depth, 2 * x.size * 2 + 4 * depth * depth
        ),
        name="values",
    )(place, *operands)


def mix_kernel(zones, chunks, count, size, rows, sign, place_ref, long_flags, *refs):
    pieces = refs[: chunks * zones]
    matrix_ref, corner_ref = refs[chunks * zones : chunks * zones + 2]
    outs, held = refs[chunks * zones + 2 : -1], refs[-1]
    place = place_ref[0]
    wide = count * size
    for c in range(chunks):
        for d in range(zones):
            source = lax.rem(place + zones - sign * d, zones)
            at = pl.ds(pl.multiple_of(source * rows, rows), rows)
            held[at, c * wide : (c + 1) * wide] = pieces[c * zones + d][...]
    lane = lax.broadcasted_iota(jnp.int32, (1, chunks * wide), 1)
    is_long = jnp.zeros((1, chunks * wide), jnp.bool_)
    for seq in range(chunks * count):
        inside = (lane >= seq * size) & (lane < (seq + 1) * size)
        is_long = is_long | (inside & (long_flags[seq] > SHORT))
    corner = dot_nn(corner_ref[0], held[:SHORT, :])
    for d in range(zones):
        target = lax.rem(place + zones + sign * d, zones)
        part = matrix_ref[0, pl.ds(pl.multiple_of(target * rows, rows), rows), :]
        full = dot_nn(part, held[...])
        small = jnp.where(target == 0, corner, jnp.zeros_like(corner))
        outs[d][...] = jnp.where(is_long, full, small).astype(BF16)


def mix(place, lengths, groups, matrix, corner, count, sign):
    chunks, zones = len(groups), len(groups[0])
    heads, full, _ = matrix.shape
    rows, wide = groups[0][0].shape
    lanes = wide // heads
    spec = pl.BlockSpec((rows, lanes), lambda h, *_: (0, h))
    out_spec = pl.BlockSpec((rows, chunks * lanes), lambda h, *_: (0, h))
    return pl.pallas_call(
        functools.partial(mix_kernel, zones, chunks, count, lanes // count, rows, sign),
        grid_spec=pltpu.PrefetchScalarGridSpec(
            num_scalar_prefetch=2,
            grid=(heads,),
            in_specs=[spec] * (chunks * zones)
            + [
                pl.BlockSpec((1, full, full), lambda h, *_: (h, 0, 0)),
                pl.BlockSpec((1, SHORT, SHORT), lambda h, *_: (h, 0, 0)),
            ],
            out_specs=[out_spec] * zones,
            scratch_shapes=[pltpu.VMEM((full, chunks * lanes), BF16)],
        ),
        out_shape=[jax.ShapeDtypeStruct((rows, chunks * wide), BF16)] * zones,
        compiler_params=params(16),
        cost_estimate=cost(
            2 * heads * full * full * lanes * chunks,
            2 * heads * full * full + 4 * full * wide * chunks,
        ),
        name="mix",
    )(place, lengths, *(piece for group in groups for piece in group), kept(matrix), corner)


def feed_kernel(zones, heads, size, steps, earlier, place_ref, *refs):
    pieces = refs[:zones]
    (x_ref, cot_ref, project_ref, gain_ref, up_ref, up_bias_ref, down_ref, down_bias_ref) = refs[
        zones : zones + 8
    ]
    outs = refs[zones + 8 + earlier :]
    grads = outs[:zones]
    (
        block_ref,
        act_t_ref,
        pre_t_ref,
        norm_out_ref,
        attended_ref,
        up_sum_ref,
        sums_ref,
        norm_ref,
        weight_ref,
        resid_ref,
        hat_ref,
        inv_ref,
        forward_ref,
        back_ref,
    ) = outs[zones:]
    count, rows, depth = x_ref.shape
    width = heads * size
    step = pl.program_id(0)

    @pl.when(step == 0)
    def _():
        for d in range(zones):
            other = lax.rem(place_ref[0] + zones - d, zones)
            at = pl.multiple_of(other * width, 16)
            weight_ref[d * width : (d + 1) * width, :] = project_ref[pl.ds(at, width), :]
        for seq in range(count):
            at = slice(seq * rows, (seq + 1) * rows)
            mixed = jnp.concatenate(
                [separate(piece[...], seq, count, heads, size) for piece in pieces], axis=1
            )
            resid = x_ref[seq].astype(F32) + dot_nn(mixed, weight_ref[...])
            hat, inverse = norm_of(resid)
            resid_ref[at, :] = resid + down_bias_ref[...]
            hat_ref[at, :] = hat
            inv_ref[at, :] = inverse
            norm_ref[at, :] = (hat * gain_ref[...]).astype(BF16)
        forward_ref[...] = jnp.zeros_like(forward_ref)
        back_ref[...] = jnp.zeros_like(back_ref)

    up_sum = jnp.zeros((1, up_ref.shape[1]), F32)
    for seq in range(count):
        at = slice(seq * rows, (seq + 1) * rows)
        pre = dot_nn(norm_ref[at, :], up_ref[...]) + up_bias_ref[...]
        grad_act = dot_nt(cot_ref[seq], down_ref[...])
        square = pre * pre
        bent = jnp.tanh(pre * (GELU_C + (GELU_C * GELU_A) * square))
        half = 0.5 + 0.5 * bent
        act = (pre * half).astype(BF16)
        slope = half + (0.5 * pre) * (1.0 - bent * bent) * (
            GELU_C + (3.0 * GELU_C * GELU_A) * square
        )
        grad_pre = (grad_act * slope).astype(BF16)
        up_sum = up_sum + jnp.sum(grad_pre.astype(F32), 0, keepdims=True)
        act_t_ref[:, at] = act.T
        pre_t_ref[:, at] = grad_pre.T
        forward = dot_nn(act, down_ref[...])
        back = dot_nt(grad_pre, up_ref[...])

        forward_ref[at, :] += forward
        back_ref[at, :] += back

    up_sum_ref[...] = up_sum
    share = norm_out_ref.shape[1]
    norm_out_ref[...] = norm_ref[:, pl.ds(pl.multiple_of(step * share, share), share)]

    @pl.when(step == steps - 1)
    def _():
        gain_sum = jnp.zeros((1, depth), F32)
        bias_sum = jnp.zeros((1, depth), F32)
        made = []
        for seq in range(count):
            at = slice(seq * rows, (seq + 1) * rows)
            block_ref[seq] = (resid_ref[at, :] + forward_ref[at, :]).astype(BF16)
            cot = cot_ref[seq].astype(F32)
            hat = hat_ref[at, :]
            back = back_ref[at, :]
            gain_sum = gain_sum + jnp.sum(back * hat, 0, keepdims=True)
            bias_sum = bias_sum + jnp.sum(cot, 0, keepdims=True)
            grad = cot + norm_back(back * gain_ref[...], hat, inv_ref[at, :])
            low = grad.astype(BF16)
            attended_ref[:, at] = low.T
            made.append(dot_nt(low, weight_ref[...]))
        sums_ref[0:1, :] = gain_sum
        sums_ref[1:2, :] = bias_sum
        for d in range(zones):
            mine = [value[:, d * width : (d + 1) * width] for value in made]
            grads[d][...] = interleave(mine, heads, size).astype(BF16)


def feed(place, pieces, x, cot, project, gain, up, up_bias, down, down_bias, heads, c, chunks, earlier):
    zones = len(pieces)
    count, rows, depth = x.shape
    size = depth // zones // heads
    hidden = up.shape[1]
    tile = min(512, hidden)
    steps = hidden // tile
    tokens = count * rows
    wide = pieces[0].shape[1]
    shapes = [jax.ShapeDtypeStruct((rows, wide), BF16)] * zones + [
        far((chunks * count, rows, depth), BF16),
        far((hidden, chunks * tokens), BF16),
        far((hidden, chunks * tokens), BF16),
        far((chunks * tokens, depth), BF16),
        far((depth, chunks * tokens), BF16),
        jax.ShapeDtypeStruct((1, hidden), F32),
        jax.ShapeDtypeStruct((2, depth), F32),
    ]
    return pl.pallas_call(
        functools.partial(feed_kernel, zones, heads, size, steps, len(earlier)),
        grid_spec=pltpu.PrefetchScalarGridSpec(
            num_scalar_prefetch=1,
            grid=(steps,),
            in_specs=[whole((rows, wide))] * zones
            + [
                whole(x.shape),
                whole(cot.shape),
                whole(project.shape),
                whole(gain.shape),
                pl.BlockSpec((depth, tile), lambda f, *_: (0, f)),
                pl.BlockSpec((1, tile), lambda f, *_: (0, f)),
                pl.BlockSpec((tile, depth), lambda f, *_: (f, 0)),
                whole(down_bias.shape),
            ]
            + [pl.BlockSpec(memory_space=pltpu.HBM)] * len(earlier),
            out_specs=[whole((rows, wide))] * zones
            + [
                pl.BlockSpec(
                    (count, rows, depth),
                    lambda *_: (c, 0, 0),
                    pipeline_mode=pl.Buffered(buffer_count=1),
                ),
                pl.BlockSpec((tile, tokens), lambda f, *_: (f, c)),
                pl.BlockSpec((tile, tokens), lambda f, *_: (f, c)),
                pl.BlockSpec((tokens, depth // steps), lambda f, *_: (c, f)),
                pl.BlockSpec(
                    (depth, tokens),
                    lambda *_: (0, c),
                    pipeline_mode=pl.Buffered(buffer_count=1),
                ),
                pl.BlockSpec((1, tile), lambda f, *_: (0, f)),
                whole((2, depth)),
            ],
            scratch_shapes=[
                pltpu.VMEM((tokens, depth), BF16),
                pltpu.VMEM((depth, depth), BF16),
                pltpu.VMEM((tokens, depth), F32),
                pltpu.VMEM((tokens, depth), F32),
                pltpu.VMEM((tokens, 1), F32),
                pltpu.VMEM((tokens, depth), F32),
                pltpu.VMEM((tokens, depth), F32),
            ],
        ),
        out_shape=shapes,
        compiler_params=params(28),
        cost_estimate=cost(
            8 * tokens * depth * hidden + 4 * tokens * depth * depth,
            4 * depth * hidden + 4 * tokens * hidden + 20 * tokens * depth,
            tokens * hidden,
        ),
        input_output_aliases={zones + 9 + i: zones + i for i in range(len(earlier))},
        name="feed",
    )(
        place,
        *map(kept, pieces),
        kept(x),
        kept(cot),
        kept(project),
        gain,
        kept(up),
        up_bias,
        kept(down),
        down_bias,
        *earlier,
    )


def relative_block(step, odd, ranks):
    rest = ranks // 8
    return odd + 2 * (step // rest) + 8 * lax.rem(step, rest)


def group_rows(rows, zones):
    return -(-rows // (8 * zones)) * 8


def pack(block, d, zones):
    rows, depth = block.shape
    width, group = depth // zones, group_rows(rows, zones)
    parts = []
    for k in range(zones):
        if k * group < rows:
            parts.append(block[k * group : (k + 1) * group, d * width : (d + 1) * width])
        else:
            parts.append(jnp.zeros((group, width), block.dtype))
    return jnp.concatenate(parts, axis=1)


def place_first(second):
    return second // 2 + 2 * (1 - lax.rem(second, 2))


def place_second(second):
    return lax.rem(second + 2, 4)


def weights_kernel(zones, chunks, heads, place_ref, *refs):
    act_ref, pre_ref, attended_ref, norm_ref, cot_ref = refs[:5]
    pieces = refs[5 : 5 + zones * chunks]
    first_ref, second_ref, scratch_ref, mixed_ref = refs[5 + zones * chunks :]
    part = scratch_ref.shape[1] // zones
    rows, wide = pieces[0].shape
    count = norm_ref.shape[0] // rows // chunks

    @pl.when(pl.program_id(0) == 0)
    def _():
        for c in range(chunks):
            group = pieces[c * zones : (c + 1) * zones]
            for seq in range(count):
                parts = [
                    separate(piece[...], seq, count, heads, wide // heads // count)
                    for piece in group
                ]
                at = (c * count + seq) * rows
                mixed_ref[at : at + rows, :] = jnp.concatenate(parts, axis=1)

    scratch_ref[0] = dot_nn(pre_ref[...], norm_ref[...])
    scratch_ref[1] = dot_nn(act_ref[...], cot_ref[...])
    square = dot_nn(attended_ref[...], mixed_ref[...])
    for d in range(zones):
        at = pl.ds(pl.multiple_of(lax.rem(place_ref[0] + d, zones) * part, 8), part)
        parts = [scratch_ref[0, at, :], scratch_ref[1, at, :], pack(square, -d % zones, zones)]
        used = sum(value.shape[0] for value in parts)
        parts.append(jnp.zeros((first_ref.shape[2] - used, first_ref.shape[3]), F32))
        side, number = (first_ref, d) if d < zones // 2 else (second_ref, d - zones // 2)
        side[0, number] = jnp.concatenate(parts, axis=0).astype(BF16)


def weight_grads(place, act, pre, attended, norm, cot, pieces, heads, odd, zones, ranks):
    chunks = len(pieces)
    hidden, tokens = act.shape
    depth = norm.shape[1]
    tile, square = hidden // ranks, depth // ranks
    rows = 2 * tile // zones + group_rows(square, zones)
    rows = -(-rows // 16) * 16
    rest = ranks // 8

    def tall(step, place_ref):
        return (lax.bitwise_xor(place_ref[1], relative_block(step, odd, ranks)), 0)

    def first(step, _):
        return (place_first(step // rest) * rest + lax.rem(step, rest), 0, 0, 0)

    def second(step, _):
        return (place_second(step // rest) * rest + lax.rem(step, rest), 0, 0, 0)

    shape = (ranks // 2, zones // 2, rows, depth)
    return pl.pallas_call(
        functools.partial(weights_kernel, zones, chunks, heads),
        grid_spec=pltpu.PrefetchScalarGridSpec(
            num_scalar_prefetch=1,
            grid=(ranks // 2,),
            in_specs=[pl.BlockSpec((tile, tokens), tall)] * 2
            + [pl.BlockSpec((square, tokens), tall)]
            + [whole((tokens, depth))] * 2
            + [whole(pieces[0][0].shape)] * (zones * chunks),
            out_specs=[pl.BlockSpec((1, *shape[1:]), first), pl.BlockSpec((1, *shape[1:]), second)],
            scratch_shapes=[
                pltpu.VMEM((2, tile, depth), F32),
                pltpu.VMEM((tokens, depth), BF16),
            ],
        ),
        out_shape=[far(shape, BF16)] * 2,
        compiler_params=params(24),
        cost_estimate=cost(
            2 * hidden * tokens * depth,
            2 * hidden * tokens + 2 * hidden * depth + 4 * tokens * depth,
        ),
        name="weights",
    )(
        place,
        *map(kept, (act, pre, attended, norm, cot)),
        *(kept(piece) for group in pieces for piece in group),
    )


def store_square(place_ref, outs, scratch_ref, extra_ref, zones, ranks):
    depth = scratch_ref.shape[0]
    part = depth // ranks
    for odd, out_ref in zip((1, 0), outs):
        for step in range(ranks // 2):
            rest = ranks // 8
            relative = odd + 2 * (step // rest) + 8 * (step % rest)
            rank = lax.bitwise_xor(place_ref[1], relative)
            block = scratch_ref[pl.ds(pl.multiple_of(rank * part, 8), part), :]
            for d in range(zones):
                zone = lax.rem(place_ref[0] + d, zones)
                line = extra_ref[pl.ds(rank * zones + zone, 1), :]
                packed = pack(block, d, zones)
                below = jnp.broadcast_to(line, (out_ref.shape[2] - packed.shape[0], depth))
                out_ref[step, d] = jnp.concatenate([packed, below], axis=0).astype(BF16)


def logits_kernel(
    zones, chunks, count, heads, size, rows, ranks, place_ref, lengths_ref, *refs
):
    grads = refs[: chunks * zones]
    values = refs[chunks * zones : 2 * chunks * zones]
    refs = refs[2 * chunks * zones :]
    logit_ref, sends, keeps = refs[0], refs[1:3], refs[3:5]
    long_ref, short_ref, value_ref, out_ref = refs[5:]
    place = place_ref[0]
    lanes = count * size
    step = pl.program_id(0)

    @pl.when(step == 0)
    def _():
        lane = lax.broadcasted_iota(jnp.int32, (1, lanes), 1)
        for c in range(chunks):
            is_long = jnp.zeros((1, lanes), jnp.bool_)
            for seq in range(count):
                inside = (lane >= seq * size) & (lane < (seq + 1) * size)
                is_long = is_long | (inside & (lengths_ref[c * count + seq] > SHORT))
            for d in range(zones):
                ahead = lax.rem(place + d, zones)
                behind = lax.rem(place + zones - d, zones)
                to = pl.ds(pl.multiple_of(ahead * rows, rows), rows)
                back = pl.ds(pl.multiple_of(behind * rows, rows), rows)
                for head in range(heads):
                    columns = slice(head * lanes, (head + 1) * lanes)
                    own = slice(c * lanes, (c + 1) * lanes)
                    grad = grads[c * zones + d][:, columns].astype(F32)
                    long_ref[head, to, own] = jnp.where(is_long, grad, 0.0).astype(BF16)
                    value_ref[head, back, own] = values[c * zones + d][:, columns]

                    @pl.when(ahead == 0)
                    def _():
                        short_ref[head, :, own] = jnp.where(is_long, 0.0, grad).astype(BF16)

    odd = jnp.where(step < ranks // 2, 1, 0)
    rank = lax.bitwise_xor(
        place_ref[1], relative_block(lax.rem(step, ranks // 2), odd, ranks)
    )
    part = logit_ref.shape[1]
    middle = part // 2
    start = rank * part
    for head in range(heads):
        logits = logit_ref[head].astype(F32)
        raised = jnp.exp(logits - jnp.max(logits, -1, keepdims=True))
        probs = raised / jnp.sum(raised, -1, keepdims=True)
        at = pl.ds(pl.multiple_of(start, part), part)
        total = dot_nt(long_ref[head, at, :], value_ref[head])
        out_ref[head] = probs * (total - jnp.sum(total * probs, -1, keepdims=True))

        @pl.when(start < SHORT)
        def _():
            corner = logits[:, :SHORT]
            lifted = jnp.exp(corner - jnp.max(corner, -1, keepdims=True))
            small = lifted / jnp.sum(lifted, -1, keepdims=True)
            sums = dot_nt(short_ref[head, at, :], value_ref[head, :SHORT, :])
            more = small * (sums - jnp.sum(sums * small, -1, keepdims=True))
            out_ref[head, :, :SHORT] += more

    @pl.when(step < ranks // 2)
    def _():
        sends[0][0] = out_ref[:, :middle, :].astype(BF16)
        sends[1][0] = out_ref[:, middle:, :].astype(BF16)

    @pl.when(step >= ranks // 2)
    def _():
        keeps[0][0] = out_ref[:, :middle, :].astype(BF16)
        keeps[1][0] = out_ref[:, middle:, :].astype(BF16)


def logit_grads(place, lengths, grads, values, logits, ranks, count):
    chunks, zones = len(grads), len(grads[0])
    heads, full, _ = logits.shape
    rows, wide = grads[0][0].shape
    size = wide // heads // count
    part = full // ranks
    half, rest = ranks // 2, ranks // 8

    def pick(step, place_ref, _):
        odd = jnp.where(step < half, 1, 0)
        block = relative_block(lax.rem(step, half), odd, ranks)
        return (0, lax.bitwise_xor(place_ref[1], block), 0)

    def spec(order, keep):
        def number(step, *_):
            at = jnp.maximum(step - half, 0) if keep else jnp.minimum(step, half - 1)
            return (order(at // rest) * rest + lax.rem(at, rest), 0, 0, 0)

        return pl.BlockSpec((1, heads, part // 2, full), number)

    flat = [piece for group in grads for piece in group] + [
        piece for group in values for piece in group
    ]
    every = chunks * count * size
    shape = (half, heads, part // 2, full)
    return pl.pallas_call(
        functools.partial(logits_kernel, zones, chunks, count, heads, size, rows, ranks),
        grid_spec=pltpu.PrefetchScalarGridSpec(
            num_scalar_prefetch=2,
            grid=(ranks,),
            in_specs=[whole((rows, wide))] * len(flat)
            + [pl.BlockSpec((heads, part, full), pick)],
            out_specs=[
                spec(order, keep) for keep in (False, True) for order in (place_first, place_second)
            ],
            scratch_shapes=[
                pltpu.VMEM((heads, full, every), BF16),
                pltpu.VMEM((heads, SHORT, every), BF16),
                pltpu.VMEM((heads, full, every), BF16),
                pltpu.VMEM((heads, part, full), F32),
            ],
        ),
        out_shape=[far(shape, BF16)] * 4,
        compiler_params=params(24),
        cost_estimate=cost(
            2 * heads * full * full * every, 4 * heads * full * full, heads * full * full
        ),
        name="logits",
    )(place, lengths, *map(kept, flat), kept(logits))


def input_kernel(zones, heads, size, ranks, count, place_ref, *refs):
    pieces = refs[:zones]
    x_ref, gain_ref, weight_ref, extra_in_ref = refs[zones : zones + 4]
    resid_ref = refs[zones + 4]
    grad_ref, send_ref, keep_ref, total_ref, gain_sum_ref, extra_ref = refs[zones + 5 :]
    depth = x_ref.shape[2]
    seq = pl.program_id(0)

    @pl.when(seq == 0)
    def _():
        total_ref[...] = jnp.zeros_like(total_ref)
        gain_sum_ref[...] = jnp.zeros_like(gain_sum_ref)

    hat, inverse = norm_of(x_ref[0].astype(F32))
    norm = (hat * gain_ref[...]).astype(BF16)
    pair = 128 // size
    parts = []
    lane = lax.broadcasted_iota(jnp.int32, (1, 128), 1)
    for piece in pieces:
        for head in range(heads):
            at = pl.multiple_of((head * count + seq // pair * pair) * size, 128)
            both = piece[:, pl.ds(at, 128)].astype(F32)
            moved = pltpu.roll(both, shift=size, axis=1)
            parts.append(jnp.where(lax.rem(seq, pair) == 0, both, moved)[:, :size])
    back = jnp.concatenate(parts, axis=1).astype(BF16)
    grad_norm = dot_nn(back, weight_ref[...])
    gain_sum_ref[...] += jnp.sum(grad_norm * hat, 0, keepdims=True)
    resid = resid_ref[...].astype(F32).T
    grad = resid + norm_back(grad_norm * gain_ref[...], hat, inverse)
    grad_ref[0] = grad.astype(BF16)
    total_ref[...] += dot_tn(norm, back)

    @pl.when(seq == count - 1)
    def _():
        extra_ref[...] = extra_in_ref[...]
        share = depth // ranks // zones
        for index in range(ranks * zones):
            extra_ref[index : index + 1, :share] = gain_sum_ref[
                :, index * share : (index + 1) * share
            ]
        store_square(place_ref, (send_ref, keep_ref), total_ref, extra_ref, zones, ranks)


def input_grads(place, pieces, x, gain, weight, resid, extra, heads, ranks):
    zones = len(pieces)
    count, rows, depth = x.shape
    size = depth // zones // heads
    assert 2 * size == 128 and count % 2 == 0
    height = -(-(group_rows(depth // ranks, zones) + 1) // 16) * 16
    shape = (ranks // 2, zones, height, depth)
    return pl.pallas_call(
        functools.partial(input_kernel, zones, heads, size, ranks, count),
        grid_spec=pltpu.PrefetchScalarGridSpec(
            num_scalar_prefetch=1,
            grid=(count,),
            in_specs=[whole(pieces[0].shape)] * zones
            + [
                pl.BlockSpec((1, rows, depth), lambda s, *_: (s, 0, 0)),
                whole(gain.shape),
                whole(weight.shape),
                whole(extra.shape),
                pl.BlockSpec((depth, rows), lambda s, *_: (0, s)),
            ],
            out_specs=[
                pl.BlockSpec((1, rows, depth), lambda s, *_: (s, 0, 0)),
                whole(shape),
                whole(shape),
            ],
            scratch_shapes=[
                pltpu.VMEM((depth, depth), F32),
                pltpu.VMEM((1, depth), F32),
                pltpu.VMEM(extra.shape, F32),
            ],
        ),
        out_shape=[
            far(x.shape, BF16),
            jax.ShapeDtypeStruct(shape, BF16),
            jax.ShapeDtypeStruct(shape, BF16),
        ],
        compiler_params=params(24),
        cost_estimate=cost(
            4 * count * rows * depth * depth, 12 * count * rows * depth + 8 * depth * depth
        ),
        name="input",
    )(place, *map(kept, pieces), kept(x), gain, kept(weight), extra, kept(resid))


def total_of(terms):
    total = terms[0][...]
    for term in terms[1:]:
        total = total + term[...].astype(F32)
    return total


def unpack(packed, rows, zones):
    width = packed.shape[1] // zones
    parts = [packed[:, k * width : (k + 1) * width] for k in range(zones)]
    return jnp.concatenate(parts, axis=0)[:rows]


def feed_sums_kernel(zones, tile, square, *refs):
    up_ref, down_ref, square_ref = refs[zones:]
    total = total_of(refs[:zones])
    up_ref[...] = total[:tile]
    down_ref[...] = total[tile : 2 * tile]
    packed = total[2 * tile : 2 * tile + group_rows(square, zones)]
    square_ref[...] = unpack(packed, square, zones).T


def feed_sums(terms, tile, square, zones):
    depth = terms[0].shape[1]
    return pl.pallas_call(
        functools.partial(feed_sums_kernel, zones, tile, square),
        grid=(1,),
        in_specs=[whole(term.shape) for term in terms],
        out_specs=[whole((tile, depth)), whole((tile, depth)), whole((depth // zones, square))],
        out_shape=[
            far((tile, depth), F32),
            far((tile, depth), F32),
            far((depth // zones, square), F32),
        ],
        compiler_params=params(12),
        name="feed_sums",
    )(*map(kept, terms))


def value_sums_kernel(zones, square, *refs):
    square_ref, line_ref = refs[zones:]
    total = total_of(refs[:zones])
    group = group_rows(square, zones)
    square_ref[...] = unpack(total[:group], square, zones)
    line_ref[...] = total[group : group + 1]


def value_sums(terms, square, zones):
    depth = terms[0].shape[1]
    return pl.pallas_call(
        functools.partial(value_sums_kernel, zones, square),
        grid=(1,),
        in_specs=[whole(term.shape) for term in terms],
        out_specs=[whole((square, depth // zones)), whole((1, depth))],
        out_shape=[far((square, depth // zones), F32), jax.ShapeDtypeStruct((1, depth), F32)],
        compiler_params=params(12),
        name="value_sums",
    )(*terms)


def shift(value, axis, extent, by):
    by = by % extent
    return lax.ppermute(value, axis, [(i, (i + by) % extent) for i in range(extent)])


def flip(value, axis, extent, mask):
    return lax.ppermute(value, axis, [(i, i ^ mask) for i in range(extent)])


def widen(value):
    return value.astype(F32)


def after(value, *results):
    return lax.optimization_barrier((value, *results))[0]


def exchange(pieces, extent, sign, *results):
    sent = pieces[1:]
    if results:
        sent = lax.optimization_barrier((*sent, *results))[: extent - 1]
    return [pieces[0]] + [
        shift(piece, "head", extent, sign * (d + 1)) for d, piece in enumerate(sent)
    ]


def exchange_some(pieces, numbers, extent, sign, *results):
    sent = [pieces[d] for d in numbers]
    if results:
        sent = lax.optimization_barrier((*sent, *results))[: len(sent)]
    return [shift(piece, "head", extent, sign * d) for d, piece in zip(numbers, sent)]


class Reduce:
    masks = ((2, 4), (4, 2))

    def __init__(self, ranks):
        self.ranks = ranks

    def core(self, sends):
        self.came = [flip(send, "dp", self.ranks, 1) for send in sends]

    def first(self, keeps, *results):
        half = self.ranks // 4
        sent = [
            (widen(keep[:half]) + widen(came[:half])).astype(BF16)
            for keep, came in zip(keeps, self.came)
        ]
        if results:
            sent = [after(value, *results) for value in sent]
        self.keeps, self.sent = keeps, sent
        self.went = [
            flip(value, "dp", self.ranks, masks[0]) for value, masks in zip(sent, self.masks)
        ]

    def rest(self, start, stop):
        half = self.ranks // 4
        return [
            widen(keep[half + start : half + stop])
            + widen(came[half + start : half + stop])
            + widen(went[start:stop])
            for keep, came, went in zip(self.keeps, self.came, self.went)
        ]

    def second(self, *results):
        sent = [value.astype(BF16) for value in self.rest(self.ranks // 8, self.ranks // 4)]
        if results:
            sent = [after(value, *results) for value in sent]
        self.last = [
            flip(value, "dp", self.ranks, masks[1]) for value, masks in zip(sent, self.masks)
        ]

    def finish(self, *results):
        lasts = self.last
        if results:
            lasts = lax.optimization_barrier((*lasts, *results))[:2]
        sides = []
        for own, last in zip(self.rest(0, self.ranks // 8), lasts):
            total = own + widen(last)
            side = total[0]
            for third in range(1, self.ranks // 8):
                side = side + widen(flip(total[third].astype(BF16), "dp", self.ranks, 8 * third))
            sides.append(side)
        return sides


def reduce_direct(send, keep, ranks, *results):
    rest = ranks // 8
    came = flip(after(send, *results), "dp", ranks, 1)
    both = [
        widen(keep[q * rest : (q + 1) * rest]) + widen(came[q * rest : (q + 1) * rest])
        for q in range(4)
    ]
    total = both[0]
    for q in range(1, 4):
        total = total + widen(flip(both[q].astype(BF16), "dp", ranks, 2 * q))
    own = total[0]
    for third in range(1, rest):
        own = own + widen(flip(total[third].astype(BF16), "dp", ranks, 8 * third))
    return own


def spread_head(blocks, zones):
    return [blocks[0]] + [
        shift(blocks[d].astype(BF16), "head", zones, d) for d in range(1, zones)
    ]


def local(
    zones,
    ranks,
    block_input,
    lengths,
    cotangent,
    norm1_gain,
    value_projection_weight,
    rand_logits,
    output_projection_weight,
    norm2_gain,
    up_projection_weight,
    up_bias,
    down_projection_weight,
    down_bias,
):
    seq_count, rows, depth = block_input.shape
    heads, full, _ = rand_logits.shape
    hidden = up_bias.shape[0]
    assert rows == SHORT and full == rows * zones and ranks % 8 == 0
    count = seq_count // 2
    assert seq_count == 2 * count
    place = jnp.stack([lax.axis_index("head"), lax.axis_index("dp")]).astype(jnp.int32)
    gain1, gain2 = norm1_gain[None], norm2_gain[None]
    width = value_projection_weight.shape[1]

    slot = width // ranks
    project = lax.dynamic_slice_in_dim(output_projection_weight, place[1] * slot, slot, 0)
    project = lax.all_gather(project, ("head", "dp"), axis=0, tiled=True)

    own = value_projection_weight.T
    half = width // 2
    parity = lax.rem(place[1], 2)
    part_rows = lax.dynamic_slice_in_dim(own, parity * half, half, 0)
    mine = [shift(part_rows, "head", zones, -d) for d in range(1, zones)]
    probs, probs_t, corner, corner_t = make_probs(rand_logits)
    others = flip(after(jnp.stack(mine), corner), "dp", ranks, 1)
    place = after(place, corner)

    def part(array, c):
        return array[c * count : (c + 1) * count]

    def call_values(place, c, weights):
        return make_values(place, part(block_input, c), gain1, weights, zones, heads, c == 0)

    def call_feed(place, c, pieces, earlier):
        return feed(
            place,
            pieces,
            part(block_input, c),
            part(cotangent, c),
            project,
            gain2,
            up_projection_weight,
            up_bias[None],
            down_projection_weight,
            down_bias[None],
            heads,
            c,
            2,
            earlier,
        )

    made = call_values(place, 0, [own, *mine, others])
    weight = made[zones]
    place = after(place, weight)
    values0 = exchange(made[:zones], zones, 1)
    made = call_values(place, 1, [weight])
    place = after(place, made[0])
    values1 = exchange(made, zones, 1, *values0)

    made = mix(place, part(lengths, 0), [values0], probs, corner, count, 1)
    place = after(place, made[0])
    mixed0 = exchange(made, zones, 1, *values1)
    made = mix(place, part(lengths, 1), [values1], probs, corner, count, 1)
    place = after(place, made[0])
    mixed1 = exchange(made, zones, 1, *mixed0)

    feed0 = call_feed(place, 0, mixed0, ())
    place = after(place, feed0[0])
    grads0 = exchange(feed0[:zones], zones, -1, *mixed1)
    feed1 = call_feed(place, 1, mixed1, feed0[zones : zones + 5])
    place = after(place, feed1[0], *grads0)
    act, pre, norm, attended = feed1[zones + 1 : zones + 5]
    up_sums, sums = zip(feed0[zones + 5 :], feed1[zones + 5 :])
    cot = cotangent.reshape(seq_count * rows, depth)

    weight_sum, rand_sum = Reduce(ranks), Reduce(ranks)

    def call_weights(place, odd):
        return weight_grads(
            place,
            act,
            pre,
            attended,
            norm,
            cot,
            (mixed0, mixed1),
            heads,
            odd,
            zones,
            ranks,
        )

    grads1 = exchange(feed1[:zones], zones, -1, *grads0)
    sends = call_weights(place, 1)
    place = after(place, sends[0], *grads1)
    weight_sum.core([after(value, *grads1) for value in sends])
    made = mix(place, lengths, [grads0, grads1], probs_t, corner_t, count, -1)
    place = after(place, made[0])
    evens = exchange_some(made, range(2, zones, 2), zones, -1)
    keeps = call_weights(place, 0)
    place = after(place, keeps[0], *evens, *weight_sum.came)
    odds = exchange_some(made, range(1, zones, 2), zones, -1, *evens)
    backs = [made[0]] + [(odds if d % 2 else evens)[(d - 1) // 2] for d in range(1, zones)]
    weight_sum.first(keeps, *evens)
    rand = logit_grads(
        place, lengths, (grads0, grads1), (values0, values1), rand_logits, ranks, count
    )
    place = after(place, rand[0], *weight_sum.went, *odds)

    rand_sum.core([after(value, *weight_sum.went, *odds) for value in rand[:2]])
    weight_sum.second(rand[0], *odds)
    place = after(place, *rand_sum.came)

    up_total = (up_sums[0] + up_sums[1]).reshape(ranks * zones, -1)
    rest_total = sums[0] + sums[1]
    gain_total, bias_total = (
        rest_total[i].reshape(ranks * zones, -1) for i in range(2)
    )
    up_size, gain_size = hidden // ranks // zones, depth // ranks // zones
    extra = jnp.concatenate([jnp.zeros_like(gain_total), gain_total, bias_total, up_total], 1)
    extra = jnp.pad(extra, ((0, 0), (0, depth - extra.shape[1])))

    rand_sum.first(rand[2:], *backs)
    grad_x, value_send, value_keep = input_grads(
        place, backs, block_input, gain1, weight, attended, extra, heads, ranks
    )
    sides = weight_sum.finish(*rand_sum.sent)
    terms = [side[d] for side in sides for d in range(zones // 2)]
    far_apart = zones // 2
    for d in (far_apart, *(d for d in range(1, zones) if d != far_apart)):
        sent = terms[d].astype(BF16)
        if d != far_apart:
            sent = after(sent, terms[far_apart])
        terms[d] = shift(sent, "head", zones, d)
    rand_sum.second(value_send, terms[far_apart])
    value_own = reduce_direct(value_send, value_keep, ranks, *rand_sum.went)
    tile, square = hidden // ranks // zones, depth // ranks
    value_blocks = [value_own[d].astype(F32 if d == 0 else BF16) for d in range(zones)]
    value_blocks[1:] = [after(value, *terms[1:]) for value in value_blocks[1:]]
    value_terms = spread_head(value_blocks, zones)
    terms = lax.optimization_barrier((*terms, *value_blocks[1:]))[:zones]
    grad_up, grad_down, grad_out = feed_sums(terms, tile, square, zones)
    grad_value, line = value_sums(value_terms, square, zones)
    line = line[0]
    grad_rand = jnp.concatenate(rand_sum.finish(*value_blocks[1:]), 1)
    return (
        feed1[zones],
        grad_x,
        grad_rand,
        grad_value,
        grad_out,
        line[:gain_size],
        line[gain_size : 2 * gain_size],
        grad_up.T,
        line[3 * gain_size : 3 * gain_size + up_size],
        grad_down,
        line[2 * gain_size : 3 * gain_size],
    )


def solution(mesh):
    in_specs = (
        P("dp", "head", None),
        P("dp"),
        P("dp", "head", None),
        P(),
        P(None, "head"),
        P("head", None, None),
        P("head", None),
        P(),
        P(),
        P(),
        P(),
        P(),
    )
    out_specs = (
        P("dp", "head", None),
        P("dp", "head", None),
        P("head", "dp", None),
        P("dp", "head"),
        P("head", "dp"),
        P(("dp", "head")),
        P(("dp", "head")),
        P(None, ("dp", "head")),
        P(("dp", "head")),
        P(("dp", "head"), None),
        P(("dp", "head")),
    )
    body = functools.partial(local, mesh.shape["head"], mesh.shape["dp"])
    return jax.shard_map(
        body, mesh=mesh, in_specs=in_specs, out_specs=out_specs, check_vma=False
    )
```

```python
import functools

import jax
import jax.numpy as jnp
from jax import lax
from jax.experimental import pallas as pl
from jax.experimental.pallas import tpu as pltpu
from jax.sharding import PartitionSpec as P

SHORT = 256
EPSILON = 1e-05
F32 = jnp.float32
BF16 = jnp.bfloat16
GELU_C = 0.7978845608028654
GELU_A = 0.044715
SHARE = 1.0


def dot_nn(a, b):
    return lax.dot_general(a, b, (((1,), (0,)), ((), ())), preferred_element_type=F32)


def dot_nt(a, b):
    return lax.dot_general(a, b, (((1,), (1,)), ((), ())), preferred_element_type=F32)


def dot_tn(a, b):
    return lax.dot_general(a, b, (((0,), (0,)), ((), ())), preferred_element_type=F32)


def norm_of(value):
    centered = value - jnp.mean(value, -1, keepdims=True)
    inverse = lax.rsqrt(jnp.mean(centered * centered, -1, keepdims=True) + EPSILON)
    return centered * inverse, inverse


def norm_back(scaled, hat, inverse):
    return inverse * (
        scaled
        - jnp.mean(scaled, -1, keepdims=True)
        - hat * jnp.mean(scaled * hat, -1, keepdims=True)
    )


def interleave(values, heads, size):
    parts = []
    for head in range(heads):
        for value in values:
            parts.append(value[:, head * size : (head + 1) * size])
    return jnp.concatenate(parts, axis=1)


def separate(piece, seq, count, heads, size):
    parts = []
    for head in range(heads):
        at = (head * count + seq) * size
        parts.append(piece[:, at : at + size])
    return jnp.concatenate(parts, axis=1)


def far(shape, dtype):
    return pltpu.HBM(shape, dtype)


def kept(value):
    return pltpu.with_memory_space_constraint(value, pltpu.HBM)


def whole(shape):
    return pl.BlockSpec(
        shape, lambda *_: (0,) * len(shape), pipeline_mode=pl.Buffered(buffer_count=1)
    )


def resident():
    return pl.BlockSpec(memory_space=pltpu.VMEM)


def cost(flops, moved, special=0):
    return pl.CostEstimate(
        flops=int(flops * SHARE), bytes_accessed=int(moved * SHARE), transcendentals=0
    )


def params(megabytes, grid_dims=1):
    return pltpu.CompilerParams(
        dimension_semantics=("arbitrary",) * grid_dims, vmem_limit_bytes=megabytes << 20
    )


def probs_kernel(logit_ref, long_ref, long_t_ref, short_ref, short_t_ref):
    logits = logit_ref[0].astype(F32)
    raised = jnp.exp(logits - jnp.max(logits, -1, keepdims=True))
    probs = raised / jnp.sum(raised, -1, keepdims=True)
    long_ref[0] = probs.astype(BF16)
    long_t_ref[0] = probs.T.astype(BF16)

    @pl.when(pl.program_id(1) == 0)
    def _():
        corner = logits[:, :SHORT]
        lifted = jnp.exp(corner - jnp.max(corner, -1, keepdims=True))
        part = lifted / jnp.sum(lifted, -1, keepdims=True)
        short_ref[0] = part.astype(BF16)
        short_t_ref[0] = part.T.astype(BF16)


def make_probs(logits):
    heads, rows, _ = logits.shape
    return pl.pallas_call(
        probs_kernel,
        grid=(heads, rows // SHORT),
        in_specs=[pl.BlockSpec((1, SHORT, rows), lambda h, i: (h, i, 0))],
        out_specs=[
            pl.BlockSpec((1, SHORT, rows), lambda h, i: (h, i, 0)),
            pl.BlockSpec((1, rows, SHORT), lambda h, i: (h, 0, i)),
            pl.BlockSpec((1, SHORT, SHORT), lambda h, i: (h, 0, 0)),
            pl.BlockSpec((1, SHORT, SHORT), lambda h, i: (h, 0, 0)),
        ],
        out_shape=[
            far((heads, rows, rows), BF16),
            far((heads, rows, rows), BF16),
            jax.ShapeDtypeStruct((heads, SHORT, SHORT), BF16),
            jax.ShapeDtypeStruct((heads, SHORT, SHORT), BF16),
        ],
        compiler_params=params(20, 2),
        cost_estimate=cost(10 * logits.size, 6 * logits.size, logits.size),
        name="probs",
    )(kept(logits))


def values_kernel(zones, heads, size, first, place_ref, x_ref, gain_ref, *rest):
    width = heads * size
    if first:
        own_ref, others_ref = rest[0], rest[zones]
        mine = rest[1:zones]
        outs, weight_ref = rest[zones + 1 : 2 * zones + 1], rest[2 * zones + 1]
        half = width // 2
        parity = lax.rem(place_ref[1], 2)
        weight_ref[:width, :] = own_ref[...]
        for d in range(1, zones):
            at = pl.multiple_of(d * width + parity * half, 16)
            weight_ref[pl.ds(at, half), :] = mine[d - 1][...]
            at = pl.multiple_of(d * width + (1 - parity) * half, 16)
            weight_ref[pl.ds(at, half), :] = others_ref[d - 1]
    else:
        weight_ref, outs = rest[0], rest[1:]
    made = []
    for seq in range(x_ref.shape[0]):
        hat, _ = norm_of(x_ref[seq].astype(F32))
        norm = (hat * gain_ref[...]).astype(BF16)
        made.append(dot_nt(norm, weight_ref[...]))
    for d in range(zones):
        own = [value[:, d * width : (d + 1) * width] for value in made]
        outs[d][...] = interleave(own, heads, size).astype(BF16)


def make_values(place, x, gain, weights, zones, heads, first):
    count, rows, depth = x.shape
    wide = count * depth // zones
    operands = [x, gain, *weights]
    shapes = [jax.ShapeDtypeStruct((rows, wide), BF16)] * zones
    if first:
        shapes.append(jax.ShapeDtypeStruct((depth, depth), BF16))
    return pl.pallas_call(
        functools.partial(values_kernel, zones, heads, depth // zones // heads, first),
        grid_spec=pltpu.PrefetchScalarGridSpec(
            num_scalar_prefetch=1,
            grid=(1,),
            in_specs=[whole(operand.shape) for operand in operands],
            out_specs=[whole(shape.shape) for shape in shapes],
        ),
        out_shape=shapes,
        compiler_params=params(12),
        cost_estimate=cost(
            2 * count * rows * depth * depth, 2 * x.size * 2 + 4 * depth * depth
        ),
        name="values",
    )(place, *operands)


def mix_kernel(zones, chunks, count, size, rows, sign, place_ref, long_flags, *refs):
    pieces = refs[: chunks * zones]
    matrix_ref, corner_ref = refs[chunks * zones : chunks * zones + 2]
    outs, held = refs[chunks * zones + 2 : -1], refs[-1]
    place = place_ref[0]
    wide = count * size
    for c in range(chunks):
        for d in range(zones):
            source = lax.rem(place + zones - sign * d, zones)
            at = pl.ds(pl.multiple_of(source * rows, rows), rows)
            held[at, c * wide : (c + 1) * wide] = pieces[c * zones + d][...]
    lane = lax.broadcasted_iota(jnp.int32, (1, chunks * wide), 1)
    is_long = jnp.zeros((1, chunks * wide), jnp.bool_)
    for seq in range(chunks * count):
        inside = (lane >= seq * size) & (lane < (seq + 1) * size)
        is_long = is_long | (inside & (long_flags[seq] > SHORT))
    corner = dot_nn(corner_ref[0], held[:SHORT, :])
    for d in range(zones):
        target = lax.rem(place + zones + sign * d, zones)
        part = matrix_ref[0, pl.ds(pl.multiple_of(target * rows, rows), rows), :]
        full = dot_nn(part, held[...])
        small = jnp.where(target == 0, corner, jnp.zeros_like(corner))
        outs[d][...] = jnp.where(is_long, full, small).astype(BF16)


def mix(place, lengths, groups, matrix, corner, count, sign):
    chunks, zones = len(groups), len(groups[0])
    heads, full, _ = matrix.shape
    rows, wide = groups[0][0].shape
    lanes = wide // heads
    spec = pl.BlockSpec((rows, lanes), lambda h, *_: (0, h))
    out_spec = pl.BlockSpec((rows, chunks * lanes), lambda h, *_: (0, h))
    return pl.pallas_call(
        functools.partial(mix_kernel, zones, chunks, count, lanes // count, rows, sign),
        grid_spec=pltpu.PrefetchScalarGridSpec(
            num_scalar_prefetch=2,
            grid=(heads,),
            in_specs=[spec] * (chunks * zones)
            + [
                pl.BlockSpec((1, full, full), lambda h, *_: (h, 0, 0)),
                pl.BlockSpec((1, SHORT, SHORT), lambda h, *_: (h, 0, 0)),
            ],
            out_specs=[out_spec] * zones,
            scratch_shapes=[pltpu.VMEM((full, chunks * lanes), BF16)],
        ),
        out_shape=[jax.ShapeDtypeStruct((rows, chunks * wide), BF16)] * zones,
        compiler_params=params(16),
        cost_estimate=cost(
            2 * heads * full * full * lanes * chunks,
            2 * heads * full * full + 4 * full * wide * chunks,
        ),
        name="mix",
    )(place, lengths, *(piece for group in groups for piece in group), kept(matrix), corner)


def feed_kernel(zones, heads, size, steps, earlier, place_ref, *refs):
    pieces = refs[:zones]
    (x_ref, cot_ref, project_ref, gain_ref, up_ref, up_bias_ref, down_ref, down_bias_ref) = refs[
        zones : zones + 8
    ]
    outs = refs[zones + 8 + earlier :]
    grads = outs[:zones]
    (
        block_ref,
        act_t_ref,
        pre_t_ref,
        norm_out_ref,
        attended_ref,
        up_sum_ref,
        sums_ref,
        norm_ref,
        weight_ref,
        resid_ref,
        hat_ref,
        inv_ref,
        forward_ref,
        back_ref,
    ) = outs[zones:]
    count, rows, depth = x_ref.shape
    width = heads * size
    step = pl.program_id(0)

    @pl.when(step == 0)
    def _():
        for d in range(zones):
            other = lax.rem(place_ref[0] + zones - d, zones)
            at = pl.multiple_of(other * width, 16)
            weight_ref[d * width : (d + 1) * width, :] = project_ref[pl.ds(at, width), :]
        for seq in range(count):
            at = slice(seq * rows, (seq + 1) * rows)
            mixed = jnp.concatenate(
                [separate(piece[...], seq, count, heads, size) for piece in pieces], axis=1
            )
            resid = x_ref[seq].astype(F32) + dot_nn(mixed, weight_ref[...])
            hat, inverse = norm_of(resid)
            resid_ref[at, :] = resid + down_bias_ref[...]
            hat_ref[at, :] = hat
            inv_ref[at, :] = inverse
            norm_ref[at, :] = (hat * gain_ref[...]).astype(BF16)
        forward_ref[...] = jnp.zeros_like(forward_ref)
        back_ref[...] = jnp.zeros_like(back_ref)

    up_sum = jnp.zeros((1, up_ref.shape[1]), F32)
    for seq in range(count):
        at = slice(seq * rows, (seq + 1) * rows)
        pre = dot_nn(norm_ref[at, :], up_ref[...]) + up_bias_ref[...]
        grad_act = dot_nt(cot_ref[seq], down_ref[...])
        square = pre * pre
        bent = jnp.tanh(pre * (GELU_C + (GELU_C * GELU_A) * square))
        half = 0.5 + 0.5 * bent
        act = (pre * half).astype(BF16)
        slope = half + (0.5 * pre) * (1.0 - bent * bent) * (
            GELU_C + (3.0 * GELU_C * GELU_A) * square
        )
        grad_pre = (grad_act * slope).astype(BF16)
        up_sum = up_sum + jnp.sum(grad_pre.astype(F32), 0, keepdims=True)
        act_t_ref[:, at] = act.T
        pre_t_ref[:, at] = grad_pre.T
        forward = dot_nn(act, down_ref[...])
        back = dot_nt(grad_pre, up_ref[...])

        forward_ref[at, :] += forward
        back_ref[at, :] += back

    up_sum_ref[...] = up_sum
    share = norm_out_ref.shape[1]
    norm_out_ref[...] = norm_ref[:, pl.ds(pl.multiple_of(step * share, share), share)]

    @pl.when(step == steps - 1)
    def _():
        gain_sum = jnp.zeros((1, depth), F32)
        bias_sum = jnp.zeros((1, depth), F32)
        made = []
        for seq in range(count):
            at = slice(seq * rows, (seq + 1) * rows)
            block_ref[seq] = (resid_ref[at, :] + forward_ref[at, :]).astype(BF16)
            cot = cot_ref[seq].astype(F32)
            hat = hat_ref[at, :]
            back = back_ref[at, :]
            gain_sum = gain_sum + jnp.sum(back * hat, 0, keepdims=True)
            bias_sum = bias_sum + jnp.sum(cot, 0, keepdims=True)
            grad = cot + norm_back(back * gain_ref[...], hat, inv_ref[at, :])
            low = grad.astype(BF16)
            attended_ref[:, at] = low.T
            made.append(dot_nt(low, weight_ref[...]))
        sums_ref[0:1, :] = gain_sum
        sums_ref[1:2, :] = bias_sum
        for d in range(zones):
            mine = [value[:, d * width : (d + 1) * width] for value in made]
            grads[d][...] = interleave(mine, heads, size).astype(BF16)


def feed(place, pieces, x, cot, project, gain, up, up_bias, down, down_bias, heads, c, chunks, earlier):
    zones = len(pieces)
    count, rows, depth = x.shape
    size = depth // zones // heads
    hidden = up.shape[1]
    tile = min(512, hidden)
    steps = hidden // tile
    tokens = count * rows
    wide = pieces[0].shape[1]
    shapes = [jax.ShapeDtypeStruct((rows, wide), BF16)] * zones + [
        far((chunks * count, rows, depth), BF16),
        far((hidden, chunks * tokens), BF16),
        far((hidden, chunks * tokens), BF16),
        far((chunks * tokens, depth), BF16),
        far((depth, chunks * tokens), BF16),
        jax.ShapeDtypeStruct((1, hidden), F32),
        jax.ShapeDtypeStruct((2, depth), F32),
    ]
    return pl.pallas_call(
        functools.partial(feed_kernel, zones, heads, size, steps, len(earlier)),
        grid_spec=pltpu.PrefetchScalarGridSpec(
            num_scalar_prefetch=1,
            grid=(steps,),
            in_specs=[whole((rows, wide))] * zones
            + [
                whole(x.shape),
                whole(cot.shape),
                whole(project.shape),
                whole(gain.shape),
                pl.BlockSpec((depth, tile), lambda f, *_: (0, f)),
                pl.BlockSpec((1, tile), lambda f, *_: (0, f)),
                pl.BlockSpec((tile, depth), lambda f, *_: (f, 0)),
                whole(down_bias.shape),
            ]
            + [pl.BlockSpec(memory_space=pltpu.HBM)] * len(earlier),
            out_specs=[whole((rows, wide))] * zones
            + [
                pl.BlockSpec(
                    (count, rows, depth),
                    lambda *_: (c, 0, 0),
                    pipeline_mode=pl.Buffered(buffer_count=1),
                ),
                pl.BlockSpec((tile, tokens), lambda f, *_: (f, c)),
                pl.BlockSpec((tile, tokens), lambda f, *_: (f, c)),
                pl.BlockSpec((tokens, depth // steps), lambda f, *_: (c, f)),
                pl.BlockSpec(
                    (depth, tokens),
                    lambda *_: (0, c),
                    pipeline_mode=pl.Buffered(buffer_count=1),
                ),
                pl.BlockSpec((1, tile), lambda f, *_: (0, f)),
                whole((2, depth)),
            ],
            scratch_shapes=[
                pltpu.VMEM((tokens, depth), BF16),
                pltpu.VMEM((depth, depth), BF16),
                pltpu.VMEM((tokens, depth), F32),
                pltpu.VMEM((tokens, depth), F32),
                pltpu.VMEM((tokens, 1), F32),
                pltpu.VMEM((tokens, depth), F32),
                pltpu.VMEM((tokens, depth), F32),
            ],
        ),
        out_shape=shapes,
        compiler_params=params(28),
        cost_estimate=cost(
            8 * tokens * depth * hidden + 4 * tokens * depth * depth,
            4 * depth * hidden + 4 * tokens * hidden + 20 * tokens * depth,
            tokens * hidden,
        ),
        input_output_aliases={zones + 9 + i: zones + i for i in range(len(earlier))},
        name="feed",
    )(
        place,
        *map(kept, pieces),
        kept(x),
        kept(cot),
        kept(project),
        gain,
        kept(up),
        up_bias,
        kept(down),
        down_bias,
        *earlier,
    )


def relative_block(step, odd, ranks):
    rest = ranks // 8
    return odd + 2 * (step // rest) + 8 * lax.rem(step, rest)


def group_rows(rows, zones):
    return -(-rows // (8 * zones)) * 8


def pack(block, d, zones):
    rows, depth = block.shape
    width, group = depth // zones, group_rows(rows, zones)
    parts = []
    for k in range(zones):
        if k * group < rows:
            parts.append(block[k * group : (k + 1) * group, d * width : (d + 1) * width])
        else:
            parts.append(jnp.zeros((group, width), block.dtype))
    return jnp.concatenate(parts, axis=1)


def place_first(second):
    return second // 2 + 2 * (1 - lax.rem(second, 2))


def place_second(second):
    return lax.rem(second + 2, 4)


def weights_kernel(zones, chunks, heads, place_ref, *refs):
    act_ref, pre_ref, attended_ref, norm_ref, cot_ref = refs[:5]
    pieces = refs[5 : 5 + zones * chunks]
    first_ref, second_ref, scratch_ref, mixed_ref = refs[5 + zones * chunks :]
    part = scratch_ref.shape[1] // zones
    rows, wide = pieces[0].shape
    count = norm_ref.shape[0] // rows // chunks

    @pl.when(pl.program_id(0) == 0)
    def _():
        for c in range(chunks):
            group = pieces[c * zones : (c + 1) * zones]
            for seq in range(count):
                parts = [
                    separate(piece[...], seq, count, heads, wide // heads // count)
                    for piece in group
                ]
                at = (c * count + seq) * rows
                mixed_ref[at : at + rows, :] = jnp.concatenate(parts, axis=1)

    scratch_ref[0] = dot_nn(pre_ref[...], norm_ref[...])
    scratch_ref[1] = dot_nn(act_ref[...], cot_ref[...])
    square = dot_nn(attended_ref[...], mixed_ref[...])
    for d in range(zones):
        at = pl.ds(pl.multiple_of(lax.rem(place_ref[0] + d, zones) * part, 8), part)
        parts = [scratch_ref[0, at, :], scratch_ref[1, at, :], pack(square, -d % zones, zones)]
        used = sum(value.shape[0] for value in parts)
        parts.append(jnp.zeros((first_ref.shape[2] - used, first_ref.shape[3]), F32))
        side, number = (first_ref, d) if d < zones // 2 else (second_ref, d - zones // 2)
        side[0, number] = jnp.concatenate(parts, axis=0).astype(BF16)


def weight_grads(place, act, pre, attended, norm, cot, pieces, heads, odd, zones, ranks):
    chunks = len(pieces)
    hidden, tokens = act.shape
    depth = norm.shape[1]
    tile, square = hidden // ranks, depth // ranks
    rows = 2 * tile // zones + group_rows(square, zones)
    rows = -(-rows // 16) * 16
    rest = ranks // 8

    def tall(step, place_ref):
        return (lax.bitwise_xor(place_ref[1], relative_block(step, odd, ranks)), 0)

    def first(step, _):
        return (place_first(step // rest) * rest + lax.rem(step, rest), 0, 0, 0)

    def second(step, _):
        return (place_second(step // rest) * rest + lax.rem(step, rest), 0, 0, 0)

    shape = (ranks // 2, zones // 2, rows, depth)
    return pl.pallas_call(
        functools.partial(weights_kernel, zones, chunks, heads),
        grid_spec=pltpu.PrefetchScalarGridSpec(
            num_scalar_prefetch=1,
            grid=(ranks // 2,),
            in_specs=[pl.BlockSpec((tile, tokens), tall)] * 2
            + [pl.BlockSpec((square, tokens), tall)]
            + [whole((tokens, depth))] * 2
            + [whole(pieces[0][0].shape)] * (zones * chunks),
            out_specs=[pl.BlockSpec((1, *shape[1:]), first), pl.BlockSpec((1, *shape[1:]), second)],
            scratch_shapes=[
                pltpu.VMEM((2, tile, depth), F32),
                pltpu.VMEM((tokens, depth), BF16),
            ],
        ),
        out_shape=[far(shape, BF16)] * 2,
        compiler_params=params(24),
        cost_estimate=cost(
            2 * hidden * tokens * depth,
            2 * hidden * tokens + 2 * hidden * depth + 4 * tokens * depth,
        ),
        name="weights",
    )(
        place,
        *map(kept, (act, pre, attended, norm, cot)),
        *(kept(piece) for group in pieces for piece in group),
    )


def store_square(place_ref, outs, scratch_ref, extra_ref, zones, ranks):
    depth = scratch_ref.shape[0]
    part = depth // ranks
    for odd, out_ref in zip((1, 0), outs):
        for step in range(ranks // 2):
            rest = ranks // 8
            relative = odd + 2 * (step // rest) + 8 * (step % rest)
            rank = lax.bitwise_xor(place_ref[1], relative)
            block = scratch_ref[pl.ds(pl.multiple_of(rank * part, 8), part), :]
            for d in range(zones):
                zone = lax.rem(place_ref[0] + d, zones)
                line = extra_ref[pl.ds(rank * zones + zone, 1), :]
                packed = pack(block, d, zones)
                below = jnp.broadcast_to(line, (out_ref.shape[2] - packed.shape[0], depth))
                out_ref[step, d] = jnp.concatenate([packed, below], axis=0).astype(BF16)


def logits_kernel(
    zones, chunks, count, heads, size, rows, ranks, place_ref, lengths_ref, *refs
):
    grads = refs[: chunks * zones]
    values = refs[chunks * zones : 2 * chunks * zones]
    refs = refs[2 * chunks * zones :]
    logit_ref, sends, keeps = refs[0], refs[1:3], refs[3:5]
    long_ref, short_ref, value_ref, out_ref = refs[5:]
    place = place_ref[0]
    lanes = count * size
    step = pl.program_id(0)

    @pl.when(step == 0)
    def _():
        lane = lax.broadcasted_iota(jnp.int32, (1, lanes), 1)
        for c in range(chunks):
            is_long = jnp.zeros((1, lanes), jnp.bool_)
            for seq in range(count):
                inside = (lane >= seq * size) & (lane < (seq + 1) * size)
                is_long = is_long | (inside & (lengths_ref[c * count + seq] > SHORT))
            for d in range(zones):
                ahead = lax.rem(place + d, zones)
                behind = lax.rem(place + zones - d, zones)
                to = pl.ds(pl.multiple_of(ahead * rows, rows), rows)
                back = pl.ds(pl.multiple_of(behind * rows, rows), rows)
                for head in range(heads):
                    columns = slice(head * lanes, (head + 1) * lanes)
                    own = slice(c * lanes, (c + 1) * lanes)
                    grad = grads[c * zones + d][:, columns].astype(F32)
                    long_ref[head, to, own] = jnp.where(is_long, grad, 0.0).astype(BF16)
                    value_ref[head, back, own] = values[c * zones + d][:, columns]

                    @pl.when(ahead == 0)
                    def _():
                        short_ref[head, :, own] = jnp.where(is_long, 0.0, grad).astype(BF16)

    odd = jnp.where(step < ranks // 2, 1, 0)
    rank = lax.bitwise_xor(
        place_ref[1], relative_block(lax.rem(step, ranks // 2), odd, ranks)
    )
    part = logit_ref.shape[1]
    middle = part // 2
    start = rank * part
    for head in range(heads):
        logits = logit_ref[head].astype(F32)
        raised = jnp.exp(logits - jnp.max(logits, -1, keepdims=True))
        probs = raised / jnp.sum(raised, -1, keepdims=True)
        at = pl.ds(pl.multiple_of(start, part), part)
        total = dot_nt(long_ref[head, at, :], value_ref[head])
        out_ref[head] = probs * (total - jnp.sum(total * probs, -1, keepdims=True))

        @pl.when(start < SHORT)
        def _():
            corner = logits[:, :SHORT]
            lifted = jnp.exp(corner - jnp.max(corner, -1, keepdims=True))
            small = lifted / jnp.sum(lifted, -1, keepdims=True)
            sums = dot_nt(short_ref[head, at, :], value_ref[head, :SHORT, :])
            more = small * (sums - jnp.sum(sums * small, -1, keepdims=True))
            out_ref[head, :, :SHORT] += more

    @pl.when(step < ranks // 2)
    def _():
        sends[0][0] = out_ref[:, :middle, :].astype(BF16)
        sends[1][0] = out_ref[:, middle:, :].astype(BF16)

    @pl.when(step >= ranks // 2)
    def _():
        keeps[0][0] = out_ref[:, :middle, :].astype(BF16)
        keeps[1][0] = out_ref[:, middle:, :].astype(BF16)


def logit_grads(place, lengths, grads, values, logits, ranks, count):
    chunks, zones = len(grads), len(grads[0])
    heads, full, _ = logits.shape
    rows, wide = grads[0][0].shape
    size = wide // heads // count
    part = full // ranks
    half, rest = ranks // 2, ranks // 8

    def pick(step, place_ref, _):
        odd = jnp.where(step < half, 1, 0)
        block = relative_block(lax.rem(step, half), odd, ranks)
        return (0, lax.bitwise_xor(place_ref[1], block), 0)

    def spec(order, keep):
        def number(step, *_):
            at = jnp.maximum(step - half, 0) if keep else jnp.minimum(step, half - 1)
            return (order(at // rest) * rest + lax.rem(at, rest), 0, 0, 0)

        return pl.BlockSpec((1, heads, part // 2, full), number)

    flat = [piece for group in grads for piece in group] + [
        piece for group in values for piece in group
    ]
    every = chunks * count * size
    shape = (half, heads, part // 2, full)
    return pl.pallas_call(
        functools.partial(logits_kernel, zones, chunks, count, heads, size, rows, ranks),
        grid_spec=pltpu.PrefetchScalarGridSpec(
            num_scalar_prefetch=2,
            grid=(ranks,),
            in_specs=[whole((rows, wide))] * len(flat)
            + [pl.BlockSpec((heads, part, full), pick)],
            out_specs=[
                spec(order, keep) for keep in (False, True) for order in (place_first, place_second)
            ],
            scratch_shapes=[
                pltpu.VMEM((heads, full, every), BF16),
                pltpu.VMEM((heads, SHORT, every), BF16),
                pltpu.VMEM((heads, full, every), BF16),
                pltpu.VMEM((heads, part, full), F32),
            ],
        ),
        out_shape=[far(shape, BF16)] * 4,
        compiler_params=params(24),
        cost_estimate=cost(
            2 * heads * full * full * every, 4 * heads * full * full, heads * full * full
        ),
        name="logits",
    )(place, lengths, *map(kept, flat), kept(logits))


def input_kernel(zones, heads, size, ranks, count, place_ref, *refs):
    pieces = refs[:zones]
    x_ref, gain_ref, weight_ref, extra_in_ref = refs[zones : zones + 4]
    resid_ref = refs[zones + 4]
    grad_ref, send_ref, keep_ref, total_ref, gain_sum_ref, extra_ref = refs[zones + 5 :]
    depth = x_ref.shape[2]
    seq = pl.program_id(0)

    @pl.when(seq == 0)
    def _():
        total_ref[...] = jnp.zeros_like(total_ref)
        gain_sum_ref[...] = jnp.zeros_like(gain_sum_ref)

    hat, inverse = norm_of(x_ref[0].astype(F32))
    norm = (hat * gain_ref[...]).astype(BF16)
    pair = 128 // size
    parts = []
    lane = lax.broadcasted_iota(jnp.int32, (1, 128), 1)
    for piece in pieces:
        for head in range(heads):
            at = pl.multiple_of((head * count + seq // pair * pair) * size, 128)
            both = piece[:, pl.ds(at, 128)].astype(F32)
            moved = pltpu.roll(both, shift=size, axis=1)
            parts.append(jnp.where(lax.rem(seq, pair) == 0, both, moved)[:, :size])
    back = jnp.concatenate(parts, axis=1).astype(BF16)
    grad_norm = dot_nn(back, weight_ref[...])
    gain_sum_ref[...] += jnp.sum(grad_norm * hat, 0, keepdims=True)
    resid = resid_ref[...].astype(F32).T
    grad = resid + norm_back(grad_norm * gain_ref[...], hat, inverse)
    grad_ref[0] = grad.astype(BF16)
    total_ref[...] += dot_tn(norm, back)

    @pl.when(seq == count - 1)
    def _():
        extra_ref[...] = extra_in_ref[...]
        share = depth // ranks // zones
        for index in range(ranks * zones):
            extra_ref[index : index + 1, :share] = gain_sum_ref[
                :, index * share : (index + 1) * share
            ]
        store_square(place_ref, (send_ref, keep_ref), total_ref, extra_ref, zones, ranks)


def input_grads(place, pieces, x, gain, weight, resid, extra, heads, ranks):
    zones = len(pieces)
    count, rows, depth = x.shape
    size = depth // zones // heads
    assert 2 * size == 128 and count % 2 == 0
    height = -(-(group_rows(depth // ranks, zones) + 1) // 16) * 16
    shape = (ranks // 2, zones, height, depth)
    return pl.pallas_call(
        functools.partial(input_kernel, zones, heads, size, ranks, count),
        grid_spec=pltpu.PrefetchScalarGridSpec(
            num_scalar_prefetch=1,
            grid=(count,),
            in_specs=[whole(pieces[0].shape)] * zones
            + [
                pl.BlockSpec((1, rows, depth), lambda s, *_: (s, 0, 0)),
                whole(gain.shape),
                whole(weight.shape),
                whole(extra.shape),
                pl.BlockSpec((depth, rows), lambda s, *_: (0, s)),
            ],
            out_specs=[
                pl.BlockSpec((1, rows, depth), lambda s, *_: (s, 0, 0)),
                whole(shape),
                whole(shape),
            ],
            scratch_shapes=[
                pltpu.VMEM((depth, depth), F32),
                pltpu.VMEM((1, depth), F32),
                pltpu.VMEM(extra.shape, F32),
            ],
        ),
        out_shape=[
            far(x.shape, BF16),
            jax.ShapeDtypeStruct(shape, BF16),
            jax.ShapeDtypeStruct(shape, BF16),
        ],
        compiler_params=params(24),
        cost_estimate=cost(
            4 * count * rows * depth * depth, 12 * count * rows * depth + 8 * depth * depth
        ),
        name="input",
    )(place, *map(kept, pieces), kept(x), gain, kept(weight), extra, kept(resid))


def total_of(terms):
    total = terms[0][...]
    for term in terms[1:]:
        total = total + term[...].astype(F32)
    return total


def unpack(packed, rows, zones):
    width = packed.shape[1] // zones
    parts = [packed[:, k * width : (k + 1) * width] for k in range(zones)]
    return jnp.concatenate(parts, axis=0)[:rows]


def feed_sums_kernel(zones, tile, square, *refs):
    up_ref, down_ref, square_ref = refs[zones:]
    total = total_of(refs[:zones])
    up_ref[...] = total[:tile]
    down_ref[...] = total[tile : 2 * tile]
    packed = total[2 * tile : 2 * tile + group_rows(square, zones)]
    square_ref[...] = unpack(packed, square, zones).T


def feed_sums(terms, tile, square, zones):
    depth = terms[0].shape[1]
    return pl.pallas_call(
        functools.partial(feed_sums_kernel, zones, tile, square),
        grid=(1,),
        in_specs=[whole(term.shape) for term in terms],
        out_specs=[whole((tile, depth)), whole((tile, depth)), whole((depth // zones, square))],
        out_shape=[
            far((tile, depth), F32),
            far((tile, depth), F32),
            far((depth // zones, square), F32),
        ],
        compiler_params=params(12),
        name="feed_sums",
    )(*map(kept, terms))


def value_sums_kernel(zones, square, *refs):
    square_ref, line_ref = refs[zones:]
    total = total_of(refs[:zones])
    group = group_rows(square, zones)
    square_ref[...] = unpack(total[:group], square, zones)
    line_ref[...] = total[group : group + 1]


def value_sums(terms, square, zones):
    depth = terms[0].shape[1]
    return pl.pallas_call(
        functools.partial(value_sums_kernel, zones, square),
        grid=(1,),
        in_specs=[whole(term.shape) for term in terms],
        out_specs=[whole((square, depth // zones)), whole((1, depth))],
        out_shape=[far((square, depth // zones), F32), jax.ShapeDtypeStruct((1, depth), F32)],
        compiler_params=params(12),
        name="value_sums",
    )(*terms)


def shift(value, axis, extent, by):
    by = by % extent
    return lax.ppermute(value, axis, [(i, (i + by) % extent) for i in range(extent)])


def flip(value, axis, extent, mask):
    return lax.ppermute(value, axis, [(i, i ^ mask) for i in range(extent)])


def widen(value):
    return value.astype(F32)


def after(value, *results):
    return lax.optimization_barrier((value, *results))[0]


def exchange(pieces, extent, sign, *results):
    sent = pieces[1:]
    if results:
        sent = lax.optimization_barrier((*sent, *results))[: extent - 1]
    return [pieces[0]] + [
        shift(piece, "head", extent, sign * (d + 1)) for d, piece in enumerate(sent)
    ]


def exchange_some(pieces, numbers, extent, sign, *results):
    sent = [pieces[d] for d in numbers]
    if results:
        sent = lax.optimization_barrier((*sent, *results))[: len(sent)]
    return [shift(piece, "head", extent, sign * d) for d, piece in zip(numbers, sent)]


class Reduce:
    masks = ((2, 4), (4, 2))

    def __init__(self, ranks):
        self.ranks = ranks

    def core(self, sends):
        self.came = [flip(send, "dp", self.ranks, 1) for send in sends]

    def first(self, keeps, *results):
        half = self.ranks // 4
        sent = [
            (widen(keep[:half]) + widen(came[:half])).astype(BF16)
            for keep, came in zip(keeps, self.came)
        ]
        if results:
            sent = [after(value, *results) for value in sent]
        self.keeps, self.sent = keeps, sent
        self.went = [
            flip(value, "dp", self.ranks, masks[0]) for value, masks in zip(sent, self.masks)
        ]

    def rest(self, start, stop):
        half = self.ranks // 4
        return [
            widen(keep[half + start : half + stop])
            + widen(came[half + start : half + stop])
            + widen(went[start:stop])
            for keep, came, went in zip(self.keeps, self.came, self.went)
        ]

    def second(self, *results):
        sent = [value.astype(BF16) for value in self.rest(self.ranks // 8, self.ranks // 4)]
        if results:
            sent = [after(value, *results) for value in sent]
        self.last = [
            flip(value, "dp", self.ranks, masks[1]) for value, masks in zip(sent, self.masks)
        ]

    def finish(self, *results):
        lasts = self.last
        if results:
            lasts = lax.optimization_barrier((*lasts, *results))[:2]
        sides = []
        for own, last in zip(self.rest(0, self.ranks // 8), lasts):
            total = own + widen(last)
            side = total[0]
            for third in range(1, self.ranks // 8):
                side = side + widen(flip(total[third].astype(BF16), "dp", self.ranks, 8 * third))
            sides.append(side)
        return sides


def reduce_direct(send, keep, ranks, *results):
    rest = ranks // 8
    came = flip(after(send, *results), "dp", ranks, 1)
    both = [
        widen(keep[q * rest : (q + 1) * rest]) + widen(came[q * rest : (q + 1) * rest])
        for q in range(4)
    ]
    total = both[0]
    for q in range(1, 4):
        total = total + widen(flip(both[q].astype(BF16), "dp", ranks, 2 * q))
    own = total[0]
    for third in range(1, rest):
        own = own + widen(flip(total[third].astype(BF16), "dp", ranks, 8 * third))
    return own


def spread_head(blocks, zones):
    return [blocks[0]] + [
        shift(blocks[d].astype(BF16), "head", zones, d) for d in range(1, zones)
    ]


def local(
    zones,
    ranks,
    block_input,
    lengths,
    cotangent,
    norm1_gain,
    value_projection_weight,
    rand_logits,
    output_projection_weight,
    norm2_gain,
    up_projection_weight,
    up_bias,
    down_projection_weight,
    down_bias,
):
    seq_count, rows, depth = block_input.shape
    heads, full, _ = rand_logits.shape
    hidden = up_bias.shape[0]
    assert rows == SHORT and full == rows * zones and ranks % 8 == 0
    count = seq_count // 2
    assert seq_count == 2 * count
    place = jnp.stack([lax.axis_index("head"), lax.axis_index("dp")]).astype(jnp.int32)
    gain1, gain2 = norm1_gain[None], norm2_gain[None]
    width = value_projection_weight.shape[1]

    slot = width // ranks
    project = lax.dynamic_slice_in_dim(output_projection_weight, place[1] * slot, slot, 0)
    project = lax.all_gather(project, ("head", "dp"), axis=0, tiled=True)

    own = value_projection_weight.T
    half = width // 2
    parity = lax.rem(place[1], 2)
    part_rows = lax.dynamic_slice_in_dim(own, parity * half, half, 0)
    mine = [shift(part_rows, "head", zones, -d) for d in range(1, zones)]
    probs, probs_t, corner, corner_t = make_probs(rand_logits)
    others = flip(after(jnp.stack(mine), corner), "dp", ranks, 1)
    place = after(place, corner)

    def part(array, c):
        return array[c * count : (c + 1) * count]

    def call_values(place, c, weights):
        return make_values(place, part(block_input, c), gain1, weights, zones, heads, c == 0)

    def call_feed(place, c, pieces, earlier):
        return feed(
            place,
            pieces,
            part(block_input, c),
            part(cotangent, c),
            project,
            gain2,
            up_projection_weight,
            up_bias[None],
            down_projection_weight,
            down_bias[None],
            heads,
            c,
            2,
            earlier,
        )

    made = call_values(place, 0, [own, *mine, others])
    weight = made[zones]
    place = after(place, weight)
    values0 = exchange(made[:zones], zones, 1)
    made = call_values(place, 1, [weight])
    place = after(place, made[0])
    values1 = exchange(made, zones, 1, *values0)

    made = mix(place, part(lengths, 0), [values0], probs, corner, count, 1)
    place = after(place, made[0])
    mixed0 = [made[0]] + exchange_some(made, range(1, zones - 1), zones, 1)
    mixed0 += exchange_some(made, (zones - 1,), zones, 1, *values1)
    made = mix(place, part(lengths, 1), [values1], probs, corner, count, 1)
    place = after(place, made[0])
    mixed1 = exchange(made, zones, 1, *mixed0)

    feed0 = call_feed(place, 0, mixed0, ())
    place = after(place, feed0[0])
    grads0 = exchange(feed0[:zones], zones, -1, *mixed1)
    feed1 = call_feed(place, 1, mixed1, feed0[zones : zones + 5])
    place = after(place, feed1[0], *grads0)
    act, pre, norm, attended = feed1[zones + 1 : zones + 5]
    up_sums, sums = zip(feed0[zones + 5 :], feed1[zones + 5 :])
    cot = cotangent.reshape(seq_count * rows, depth)

    weight_sum, rand_sum = Reduce(ranks), Reduce(ranks)

    def call_weights(place, odd):
        return weight_grads(
            place,
            act,
            pre,
            attended,
            norm,
            cot,
            (mixed0, mixed1),
            heads,
            odd,
            zones,
            ranks,
        )

    grads1 = exchange(feed1[:zones], zones, -1, *grads0)
    sends = call_weights(place, 1)
    place = after(place, sends[0], *grads1)
    weight_sum.core([after(value, *grads1) for value in sends])
    made = mix(place, lengths, [grads0, grads1], probs_t, corner_t, count, -1)
    place = after(place, made[0])
    evens = exchange_some(made, range(2, zones, 2), zones, -1)
    keeps = call_weights(place, 0)
    place = after(place, keeps[0], *evens, *weight_sum.came)
    odds = exchange_some(made, range(1, zones, 2), zones, -1, *evens)
    backs = [made[0]] + [(odds if d % 2 else evens)[(d - 1) // 2] for d in range(1, zones)]
    weight_sum.first(keeps, *evens)
    rand = logit_grads(
        place, lengths, (grads0, grads1), (values0, values1), rand_logits, ranks, count
    )
    place = after(place, rand[0], *weight_sum.went, *odds)

    rand_sum.core([after(value, *weight_sum.went, *odds) for value in rand[:2]])
    weight_sum.second(rand[0], *odds)
    place = after(place, *rand_sum.came)

    up_total = (up_sums[0] + up_sums[1]).reshape(ranks * zones, -1)
    rest_total = sums[0] + sums[1]
    gain_total, bias_total = (
        rest_total[i].reshape(ranks * zones, -1) for i in range(2)
    )
    up_size, gain_size = hidden // ranks // zones, depth // ranks // zones
    extra = jnp.concatenate([jnp.zeros_like(gain_total), gain_total, bias_total, up_total], 1)
    extra = jnp.pad(extra, ((0, 0), (0, depth - extra.shape[1])))

    rand_sum.first(rand[2:], *backs)
    grad_x, value_send, value_keep = input_grads(
        place, backs, block_input, gain1, weight, attended, extra, heads, ranks
    )
    sides = weight_sum.finish(*rand_sum.sent)
    terms = [side[d] for side in sides for d in range(zones // 2)]
    far_apart = zones // 2
    for d in (far_apart, *(d for d in range(1, zones) if d != far_apart)):
        sent = terms[d].astype(BF16)
        if d != far_apart:
            sent = after(sent, terms[far_apart])
        terms[d] = shift(sent, "head", zones, d)
    rand_sum.second(value_send, terms[far_apart])
    value_own = reduce_direct(value_send, value_keep, ranks, *rand_sum.went)
    tile, square = hidden // ranks // zones, depth // ranks
    value_blocks = [value_own[d].astype(F32 if d == 0 else BF16) for d in range(zones)]
    value_blocks[1:] = [after(value, *terms[1:]) for value in value_blocks[1:]]
    value_terms = spread_head(value_blocks, zones)
    terms = lax.optimization_barrier((*terms, *value_blocks[1:]))[:zones]
    grad_up, grad_down, grad_out = feed_sums(terms, tile, square, zones)
    grad_value, line = value_sums(value_terms, square, zones)
    line = line[0]
    grad_rand = jnp.concatenate(rand_sum.finish(*value_blocks[1:]), 1)
    return (
        feed1[zones],
        grad_x,
        grad_rand,
        grad_value,
        grad_out,
        line[:gain_size],
        line[gain_size : 2 * gain_size],
        grad_up.T,
        line[3 * gain_size : 3 * gain_size + up_size],
        grad_down,
        line[2 * gain_size : 3 * gain_size],
    )


def solution(mesh):
    in_specs = (
        P("dp", "head", None),
        P("dp"),
        P("dp", "head", None),
        P(),
        P(None, "head"),
        P("head", None, None),
        P("head", None),
        P(),
        P(),
        P(),
        P(),
        P(),
    )
    out_specs = (
        P("dp", "head", None),
        P("dp", "head", None),
        P("head", "dp", None),
        P("dp", "head"),
        P("head", "dp"),
        P(("dp", "head")),
        P(("dp", "head")),
        P(None, ("dp", "head")),
        P(("dp", "head")),
        P(("dp", "head"), None),
        P(("dp", "head")),
    )
    body = functools.partial(local, mesh.shape["head"], mesh.shape["dp"])
    return jax.shard_map(
        body, mesh=mesh, in_specs=in_specs, out_specs=out_specs, check_vma=False
    )
```

```python
import functools

import jax
import jax.numpy as jnp
from jax import lax
from jax.experimental import pallas as pl
from jax.experimental.pallas import tpu as pltpu
from jax.sharding import PartitionSpec as P

SHORT = 256
EPSILON = 1e-05
F32 = jnp.float32
BF16 = jnp.bfloat16
GELU_C = 0.7978845608028654
GELU_A = 0.044715
SHARE = 1.0


def dot_nn(a, b):
    return lax.dot_general(a, b, (((1,), (0,)), ((), ())), preferred_element_type=F32)


def dot_nt(a, b):
    return lax.dot_general(a, b, (((1,), (1,)), ((), ())), preferred_element_type=F32)


def dot_tn(a, b):
    return lax.dot_general(a, b, (((0,), (0,)), ((), ())), preferred_element_type=F32)


def norm_of(value):
    centered = value - jnp.mean(value, -1, keepdims=True)
    inverse = lax.rsqrt(jnp.mean(centered * centered, -1, keepdims=True) + EPSILON)
    return centered * inverse, inverse


def norm_back(scaled, hat, inverse):
    return inverse * (
        scaled
        - jnp.mean(scaled, -1, keepdims=True)
        - hat * jnp.mean(scaled * hat, -1, keepdims=True)
    )


def interleave(values, heads, size):
    parts = []
    for head in range(heads):
        for value in values:
            parts.append(value[:, head * size : (head + 1) * size])
    return jnp.concatenate(parts, axis=1)


def separate(piece, seq, count, heads, size):
    parts = []
    for head in range(heads):
        at = (head * count + seq) * size
        parts.append(piece[:, at : at + size])
    return jnp.concatenate(parts, axis=1)


def far(shape, dtype):
    return pltpu.HBM(shape, dtype)


def kept(value):
    return pltpu.with_memory_space_constraint(value, pltpu.HBM)


def whole(shape):
    return pl.BlockSpec(
        shape, lambda *_: (0,) * len(shape), pipeline_mode=pl.Buffered(buffer_count=1)
    )


def resident():
    return pl.BlockSpec(memory_space=pltpu.VMEM)


def cost(flops, moved, special=0):
    return pl.CostEstimate(
        flops=int(flops * SHARE), bytes_accessed=int(moved * SHARE), transcendentals=0
    )


def params(megabytes, grid_dims=1):
    return pltpu.CompilerParams(
        dimension_semantics=("arbitrary",) * grid_dims, vmem_limit_bytes=megabytes << 20
    )


def probs_kernel(logit_ref, long_ref, long_t_ref, short_ref, short_t_ref):
    logits = logit_ref[0].astype(F32)
    raised = jnp.exp(logits - jnp.max(logits, -1, keepdims=True))
    probs = raised / jnp.sum(raised, -1, keepdims=True)
    long_ref[0] = probs.astype(BF16)
    long_t_ref[0] = probs.T.astype(BF16)

    @pl.when(pl.program_id(1) == 0)
    def _():
        corner = logits[:, :SHORT]
        lifted = jnp.exp(corner - jnp.max(corner, -1, keepdims=True))
        part = lifted / jnp.sum(lifted, -1, keepdims=True)
        short_ref[0] = part.astype(BF16)
        short_t_ref[0] = part.T.astype(BF16)


def make_probs(logits):
    heads, rows, _ = logits.shape
    return pl.pallas_call(
        probs_kernel,
        grid=(heads, rows // SHORT),
        in_specs=[pl.BlockSpec((1, SHORT, rows), lambda h, i: (h, i, 0))],
        out_specs=[
            pl.BlockSpec((1, SHORT, rows), lambda h, i: (h, i, 0)),
            pl.BlockSpec((1, rows, SHORT), lambda h, i: (h, 0, i)),
            pl.BlockSpec((1, SHORT, SHORT), lambda h, i: (h, 0, 0)),
            pl.BlockSpec((1, SHORT, SHORT), lambda h, i: (h, 0, 0)),
        ],
        out_shape=[
            far((heads, rows, rows), BF16),
            far((heads, rows, rows), BF16),
            jax.ShapeDtypeStruct((heads, SHORT, SHORT), BF16),
            jax.ShapeDtypeStruct((heads, SHORT, SHORT), BF16),
        ],
        compiler_params=params(20, 2),
        cost_estimate=cost(10 * logits.size, 6 * logits.size, logits.size),
        name="probs",
    )(kept(logits))


def values_kernel(zones, heads, size, first, place_ref, x_ref, gain_ref, *rest):
    width = heads * size
    if first:
        own_ref, others_ref = rest[0], rest[zones]
        mine = rest[1:zones]
        outs, weight_ref = rest[zones + 1 : 2 * zones + 1], rest[2 * zones + 1]
        half = width // 2
        parity = lax.rem(place_ref[1], 2)
        weight_ref[:width, :] = own_ref[...]
        for d in range(1, zones):
            at = pl.multiple_of(d * width + parity * half, 16)
            weight_ref[pl.ds(at, half), :] = mine[d - 1][...]
            at = pl.multiple_of(d * width + (1 - parity) * half, 16)
            weight_ref[pl.ds(at, half), :] = others_ref[d - 1]
    else:
        weight_ref, outs = rest[0], rest[1:]
    made = []
    for seq in range(x_ref.shape[0]):
        hat, _ = norm_of(x_ref[seq].astype(F32))
        norm = (hat * gain_ref[...]).astype(BF16)
        made.append(dot_nt(norm, weight_ref[...]))
    for d in range(zones):
        own = [value[:, d * width : (d + 1) * width] for value in made]
        outs[d][...] = interleave(own, heads, size).astype(BF16)


def make_values(place, x, gain, weights, zones, heads, first):
    count, rows, depth = x.shape
    wide = count * depth // zones
    operands = [x, gain, *weights]
    shapes = [jax.ShapeDtypeStruct((rows, wide), BF16)] * zones
    if first:
        shapes.append(jax.ShapeDtypeStruct((depth, depth), BF16))
    return pl.pallas_call(
        functools.partial(values_kernel, zones, heads, depth // zones // heads, first),
        grid_spec=pltpu.PrefetchScalarGridSpec(
            num_scalar_prefetch=1,
            grid=(1,),
            in_specs=[whole(operand.shape) for operand in operands],
            out_specs=[whole(shape.shape) for shape in shapes],
        ),
        out_shape=shapes,
        compiler_params=params(12),
        cost_estimate=cost(
            2 * count * rows * depth * depth, 2 * x.size * 2 + 4 * depth * depth
        ),
        name="values",
    )(place, *operands)


def mix_kernel(zones, chunks, count, size, rows, sign, place_ref, long_flags, *refs):
    pieces = refs[: chunks * zones]
    matrix_ref, corner_ref = refs[chunks * zones : chunks * zones + 2]
    outs, held = refs[chunks * zones + 2 : -1], refs[-1]
    place = place_ref[0]
    wide = count * size
    for c in range(chunks):
        for d in range(zones):
            source = lax.rem(place + zones - sign * d, zones)
            at = pl.ds(pl.multiple_of(source * rows, rows), rows)
            held[at, c * wide : (c + 1) * wide] = pieces[c * zones + d][...]
    lane = lax.broadcasted_iota(jnp.int32, (1, chunks * wide), 1)
    is_long = jnp.zeros((1, chunks * wide), jnp.bool_)
    for seq in range(chunks * count):
        inside = (lane >= seq * size) & (lane < (seq + 1) * size)
        is_long = is_long | (inside & (long_flags[seq] > SHORT))
    corner = dot_nn(corner_ref[0], held[:SHORT, :])
    for d in range(zones):
        target = lax.rem(place + zones + sign * d, zones)
        part = matrix_ref[0, pl.ds(pl.multiple_of(target * rows, rows), rows), :]
        full = dot_nn(part, held[...])
        small = jnp.where(target == 0, corner, jnp.zeros_like(corner))
        outs[d][...] = jnp.where(is_long, full, small).astype(BF16)


def mix(place, lengths, groups, matrix, corner, count, sign):
    chunks, zones = len(groups), len(groups[0])
    heads, full, _ = matrix.shape
    rows, wide = groups[0][0].shape
    lanes = wide // heads
    spec = pl.BlockSpec((rows, lanes), lambda h, *_: (0, h))
    out_spec = pl.BlockSpec((rows, chunks * lanes), lambda h, *_: (0, h))
    return pl.pallas_call(
        functools.partial(mix_kernel, zones, chunks, count, lanes // count, rows, sign),
        grid_spec=pltpu.PrefetchScalarGridSpec(
            num_scalar_prefetch=2,
            grid=(heads,),
            in_specs=[spec] * (chunks * zones)
            + [
                pl.BlockSpec((1, full, full), lambda h, *_: (h, 0, 0)),
                pl.BlockSpec((1, SHORT, SHORT), lambda h, *_: (h, 0, 0)),
            ],
            out_specs=[out_spec] * zones,
            scratch_shapes=[pltpu.VMEM((full, chunks * lanes), BF16)],
        ),
        out_shape=[jax.ShapeDtypeStruct((rows, chunks * wide), BF16)] * zones,
        compiler_params=params(16),
        cost_estimate=cost(
            2 * heads * full * full * lanes * chunks,
            2 * heads * full * full + 4 * full * wide * chunks,
        ),
        name="mix",
    )(place, lengths, *(piece for group in groups for piece in group), kept(matrix), corner)


def feed_kernel(zones, heads, size, steps, earlier, place_ref, *refs):
    pieces = refs[:zones]
    (x_ref, cot_ref, project_ref, gain_ref, up_ref, up_bias_ref, down_ref, down_bias_ref) = refs[
        zones : zones + 8
    ]
    outs = refs[zones + 8 + earlier :]
    grads = outs[:zones]
    (
        block_ref,
        act_t_ref,
        pre_t_ref,
        norm_out_ref,
        attended_ref,
        up_sum_ref,
        sums_ref,
        norm_ref,
        weight_ref,
        resid_ref,
        hat_ref,
        inv_ref,
        forward_ref,
        back_ref,
    ) = outs[zones:]
    count, rows, depth = x_ref.shape
    width = heads * size
    step = pl.program_id(0)

    @pl.when(step == 0)
    def _():
        for d in range(zones):
            other = lax.rem(place_ref[0] + zones - d, zones)
            at = pl.multiple_of(other * width, 16)
            weight_ref[d * width : (d + 1) * width, :] = project_ref[pl.ds(at, width), :]
        for seq in range(count):
            at = slice(seq * rows, (seq + 1) * rows)
            mixed = jnp.concatenate(
                [separate(piece[...], seq, count, heads, size) for piece in pieces], axis=1
            )
            resid = x_ref[seq].astype(F32) + dot_nn(mixed, weight_ref[...])
            hat, inverse = norm_of(resid)
            resid_ref[at, :] = resid + down_bias_ref[...]
            hat_ref[at, :] = hat
            inv_ref[at, :] = inverse
            norm_ref[at, :] = (hat * gain_ref[...]).astype(BF16)
        forward_ref[...] = jnp.zeros_like(forward_ref)
        back_ref[...] = jnp.zeros_like(back_ref)

    up_sum = jnp.zeros((1, up_ref.shape[1]), F32)
    for seq in range(count):
        at = slice(seq * rows, (seq + 1) * rows)
        pre = dot_nn(norm_ref[at, :], up_ref[...]) + up_bias_ref[...]
        grad_act = dot_nt(cot_ref[seq], down_ref[...])
        square = pre * pre
        bent = jnp.tanh(pre * (GELU_C + (GELU_C * GELU_A) * square))
        half = 0.5 + 0.5 * bent
        act = (pre * half).astype(BF16)
        slope = half + (0.5 * pre) * (1.0 - bent * bent) * (
            GELU_C + (3.0 * GELU_C * GELU_A) * square
        )
        grad_pre = (grad_act * slope).astype(BF16)
        up_sum = up_sum + jnp.sum(grad_pre.astype(F32), 0, keepdims=True)
        act_t_ref[:, at] = act.T
        pre_t_ref[:, at] = grad_pre.T
        forward = dot_nn(act, down_ref[...])
        back = dot_nt(grad_pre, up_ref[...])

        forward_ref[at, :] += forward
        back_ref[at, :] += back

    up_sum_ref[...] = up_sum
    share = norm_out_ref.shape[1]
    norm_out_ref[...] = norm_ref[:, pl.ds(pl.multiple_of(step * share, share), share)]

    @pl.when(step == steps - 1)
    def _():
        gain_sum = jnp.zeros((1, depth), F32)
        bias_sum = jnp.zeros((1, depth), F32)
        made = []
        for seq in range(count):
            at = slice(seq * rows, (seq + 1) * rows)
            block_ref[seq] = (resid_ref[at, :] + forward_ref[at, :]).astype(BF16)
            cot = cot_ref[seq].astype(F32)
            hat = hat_ref[at, :]
            back = back_ref[at, :]
            gain_sum = gain_sum + jnp.sum(back * hat, 0, keepdims=True)
            bias_sum = bias_sum + jnp.sum(cot, 0, keepdims=True)
            grad = cot + norm_back(back * gain_ref[...], hat, inv_ref[at, :])
            low = grad.astype(BF16)
            attended_ref[:, at] = low.T
            made.append(dot_nt(low, weight_ref[...]))
        sums_ref[0:1, :] = gain_sum
        sums_ref[1:2, :] = bias_sum
        for d in range(zones):
            mine = [value[:, d * width : (d + 1) * width] for value in made]
            grads[d][...] = interleave(mine, heads, size).astype(BF16)


def feed(place, pieces, x, cot, project, gain, up, up_bias, down, down_bias, heads, c, chunks, earlier):
    zones = len(pieces)
    count, rows, depth = x.shape
    size = depth // zones // heads
    hidden = up.shape[1]
    tile = min(512, hidden)
    steps = hidden // tile
    tokens = count * rows
    wide = pieces[0].shape[1]
    shapes = [jax.ShapeDtypeStruct((rows, wide), BF16)] * zones + [
        far((chunks * count, rows, depth), BF16),
        far((hidden, chunks * tokens), BF16),
        far((hidden, chunks * tokens), BF16),
        far((chunks * tokens, depth), BF16),
        far((depth, chunks * tokens), BF16),
        jax.ShapeDtypeStruct((1, hidden), F32),
        jax.ShapeDtypeStruct((2, depth), F32),
    ]
    return pl.pallas_call(
        functools.partial(feed_kernel, zones, heads, size, steps, len(earlier)),
        grid_spec=pltpu.PrefetchScalarGridSpec(
            num_scalar_prefetch=1,
            grid=(steps,),
            in_specs=[whole((rows, wide))] * zones
            + [
                whole(x.shape),
                whole(cot.shape),
                whole(project.shape),
                whole(gain.shape),
                pl.BlockSpec((depth, tile), lambda f, *_: (0, f)),
                pl.BlockSpec((1, tile), lambda f, *_: (0, f)),
                pl.BlockSpec((tile, depth), lambda f, *_: (f, 0)),
                whole(down_bias.shape),
            ]
            + [pl.BlockSpec(memory_space=pltpu.HBM)] * len(earlier),
            out_specs=[whole((rows, wide))] * zones
            + [
                pl.BlockSpec(
                    (count, rows, depth),
                    lambda *_: (c, 0, 0),
                    pipeline_mode=pl.Buffered(buffer_count=1),
                ),
                pl.BlockSpec((tile, tokens), lambda f, *_: (f, c)),
                pl.BlockSpec((tile, tokens), lambda f, *_: (f, c)),
                pl.BlockSpec((tokens, depth // steps), lambda f, *_: (c, f)),
                pl.BlockSpec(
                    (depth, tokens),
                    lambda *_: (0, c),
                    pipeline_mode=pl.Buffered(buffer_count=1),
                ),
                pl.BlockSpec((1, tile), lambda f, *_: (0, f)),
                whole((2, depth)),
            ],
            scratch_shapes=[
                pltpu.VMEM((tokens, depth), BF16),
                pltpu.VMEM((depth, depth), BF16),
                pltpu.VMEM((tokens, depth), F32),
                pltpu.VMEM((tokens, depth), F32),
                pltpu.VMEM((tokens, 1), F32),
                pltpu.VMEM((tokens, depth), F32),
                pltpu.VMEM((tokens, depth), F32),
            ],
        ),
        out_shape=shapes,
        compiler_params=params(28),
        cost_estimate=cost(
            8 * tokens * depth * hidden + 4 * tokens * depth * depth,
            4 * depth * hidden + 4 * tokens * hidden + 20 * tokens * depth,
            tokens * hidden,
        ),
        input_output_aliases={zones + 9 + i: zones + i for i in range(len(earlier))},
        name="feed",
    )(
        place,
        *map(kept, pieces),
        kept(x),
        kept(cot),
        kept(project),
        gain,
        kept(up),
        up_bias,
        kept(down),
        down_bias,
        *earlier,
    )


def relative_block(step, odd, ranks):
    rest = ranks // 8
    return odd + 2 * (step // rest) + 8 * lax.rem(step, rest)


def group_rows(rows, zones):
    return -(-rows // (8 * zones)) * 8


def pack(block, d, zones):
    rows, depth = block.shape
    width, group = depth // zones, group_rows(rows, zones)
    parts = []
    for k in range(zones):
        if k * group < rows:
            parts.append(block[k * group : (k + 1) * group, d * width : (d + 1) * width])
        else:
            parts.append(jnp.zeros((group, width), block.dtype))
    return jnp.concatenate(parts, axis=1)


def place_first(second):
    return second // 2 + 2 * (1 - lax.rem(second, 2))


def place_second(second):
    return lax.rem(second + 2, 4)


def weights_kernel(zones, chunks, heads, place_ref, *refs):
    act_ref, pre_ref, attended_ref, norm_ref, cot_ref = refs[:5]
    pieces = refs[5 : 5 + zones * chunks]
    first_ref, second_ref, scratch_ref, mixed_ref = refs[5 + zones * chunks :]
    part = scratch_ref.shape[1] // zones
    rows, wide = pieces[0].shape
    count = norm_ref.shape[0] // rows // chunks

    @pl.when(pl.program_id(0) == 0)
    def _():
        for c in range(chunks):
            group = pieces[c * zones : (c + 1) * zones]
            for seq in range(count):
                parts = [
                    separate(piece[...], seq, count, heads, wide // heads // count)
                    for piece in group
                ]
                at = (c * count + seq) * rows
                mixed_ref[at : at + rows, :] = jnp.concatenate(parts, axis=1)

    scratch_ref[0] = dot_nn(pre_ref[...], norm_ref[...])
    scratch_ref[1] = dot_nn(act_ref[...], cot_ref[...])
    square = dot_nn(attended_ref[...], mixed_ref[...])
    for d in range(zones):
        at = pl.ds(pl.multiple_of(lax.rem(place_ref[0] + d, zones) * part, 8), part)
        parts = [scratch_ref[0, at, :], scratch_ref[1, at, :], pack(square, -d % zones, zones)]
        used = sum(value.shape[0] for value in parts)
        parts.append(jnp.zeros((first_ref.shape[2] - used, first_ref.shape[3]), F32))
        side, number = (first_ref, d) if d < zones // 2 else (second_ref, d - zones // 2)
        side[0, number] = jnp.concatenate(parts, axis=0).astype(BF16)


def weight_grads(place, act, pre, attended, norm, cot, pieces, heads, odd, zones, ranks):
    chunks = len(pieces)
    hidden, tokens = act.shape
    depth = norm.shape[1]
    tile, square = hidden // ranks, depth // ranks
    rows = 2 * tile // zones + group_rows(square, zones)
    rows = -(-rows // 16) * 16
    rest = ranks // 8

    def tall(step, place_ref):
        return (lax.bitwise_xor(place_ref[1], relative_block(step, odd, ranks)), 0)

    def first(step, _):
        return (place_first(step // rest) * rest + lax.rem(step, rest), 0, 0, 0)

    def second(step, _):
        return (place_second(step // rest) * rest + lax.rem(step, rest), 0, 0, 0)

    shape = (ranks // 2, zones // 2, rows, depth)
    return pl.pallas_call(
        functools.partial(weights_kernel, zones, chunks, heads),
        grid_spec=pltpu.PrefetchScalarGridSpec(
            num_scalar_prefetch=1,
            grid=(ranks // 2,),
            in_specs=[pl.BlockSpec((tile, tokens), tall)] * 2
            + [pl.BlockSpec((square, tokens), tall)]
            + [whole((tokens, depth))] * 2
            + [whole(pieces[0][0].shape)] * (zones * chunks),
            out_specs=[pl.BlockSpec((1, *shape[1:]), first), pl.BlockSpec((1, *shape[1:]), second)],
            scratch_shapes=[
                pltpu.VMEM((2, tile, depth), F32),
                pltpu.VMEM((tokens, depth), BF16),
            ],
        ),
        out_shape=[far(shape, BF16)] * 2,
        compiler_params=params(24),
        cost_estimate=cost(
            2 * hidden * tokens * depth,
            2 * hidden * tokens + 2 * hidden * depth + 4 * tokens * depth,
        ),
        name="weights",
    )(
        place,
        *map(kept, (act, pre, attended, norm, cot)),
        *(kept(piece) for group in pieces for piece in group),
    )


def store_square(place_ref, outs, scratch_ref, extra_ref, zones, ranks):
    depth = scratch_ref.shape[0]
    part = depth // ranks
    for odd, out_ref in zip((1, 0), outs):
        for step in range(ranks // 2):
            rest = ranks // 8
            relative = odd + 2 * (step // rest) + 8 * (step % rest)
            rank = lax.bitwise_xor(place_ref[1], relative)
            block = scratch_ref[pl.ds(pl.multiple_of(rank * part, 8), part), :]
            for d in range(zones):
                zone = lax.rem(place_ref[0] + d, zones)
                line = extra_ref[pl.ds(rank * zones + zone, 1), :]
                packed = pack(block, d, zones)
                below = jnp.broadcast_to(line, (out_ref.shape[2] - packed.shape[0], depth))
                out_ref[step, d] = jnp.concatenate([packed, below], axis=0).astype(BF16)


def logits_kernel(
    zones, chunks, count, heads, size, rows, ranks, place_ref, lengths_ref, *refs
):
    grads = refs[: chunks * zones]
    values = refs[chunks * zones : 2 * chunks * zones]
    refs = refs[2 * chunks * zones :]
    logit_ref, sends, keeps = refs[0], refs[1:3], refs[3:5]
    long_ref, short_ref, value_ref, out_ref = refs[5:]
    place = place_ref[0]
    lanes = count * size
    step = pl.program_id(0)

    @pl.when(step == 0)
    def _():
        lane = lax.broadcasted_iota(jnp.int32, (1, lanes), 1)
        for c in range(chunks):
            is_long = jnp.zeros((1, lanes), jnp.bool_)
            for seq in range(count):
                inside = (lane >= seq * size) & (lane < (seq + 1) * size)
                is_long = is_long | (inside & (lengths_ref[c * count + seq] > SHORT))
            for d in range(zones):
                ahead = lax.rem(place + d, zones)
                behind = lax.rem(place + zones - d, zones)
                to = pl.ds(pl.multiple_of(ahead * rows, rows), rows)
                back = pl.ds(pl.multiple_of(behind * rows, rows), rows)
                for head in range(heads):
                    columns = slice(head * lanes, (head + 1) * lanes)
                    own = slice(c * lanes, (c + 1) * lanes)
                    grad = grads[c * zones + d][:, columns].astype(F32)
                    long_ref[head, to, own] = jnp.where(is_long, grad, 0.0).astype(BF16)
                    value_ref[head, back, own] = values[c * zones + d][:, columns]

                    @pl.when(ahead == 0)
                    def _():
                        short_ref[head, :, own] = jnp.where(is_long, 0.0, grad).astype(BF16)

    odd = jnp.where(step < ranks // 2, 1, 0)
    rank = lax.bitwise_xor(
        place_ref[1], relative_block(lax.rem(step, ranks // 2), odd, ranks)
    )
    part = logit_ref.shape[1]
    middle = part // 2
    start = rank * part
    for head in range(heads):
        logits = logit_ref[head].astype(F32)
        raised = jnp.exp(logits - jnp.max(logits, -1, keepdims=True))
        probs = raised / jnp.sum(raised, -1, keepdims=True)
        at = pl.ds(pl.multiple_of(start, part), part)
        total = dot_nt(long_ref[head, at, :], value_ref[head])
        out_ref[head] = probs * (total - jnp.sum(total * probs, -1, keepdims=True))

        @pl.when(start < SHORT)
        def _():
            corner = logits[:, :SHORT]
            lifted = jnp.exp(corner - jnp.max(corner, -1, keepdims=True))
            small = lifted / jnp.sum(lifted, -1, keepdims=True)
            sums = dot_nt(short_ref[head, at, :], value_ref[head, :SHORT, :])
            more = small * (sums - jnp.sum(sums * small, -1, keepdims=True))
            out_ref[head, :, :SHORT] += more

    @pl.when(step < ranks // 2)
    def _():
        sends[0][0] = out_ref[:, :middle, :].astype(BF16)
        sends[1][0] = out_ref[:, middle:, :].astype(BF16)

    @pl.when(step >= ranks // 2)
    def _():
        keeps[0][0] = out_ref[:, :middle, :].astype(BF16)
        keeps[1][0] = out_ref[:, middle:, :].astype(BF16)


def logit_grads(place, lengths, grads, values, logits, ranks, count):
    chunks, zones = len(grads), len(grads[0])
    heads, full, _ = logits.shape
    rows, wide = grads[0][0].shape
    size = wide // heads // count
    part = full // ranks
    half, rest = ranks // 2, ranks // 8

    def pick(step, place_ref, _):
        odd = jnp.where(step < half, 1, 0)
        block = relative_block(lax.rem(step, half), odd, ranks)
        return (0, lax.bitwise_xor(place_ref[1], block), 0)

    def spec(order, keep):
        def number(step, *_):
            at = jnp.maximum(step - half, 0) if keep else jnp.minimum(step, half - 1)
            return (order(at // rest) * rest + lax.rem(at, rest), 0, 0, 0)

        return pl.BlockSpec((1, heads, part // 2, full), number)

    flat = [piece for group in grads for piece in group] + [
        piece for group in values for piece in group
    ]
    every = chunks * count * size
    shape = (half, heads, part // 2, full)
    return pl.pallas_call(
        functools.partial(logits_kernel, zones, chunks, count, heads, size, rows, ranks),
        grid_spec=pltpu.PrefetchScalarGridSpec(
            num_scalar_prefetch=2,
            grid=(ranks,),
            in_specs=[whole((rows, wide))] * len(flat)
            + [pl.BlockSpec((heads, part, full), pick)],
            out_specs=[
                spec(order, keep) for keep in (False, True) for order in (place_first, place_second)
            ],
            scratch_shapes=[
                pltpu.VMEM((heads, full, every), BF16),
                pltpu.VMEM((heads, SHORT, every), BF16),
                pltpu.VMEM((heads, full, every), BF16),
                pltpu.VMEM((heads, part, full), F32),
            ],
        ),
        out_shape=[far(shape, BF16)] * 4,
        compiler_params=params(24),
        cost_estimate=cost(
            2 * heads * full * full * every, 4 * heads * full * full, heads * full * full
        ),
        name="logits",
    )(place, lengths, *map(kept, flat), kept(logits))


def input_kernel(zones, heads, size, ranks, count, place_ref, *refs):
    pieces = refs[:zones]
    x_ref, gain_ref, weight_ref, extra_in_ref = refs[zones : zones + 4]
    resid_ref = refs[zones + 4]
    grad_ref, send_ref, keep_ref, total_ref, gain_sum_ref, extra_ref = refs[zones + 5 :]
    depth = x_ref.shape[2]
    seq = pl.program_id(0)

    @pl.when(seq == 0)
    def _():
        total_ref[...] = jnp.zeros_like(total_ref)
        gain_sum_ref[...] = jnp.zeros_like(gain_sum_ref)

    hat, inverse = norm_of(x_ref[0].astype(F32))
    norm = (hat * gain_ref[...]).astype(BF16)
    pair = 128 // size
    parts = []
    lane = lax.broadcasted_iota(jnp.int32, (1, 128), 1)
    for piece in pieces:
        for head in range(heads):
            at = pl.multiple_of((head * count + seq // pair * pair) * size, 128)
            both = piece[:, pl.ds(at, 128)].astype(F32)
            moved = pltpu.roll(both, shift=size, axis=1)
            parts.append(jnp.where(lax.rem(seq, pair) == 0, both, moved)[:, :size])
    back = jnp.concatenate(parts, axis=1).astype(BF16)
    grad_norm = dot_nn(back, weight_ref[...])
    gain_sum_ref[...] += jnp.sum(grad_norm * hat, 0, keepdims=True)
    resid = resid_ref[...].astype(F32).T
    grad = resid + norm_back(grad_norm * gain_ref[...], hat, inverse)
    grad_ref[0] = grad.astype(BF16)
    total_ref[...] += dot_tn(norm, back)

    @pl.when(seq == count - 1)
    def _():
        extra_ref[...] = extra_in_ref[...]
        share = depth // ranks // zones
        for index in range(ranks * zones):
            extra_ref[index : index + 1, :share] = gain_sum_ref[
                :, index * share : (index + 1) * share
            ]
        store_square(place_ref, (send_ref, keep_ref), total_ref, extra_ref, zones, ranks)


def input_grads(place, pieces, x, gain, weight, resid, extra, heads, ranks):
    zones = len(pieces)
    count, rows, depth = x.shape
    size = depth // zones // heads
    assert 2 * size == 128 and count % 2 == 0
    height = -(-(group_rows(depth // ranks, zones) + 1) // 16) * 16
    shape = (ranks // 2, zones, height, depth)
    return pl.pallas_call(
        functools.partial(input_kernel, zones, heads, size, ranks, count),
        grid_spec=pltpu.PrefetchScalarGridSpec(
            num_scalar_prefetch=1,
            grid=(count,),
            in_specs=[whole(pieces[0].shape)] * zones
            + [
                pl.BlockSpec((1, rows, depth), lambda s, *_: (s, 0, 0)),
                whole(gain.shape),
                whole(weight.shape),
                whole(extra.shape),
                pl.BlockSpec((depth, rows), lambda s, *_: (0, s)),
            ],
            out_specs=[
                pl.BlockSpec((1, rows, depth), lambda s, *_: (s, 0, 0)),
                whole(shape),
                whole(shape),
            ],
            scratch_shapes=[
                pltpu.VMEM((depth, depth), F32),
                pltpu.VMEM((1, depth), F32),
                pltpu.VMEM(extra.shape, F32),
            ],
        ),
        out_shape=[
            far(x.shape, BF16),
            jax.ShapeDtypeStruct(shape, BF16),
            jax.ShapeDtypeStruct(shape, BF16),
        ],
        compiler_params=params(24),
        cost_estimate=cost(
            4 * count * rows * depth * depth, 12 * count * rows * depth + 8 * depth * depth
        ),
        name="input",
    )(place, *map(kept, pieces), kept(x), gain, kept(weight), extra, kept(resid))


def total_of(terms):
    total = terms[0][...]
    for term in terms[1:]:
        total = total + term[...].astype(F32)
    return total


def unpack(packed, rows, zones):
    width = packed.shape[1] // zones
    parts = [packed[:, k * width : (k + 1) * width] for k in range(zones)]
    return jnp.concatenate(parts, axis=0)[:rows]


def feed_sums_kernel(zones, tile, square, *refs):
    up_ref, down_ref, square_ref = refs[zones:]
    total = total_of(refs[:zones])
    up_ref[...] = total[:tile]
    down_ref[...] = total[tile : 2 * tile]
    packed = total[2 * tile : 2 * tile + group_rows(square, zones)]
    square_ref[...] = unpack(packed, square, zones).T


def feed_sums(terms, tile, square, zones):
    depth = terms[0].shape[1]
    return pl.pallas_call(
        functools.partial(feed_sums_kernel, zones, tile, square),
        grid=(1,),
        in_specs=[whole(term.shape) for term in terms],
        out_specs=[whole((tile, depth)), whole((tile, depth)), whole((depth // zones, square))],
        out_shape=[
            far((tile, depth), F32),
            far((tile, depth), F32),
            far((depth // zones, square), F32),
        ],
        compiler_params=params(12),
        name="feed_sums",
    )(*map(kept, terms))


def value_sums_kernel(zones, square, *refs):
    square_ref, line_ref = refs[zones:]
    total = total_of(refs[:zones])
    group = group_rows(square, zones)
    square_ref[...] = unpack(total[:group], square, zones)
    line_ref[...] = total[group : group + 1]


def value_sums(terms, square, zones):
    depth = terms[0].shape[1]
    return pl.pallas_call(
        functools.partial(value_sums_kernel, zones, square),
        grid=(1,),
        in_specs=[whole(term.shape) for term in terms],
        out_specs=[whole((square, depth // zones)), whole((1, depth))],
        out_shape=[far((square, depth // zones), F32), jax.ShapeDtypeStruct((1, depth), F32)],
        compiler_params=params(12),
        name="value_sums",
    )(*terms)


def logit_sums_kernel(*refs):
    out_ref = refs[-1]
    middle = out_ref.shape[1] // 2
    for side in range(2):
        keep, came, went, last = (ref[0].astype(F32) for ref in refs[4 * side : 4 * side + 4])
        out_ref[:, side * middle : (side + 1) * middle, :] = keep + came + went + last


def logit_sums(keeps, cames, wents, lasts):
    half = keeps[0].shape[0] // 2
    _, heads, middle, full = keeps[0].shape
    block = (1, heads, middle, full)
    later = pl.BlockSpec(block, lambda _: (half, 0, 0, 0))
    early = pl.BlockSpec(block, lambda _: (0, 0, 0, 0))
    operands = [v for group in zip(keeps, cames, wents, lasts) for v in group]
    return pl.pallas_call(
        logit_sums_kernel,
        grid=(1,),
        in_specs=[later, later, early, early] * 2,
        out_specs=whole((heads, 2 * middle, full)),
        out_shape=far((heads, 2 * middle, full), F32),
        compiler_params=params(16),
        name="logit_sums",
    )(*map(kept, operands))


def shift(value, axis, extent, by):
    by = by % extent
    return lax.ppermute(value, axis, [(i, (i + by) % extent) for i in range(extent)])


def flip(value, axis, extent, mask):
    return lax.ppermute(value, axis, [(i, i ^ mask) for i in range(extent)])


def widen(value):
    return value.astype(F32)


def after(value, *results):
    return lax.optimization_barrier((value, *results))[0]


def exchange(pieces, extent, sign, *results):
    sent = pieces[1:]
    if results:
        sent = lax.optimization_barrier((*sent, *results))[: extent - 1]
    return [pieces[0]] + [
        shift(piece, "head", extent, sign * (d + 1)) for d, piece in enumerate(sent)
    ]


def exchange_some(pieces, numbers, extent, sign, *results):
    sent = [pieces[d] for d in numbers]
    if results:
        sent = lax.optimization_barrier((*sent, *results))[: len(sent)]
    return [shift(piece, "head", extent, sign * d) for d, piece in zip(numbers, sent)]


class Reduce:
    masks = ((2, 4), (4, 2))

    def __init__(self, ranks):
        self.ranks = ranks

    def core(self, sends):
        self.came = [flip(send, "dp", self.ranks, 1) for send in sends]

    def first(self, keeps, *results):
        half = self.ranks // 4
        sent = [
            (widen(keep[:half]) + widen(came[:half])).astype(BF16)
            for keep, came in zip(keeps, self.came)
        ]
        if results:
            sent = [after(value, *results) for value in sent]
        self.keeps, self.sent = keeps, sent
        self.went = [
            flip(value, "dp", self.ranks, masks[0]) for value, masks in zip(sent, self.masks)
        ]

    def rest(self, start, stop):
        half = self.ranks // 4
        return [
            widen(keep[half + start : half + stop])
            + widen(came[half + start : half + stop])
            + widen(went[start:stop])
            for keep, came, went in zip(self.keeps, self.came, self.went)
        ]

    def second(self, *results):
        sent = [value.astype(BF16) for value in self.rest(self.ranks // 8, self.ranks // 4)]
        if results:
            sent = [after(value, *results) for value in sent]
        self.last = [
            flip(value, "dp", self.ranks, masks[1]) for value, masks in zip(sent, self.masks)
        ]

    def finish(self, *results):
        lasts = self.last
        if results:
            lasts = lax.optimization_barrier((*lasts, *results))[:2]
        sides = []
        for own, last in zip(self.rest(0, self.ranks // 8), lasts):
            total = own + widen(last)
            side = total[0]
            for third in range(1, self.ranks // 8):
                side = side + widen(flip(total[third].astype(BF16), "dp", self.ranks, 8 * third))
            sides.append(side)
        return sides


def reduce_direct(send, keep, ranks, *results):
    rest = ranks // 8
    came = flip(after(send, *results), "dp", ranks, 1)
    both = [
        widen(keep[q * rest : (q + 1) * rest]) + widen(came[q * rest : (q + 1) * rest])
        for q in range(4)
    ]
    total = both[0]
    for q in range(1, 4):
        total = total + widen(flip(both[q].astype(BF16), "dp", ranks, 2 * q))
    own = total[0]
    for third in range(1, rest):
        own = own + widen(flip(total[third].astype(BF16), "dp", ranks, 8 * third))
    return own


def spread_head(blocks, zones):
    return [blocks[0]] + [
        shift(blocks[d].astype(BF16), "head", zones, d) for d in range(1, zones)
    ]


def local(
    zones,
    ranks,
    block_input,
    lengths,
    cotangent,
    norm1_gain,
    value_projection_weight,
    rand_logits,
    output_projection_weight,
    norm2_gain,
    up_projection_weight,
    up_bias,
    down_projection_weight,
    down_bias,
):
    seq_count, rows, depth = block_input.shape
    heads, full, _ = rand_logits.shape
    hidden = up_bias.shape[0]
    assert rows == SHORT and full == rows * zones and ranks % 8 == 0
    count = seq_count // 2
    assert seq_count == 2 * count
    place = jnp.stack([lax.axis_index("head"), lax.axis_index("dp")]).astype(jnp.int32)
    gain1, gain2 = norm1_gain[None], norm2_gain[None]
    width = value_projection_weight.shape[1]

    slot = width // ranks
    project = lax.dynamic_slice_in_dim(output_projection_weight, place[1] * slot, slot, 0)
    project = lax.all_gather(project, ("head", "dp"), axis=0, tiled=True)

    own = value_projection_weight.T
    half = width // 2
    parity = lax.rem(place[1], 2)
    part_rows = lax.dynamic_slice_in_dim(own, parity * half, half, 0)
    mine = [shift(part_rows, "head", zones, -d) for d in range(1, zones)]
    probs, probs_t, corner, corner_t = make_probs(rand_logits)
    others = flip(after(jnp.stack(mine), corner), "dp", ranks, 1)
    place = after(place, corner)

    def part(array, c):
        return array[c * count : (c + 1) * count]

    def call_values(place, c, weights):
        return make_values(place, part(block_input, c), gain1, weights, zones, heads, c == 0)

    def call_feed(place, c, pieces, earlier):
        return feed(
            place,
            pieces,
            part(block_input, c),
            part(cotangent, c),
            project,
            gain2,
            up_projection_weight,
            up_bias[None],
            down_projection_weight,
            down_bias[None],
            heads,
            c,
            2,
            earlier,
        )

    made = call_values(place, 0, [own, *mine, others])
    weight = made[zones]
    place = after(place, weight)
    values0 = exchange(made[:zones], zones, 1)
    made = call_values(place, 1, [weight])
    place = after(place, made[0])
    values1 = exchange(made, zones, 1, *values0)

    made = mix(place, part(lengths, 0), [values0], probs, corner, count, 1)
    place = after(place, made[0])
    mixed0 = [made[0]] + exchange_some(made, range(1, zones - 1), zones, 1)
    mixed0 += exchange_some(made, (zones - 1,), zones, 1, *values1)
    made = mix(place, part(lengths, 1), [values1], probs, corner, count, 1)
    place = after(place, made[0])
    mixed1 = exchange(made, zones, 1, *mixed0)

    feed0 = call_feed(place, 0, mixed0, ())
    place = after(place, feed0[0])
    grads0 = exchange(feed0[:zones], zones, -1, *mixed1)
    feed1 = call_feed(place, 1, mixed1, feed0[zones : zones + 5])
    place = after(place, feed1[0], *grads0)
    act, pre, norm, attended = feed1[zones + 1 : zones + 5]
    up_sums, sums = zip(feed0[zones + 5 :], feed1[zones + 5 :])
    cot = cotangent.reshape(seq_count * rows, depth)

    weight_sum, rand_sum = Reduce(ranks), Reduce(ranks)

    def call_weights(place, odd):
        return weight_grads(
            place,
            act,
            pre,
            attended,
            norm,
            cot,
            (mixed0, mixed1),
            heads,
            odd,
            zones,
            ranks,
        )

    grads1 = exchange(feed1[:zones], zones, -1, *grads0)
    sends = call_weights(place, 1)
    place = after(place, sends[0], *grads1)
    weight_sum.core([after(value, *grads1) for value in sends])
    made = mix(place, lengths, [grads0, grads1], probs_t, corner_t, count, -1)
    place = after(place, made[0])
    evens = exchange_some(made, range(2, zones, 2), zones, -1)
    keeps = call_weights(place, 0)
    place = after(place, keeps[0], *evens, *weight_sum.came)
    odds = exchange_some(made, range(1, zones, 2), zones, -1, *evens)
    backs = [made[0]] + [(odds if d % 2 else evens)[(d - 1) // 2] for d in range(1, zones)]
    weight_sum.first(keeps, *evens)
    rand = logit_grads(
        place, lengths, (grads0, grads1), (values0, values1), rand_logits, ranks, count
    )
    place = after(place, rand[0], *weight_sum.went, *odds)

    rand_sum.core([after(value, *weight_sum.went, *odds) for value in rand[:2]])
    weight_sum.second(rand[0], *odds)
    place = after(place, *rand_sum.came)

    up_total = (up_sums[0] + up_sums[1]).reshape(ranks * zones, -1)
    rest_total = sums[0] + sums[1]
    gain_total, bias_total = (
        rest_total[i].reshape(ranks * zones, -1) for i in range(2)
    )
    up_size, gain_size = hidden // ranks // zones, depth // ranks // zones
    extra = jnp.concatenate([jnp.zeros_like(gain_total), gain_total, bias_total, up_total], 1)
    extra = jnp.pad(extra, ((0, 0), (0, depth - extra.shape[1])))

    rand_sum.first(rand[2:], *backs)
    grad_x, value_send, value_keep = input_grads(
        place, backs, block_input, gain1, weight, attended, extra, heads, ranks
    )
    sides = weight_sum.finish(*rand_sum.sent)
    terms = [side[d] for side in sides for d in range(zones // 2)]
    far_apart = zones // 2
    for d in (far_apart, *(d for d in range(1, zones) if d != far_apart)):
        sent = terms[d].astype(BF16)
        if d != far_apart:
            sent = after(sent, terms[far_apart])
        terms[d] = shift(sent, "head", zones, d)
    rand_sum.second(value_send, terms[far_apart])
    value_own = reduce_direct(value_send, value_keep, ranks, *rand_sum.went)
    tile, square = hidden // ranks // zones, depth // ranks
    value_blocks = [value_own[d].astype(F32 if d == 0 else BF16) for d in range(zones)]
    value_blocks[1:] = [after(value, *terms[1:]) for value in value_blocks[1:]]
    value_terms = spread_head(value_blocks, zones)
    terms = lax.optimization_barrier((*terms, *value_blocks[1:]))[:zones]
    grad_up, grad_down, grad_out = feed_sums(terms, tile, square, zones)
    grad_value, line = value_sums(value_terms, square, zones)
    line = line[0]
    if ranks == 8:
        lasts = lax.optimization_barrier((*rand_sum.last, *value_blocks[1:]))[:2]
        grad_rand = logit_sums(rand_sum.keeps, rand_sum.came, rand_sum.went, lasts)
    else:
        grad_rand = jnp.concatenate(rand_sum.finish(*value_blocks[1:]), 1)
    return (
        feed1[zones],
        grad_x,
        grad_rand,
        grad_value,
        grad_out,
        line[:gain_size],
        line[gain_size : 2 * gain_size],
        grad_up.T,
        line[3 * gain_size : 3 * gain_size + up_size],
        grad_down,
        line[2 * gain_size : 3 * gain_size],
    )


def solution(mesh):
    in_specs = (
        P("dp", "head", None),
        P("dp"),
        P("dp", "head", None),
        P(),
        P(None, "head"),
        P("head", None, None),
        P("head", None),
        P(),
        P(),
        P(),
        P(),
        P(),
    )
    out_specs = (
        P("dp", "head", None),
        P("dp", "head", None),
        P("head", "dp", None),
        P("dp", "head"),
        P("head", "dp"),
        P(("dp", "head")),
        P(("dp", "head")),
        P(None, ("dp", "head")),
        P(("dp", "head")),
        P(("dp", "head"), None),
        P(("dp", "head")),
    )
    body = functools.partial(local, mesh.shape["head"], mesh.shape["dp"])
    return jax.shard_map(
        body, mesh=mesh, in_specs=in_specs, out_specs=out_specs, check_vma=False
    )
```
